128 devices in a mesh: gx: 16 (over y_lo, z, core), gy: 8 (over y_hi, x).
Axes of the slice: x: 4, y: 4 (y_hi: 2, y_lo: 2; y = y_hi * 2 + y_lo), z: 4, core: 2. Of those that a mesh axis runs over, the one named last changes fastest.
Arguments:
- particle_locations: float32 [3, 2097152], P(None, ('gx', 'gy')), may hold values from -3 to 3
- particle_speeds: float32 [3, 2097152], P(None, ('gx', 'gy')), may hold values from -3 to 3
- particle_bulk: float32 [2097152], P(('gx', 'gy')), may hold values from 0.5 to 2
- receiving_group_per_pair: int32 [32768], P(('gx', 'gy')), may hold values from 0 to 16383, as said below
- emitting_group_per_pair: int32 [32768], P(('gx', 'gy')), may hold values from 0 to 16383, as said below
- active_pair_slots: int32 [128], P(('gx', 'gy')), may hold values from 2 to 256, as said below
- landing_site_triple: int32 [3, 2097152], P(None, ('gx', 'gy')), may hold values from 0 to 4095, as said below
- landing_weight_octants: int32 [2097152], P(('gx', 'gy')), may hold values from 1 to 8
- thermal_excess: float32 [64, 512, 4096], P(None, 'gx', 'gy'), may hold values from -6 to 6
- molten_strip_midlines: int32 [2], replicated, may hold values from 0 to 511
Outputs:
- advanced_locations: float32 [3, 2097152], P(None, ('gx', 'gy'))
- advanced_speeds: float32 [3, 2097152], P(None, ('gx', 'gy'))
- packing_share_per_site: float32 [64, 512, 4096], P(None, 'gx', 'gy')
- advanced_thermal_excess: float32 [64, 512, 4096], P(None, 'gx', 'gy')
The draws below stay inside these ranges and needn't reach their ends.
Inputs may be any that keep to these rules, and one draw needn't show every extreme that they name: `receiving_group_per_pair`: slots t of device k = t div 256 have a target block among that device's blocks k * 128 to (k + 1) * 128 - 1. For every slot, emitting_group_per_pair differs from receiving_group_per_pair by at most 2; the difference 2 is reached in both directions. `active_pair_slots`: slots at or past a device's count are not live and hold arbitrary blocks that still satisfy the other promises; some device has all 256 slots live. `landing_site_triple`: particle p of device k = p div 16384 (device row r = p div 131072, column c = k mod 8) deposits into grid rows r * 32 - 16 to (r + 1) * 32 + 15 and columns c * 512 to (c + 1) * 512 - 1; both row limits are reached. At most 4096 of one device's particles lie below its own rows and at most 4096 above them, and both counts 4096 are reached.
All inputs are finite; a program needn't handle non-finite values.
Results may differ from the reference program's by a relative error of at most 0.0003.
Values sent between devices are 32-bit elements; how exact they have to be, the bound alone decides.
No kernel may reach another device: no remote copies, remote signals or barrier semaphores. Data moves between devices by JAX's collectives and lax.ppermute only.
A program may use at most 128 MiB of HBM per device.

```python
import math
import jax
import jax.numpy as jnp
from jax import lax

LAYER_SITES_DOWN = 64
CX = 32
CY = 512
P_DEV = 16384
G = 16
HB = 2
ROWS = 16
COLS = 8
NB_DEV = 128
TILES_DEV = 256
GCAP = 4096
PARTICLES = 2097152
NBLK = 16384
MESH_LINE_TOTAL = 512
MESH_CROSS_TOTAL = 4096
BAND = 64


def tile_lists(key):
    subkeys = jax.random.split(jax.random.fold_in(key, 41), 4)
    device_total = ROWS * COLS
    tile_ids = jnp.arange(device_total * TILES_DEV, dtype=jnp.int32)
    owners = tile_ids // TILES_DEV
    slot_ids = tile_ids % TILES_DEV
    picked = jax.random.randint(subkeys[0], tile_ids.shape, 0, NB_DEV)
    offsets = jax.random.randint(subkeys[1], tile_ids.shape, -HB, HB + 1)
    local_block = jnp.where(slot_ids == 0, 0, jnp.where(slot_ids == 1, NB_DEV - 1, picked))
    targets = owners * NB_DEV + local_block
    reaches = jnp.where(slot_ids == 0, -HB, jnp.where(slot_ids == 1, HB, offsets))
    sources = jnp.clip(targets + reaches, 0, NBLK - 1)
    least_count = max(2, TILES_DEV // 8)
    most_count = max(least_count, TILES_DEV // 2)
    counts = jax.random.randint(subkeys[2], (device_total,), least_count, most_count + 1)
    busiest = jax.random.randint(subkeys[3], (), 0, device_total)
    counts = jnp.where(jnp.arange(device_total) == busiest, TILES_DEV, counts)
    return (targets.astype(jnp.int32), sources.astype(jnp.int32), counts.astype(jnp.int32))


def draw_receiving_group_per_pair(key, part):
    return tile_lists(key)[0]


def draw_emitting_group_per_pair(key, part):
    return tile_lists(key)[1]


def draw_active_pair_slots(key, part):
    return tile_lists(key)[2]


def draw_landing_site_triple(key, part):
    subkeys = jax.random.split(jax.random.fold_in(key, 53), 10)
    device_total = ROWS * COLS
    particle_total = device_total * P_DEV
    particle_ids = jnp.arange(particle_total, dtype=jnp.int32)
    device_ids = particle_ids // P_DEV
    slot_ids = particle_ids % P_DEV
    row_ids = device_ids // COLS
    col_ids = device_ids % COLS
    device_list = jnp.arange(device_total, dtype=jnp.int32)
    device_row = device_list // COLS
    below_count = jax.random.randint(subkeys[0], (device_total,), GCAP // 2, GCAP + 1)
    above_count = jax.random.randint(subkeys[1], (device_total,), GCAP // 2, GCAP + 1)
    below_pick = jax.random.randint(subkeys[2], (), COLS, device_total)
    above_pick = jax.random.randint(subkeys[3], (), 0, device_total - COLS)
    below_count = jnp.where(device_list == below_pick, GCAP, below_count)
    below_count = jnp.where(device_row == 0, 0, below_count)
    above_count = jnp.where(device_list == above_pick, GCAP, above_count)
    above_count = jnp.where(device_row == ROWS - 1, 0, above_count)
    below_each = below_count[device_ids]
    above_each = above_count[device_ids]
    x_below = jax.random.randint(subkeys[4], (particle_total,), -G, 0)
    x_below = jnp.where(slot_ids == 0, -G, x_below)
    x_above = jax.random.randint(subkeys[5], (particle_total,), CX, CX + G)
    x_above = jnp.where(slot_ids == below_each, CX + G - 1, x_above)
    x_inside = jax.random.randint(subkeys[6], (particle_total,), 0, CX)
    x_local = jnp.where(slot_ids < below_each, x_below, jnp.where(slot_ids < below_each + above_each, x_above, x_inside))
    scores = jax.random.randint(subkeys[7], (device_total, P_DEV), 0, 2 ** 30 // P_DEV) * P_DEV + jnp.arange(P_DEV, dtype=jnp.int32)[None, :]
    shuffle = jnp.argsort(scores, axis=1, stable=True)
    x_local = jnp.take_along_axis(x_local.reshape(device_total, P_DEV), shuffle, axis=1).reshape(particle_total)
    grid_row = row_ids * CX + x_local
    grid_col = col_ids * CY + jax.random.randint(subkeys[8], (particle_total,), 0, CY)
    layer = jax.random.randint(subkeys[9], (particle_total,), 0, LAYER_SITES_DOWN)
    return jnp.stack([layer, grid_row, grid_col]).astype(jnp.int32)


def touch_ends(values, key, smallest, largest):
    index_at = [jax.random.randint(jax.random.fold_in(key, axis), (), 0, length) for axis, length in enumerate(values.shape)]
    longest = values.shape.index(max(values.shape))
    neighbour = index_at[:longest] + [(index_at[longest] + 1) % values.shape[longest]] + index_at[longest + 1:]
    return values.at[tuple(index_at)].set(smallest).at[tuple(neighbour)].set(largest)


def steps_of(own_key, shape, cuts, smallest, high):
    level = 1.0
    for position, parts in cuts:
        heights = jax.random.uniform(jax.random.fold_in(jax.random.fold_in(own_key, 6), position), (parts,), jnp.float32, smallest / len(cuts), high / len(cuts))
        level = level * jnp.repeat(jnp.exp(heights), shape[position] // parts).reshape((-1,) + (1,) * (len(shape) - 1 - position))
    return level


def centred(stream_key, dims, deviation, most, shards=(), kind=jnp.bfloat16):
    factor_of = steps_of(stream_key, dims, shards, -0.22, 0.18) if shards else 1.0
    result = jax.random.normal(stream_key, dims, jnp.float32) * deviation * factor_of
    return jnp.minimum(jnp.maximum(result, -most), most).astype(kind)


def setup_inputs(seed: int = 0) -> dict:
    arg_keys = jax.random.split(jax.random.key(seed), 11)
    particle_locations = centred(arg_keys[0], (3, PARTICLES), 0.5, 3.0, ((1, 128),), jnp.float32)
    particle_speeds = centred(arg_keys[1], (3, PARTICLES), 0.5, 3.0, ((1, 128),), jnp.float32)
    particle_bulk = jnp.clip(jnp.exp(math.log(2.0) - 1.3862944 * jax.random.uniform(arg_keys[2], (PARTICLES,), jnp.float32) ** steps_of(arg_keys[2], (PARTICLES,), ((0, 128),), -0.2, 0.2)), 0.5, 2.0)
    receiving_group_per_pair = draw_receiving_group_per_pair(jax.random.fold_in(arg_keys[10], 71), 0)
    emitting_group_per_pair = draw_emitting_group_per_pair(jax.random.fold_in(arg_keys[10], 71), 0)
    active_pair_slots = draw_active_pair_slots(jax.random.fold_in(arg_keys[10], 71), 0)
    landing_site_triple = draw_landing_site_triple(jax.random.fold_in(arg_keys[10], 71), 0)
    landing_weight_octants = touch_ends(jax.random.randint(arg_keys[7], (PARTICLES,), 1, 9), jax.random.fold_in(arg_keys[7], 1), 1, 8).astype(jnp.int32)
    thermal_excess = centred(arg_keys[8], (LAYER_SITES_DOWN, MESH_LINE_TOTAL, MESH_CROSS_TOTAL), 1.0, 6.0, ((1, 16), (2, 8)), jnp.float32)
    molten_strip_midlines = jax.random.randint(arg_keys[9], (2,), 0, MESH_LINE_TOTAL).astype(jnp.int32)
    return dict(particle_locations=particle_locations, particle_speeds=particle_speeds, particle_bulk=particle_bulk, receiving_group_per_pair=receiving_group_per_pair, emitting_group_per_pair=emitting_group_per_pair, active_pair_slots=active_pair_slots, landing_site_triple=landing_site_triple, landing_weight_octants=landing_weight_octants, thermal_excess=thermal_excess, molten_strip_midlines=molten_strip_midlines)


stiffness = 0.0078125
damping = 0.00390625
time_step = 0.5
depth_scale = 12.0
conduct = 0.1
laser_power = 0.5


def tile_force(target, source):
    offset = target[:, 0:3, :, None] - source[:, 0:3, None, :]
    weight = jnp.exp(-0.5 * jnp.sum(offset * offset, axis=1))
    relative = target[:, 3:6, :, None] - source[:, 3:6, None, :]
    repulse = jnp.sum(weight[:, None] * offset, axis=3)
    friction = jnp.sum(weight[:, None] * relative, axis=3)
    return stiffness * repulse - damping * friction


def neighbours(array):
    return (array[2:, 1:-1, 1:-1], array[:-2, 1:-1, 1:-1], array[1:-1, 2:, 1:-1],
            array[1:-1, :-2, 1:-1], array[1:-1, 1:-1, 2:], array[1:-1, 1:-1, :-2])


def thermal_advance(field_now, granular_share, mesh_line_number, band_row):
    conductance = conduct * (1.0 + 0.5 * jnp.tanh(field_now)) / (1.0 + granular_share)
    centre = field_now[1:-1, 1:-1, 1:-1]
    centre_cond = conductance[1:-1, 1:-1, 1:-1]
    change = jnp.zeros_like(centre)
    for near_field, near_cond in zip(neighbours(field_now), neighbours(conductance)):
        change = change + 0.5 * (centre_cond + near_cond) * (near_field - centre)
    beam_row = laser_power * jnp.exp(-jnp.square((mesh_line_number - band_row) / BAND))
    heating = beam_row[None, :, None] * granular_share[1:-1, 1:-1, 1:-1]
    return centre + change + heating


def reference(particle_locations, particle_speeds, particle_bulk, receiving_group_per_pair, emitting_group_per_pair, active_pair_slots, landing_site_triple, landing_weight_octants, thermal_excess, molten_strip_midlines):
    states = jnp.concatenate([particle_locations, particle_speeds], axis=0).reshape(6, NBLK, 128).transpose(1, 0, 2)
    tile_total = receiving_group_per_pair.shape[0]
    tile_order = jnp.arange(tile_total, dtype=jnp.int32)
    tile_live = (tile_order % TILES_DEV) < active_pair_slots[tile_order // TILES_DEV]
    group_size = math.gcd(tile_total, 64)

    def one_group(pair_ids):
        return tile_force(states[pair_ids[0]], states[pair_ids[1]])

    forces = lax.map(one_group, (receiving_group_per_pair.reshape(-1, group_size), emitting_group_per_pair.reshape(-1, group_size)))
    forces = forces.reshape(tile_total, 3, 128) * tile_live[:, None, None].astype(forces.dtype)
    summed = jnp.zeros((NBLK, 3, 128), jnp.float32).at[receiving_group_per_pair].add(forces)
    forces_all = summed.transpose(1, 0, 2).reshape(3, PARTICLES)
    advanced_speeds = particle_speeds + time_step * forces_all
    advanced_locations = particle_locations + time_step * advanced_speeds
    charge = particle_bulk * landing_weight_octants.astype(jnp.float32) * 0.125 * (1.0 + 0.5 * jnp.tanh(advanced_locations[2]))
    levels = jnp.arange(LAYER_SITES_DOWN, dtype=jnp.float32)
    profile = jnp.exp(-jnp.square((levels[:, None] - landing_site_triple[0][None, :].astype(jnp.float32)) / depth_scale)) * charge[None, :]
    column = landing_site_triple[1] * MESH_CROSS_TOTAL + landing_site_triple[2]
    packing_share_per_site = jnp.zeros((LAYER_SITES_DOWN, MESH_LINE_TOTAL * MESH_CROSS_TOTAL), jnp.float32).at[:, column].add(profile).reshape(LAYER_SITES_DOWN, MESH_LINE_TOTAL, MESH_CROSS_TOTAL)
    mesh_line_number = jnp.arange(MESH_LINE_TOTAL, dtype=jnp.float32)
    share_with_margin = jnp.pad(packing_share_per_site, 1)
    central_portion = thermal_advance(jnp.pad(thermal_excess, 1), share_with_margin, mesh_line_number, molten_strip_midlines[0].astype(jnp.float32))
    advanced_thermal_excess = thermal_advance(jnp.pad(central_portion, 1), share_with_margin, mesh_line_number, molten_strip_midlines[1].astype(jnp.float32))
    return advanced_locations, advanced_speeds, packing_share_per_site, advanced_thermal_excess
```

```python
import math

import jax
import jax.numpy as jnp
from jax import lax
from jax.experimental import pallas as pl
from jax.experimental.pallas import tpu as pltpu
from jax.sharding import PartitionSpec as P

F32 = jnp.float32
BF16 = jnp.bfloat16
I32 = jnp.int32

DEPTH = 64
CX = 32
CY = 512
NPART = 16384
G = 16
HB = 2
NB = 128
NEXT = NB + 2 * HB
SLOTS = 256
BAND = 64.0
BIN = 256
LOG2E = 1.4426950408889634
VMEM_LIMIT = 56 * 1024 * 1024
UNROLL = 4

VSPEC = pl.BlockSpec(memory_space=pltpu.VMEM)
SSPEC = pl.BlockSpec(memory_space=pltpu.SMEM)


def iota(shape, dim):
    return lax.broadcasted_iota(I32, shape, dim)


def partner(a, step, axis, low):
    size = a.shape[axis]
    return jnp.where(low, pltpu.roll(a, size - step, axis), pltpu.roll(a, step, axis))


def cross_stage(ks, cs, step, axis, low):
    nk, nc = [], []
    for k, c in zip(ks, cs):
        pk = partner(k, step, axis, low)
        pc = partner(c, step, axis, low)
        m = jnp.where(low, jnp.minimum(k, pk), jnp.maximum(k, pk))
        nk.append(m)
        nc.append(jnp.where(m != k, pc, c))
    return nk, nc


def vreg_stage(ks, cs, j, descending):
    ks, cs = list(ks), list(cs)
    for r in range(16):
        if r & (1 << j):
            continue
        a, b = r, r | (1 << j)
        if descending(r):
            a, b = b, a
        less = ks[b] < ks[a]
        ks[a], ks[b] = jnp.minimum(ks[a], ks[b]), jnp.maximum(ks[a], ks[b])
        cs[a], cs[b] = jnp.where(less, cs[b], cs[a]), jnp.where(less, cs[a], cs[b])
    return ks, cs


def bitonic(ks, cs):
    sub = iota((8, 128), 0)
    lane = iota((8, 128), 1)
    up = lambda r: False

    def low_stages(ks, cs, top):
        for j in range(top, 3, -1):
            step = 1 << (j - 4)
            ks, cs = cross_stage(ks, cs, step, 0, (sub & step) == 0)
        for j in range(min(top, 3), -1, -1):
            ks, cs = vreg_stage(ks, cs, j, up)
        return ks, cs

    for k in range(1, 4):
        for j in range(k - 1, -1, -1):
            ks, cs = vreg_stage(ks, cs, j, lambda r: bool(r & (1 << k)))
    for k in range(4, 7):
        flip = -((sub >> (k - 4)) & 1)
        ks = [a ^ flip for a in ks]
        ks, cs = low_stages(ks, cs, k - 1)
        ks = [a ^ flip for a in ks]

    def phase(k, carry):
        ks, cs = list(carry[:16]), list(carry[16:])
        flip = -((lane >> (k - 7)) & 1)
        ks = [a ^ flip for a in ks]

        def lane_step(t, inner):
            step = jnp.left_shift(jnp.int32(1), k - 8 - t)
            low = (lane & step) == 0
            nk, nc = cross_stage(list(inner[:16]), list(inner[16:]), step, 1, low)
            return tuple(nk) + tuple(nc)

        out = lax.fori_loop(0, k - 7, lane_step, tuple(ks) + tuple(cs))
        ks, cs = low_stages(list(out[:16]), list(out[16:]), 6)
        ks = [a ^ flip for a in ks]
        return tuple(ks) + tuple(cs)

    out = lax.fori_loop(7, 15, phase, tuple(ks) + tuple(cs))
    return list(out[:16]), list(out[16:])


def split3(a):
    h1 = a.astype(BF16)
    r = a - h1.astype(F32)
    h2 = r.astype(BF16)
    h3 = (r - h2.astype(F32)).astype(BF16)
    return h1, h2, h3


def particle_kernel(
    tgt, src, cnt, loc, vel, halo_lo, halo_hi, key, wb,
    nloc, nvel, skey, schg, last, send_lo, send_hi,
    left, right, stat, acc, zrow,
):
    wide = 4 * 128

    def prepare(x3, v3, at, width):
        pad = jnp.zeros((5, width), F32)
        x = jnp.concatenate([x3, pad], axis=0)
        v = jnp.concatenate([v3, pad], axis=0)
        row = iota((8, width), 0)
        xs = x * math.sqrt(LOG2E)
        q = 0.5 * jnp.sum(xs * xs, axis=0, keepdims=True)
        full = jnp.where(row < 3, xs, jnp.where(row < 5, q, 0.0))
        h = [p.astype(F32) for p in split3(full)]

        def mix(a, b, is_target):
            base = h[a]
            if b is None:
                return jnp.where(row < 3, base, 0.0)
            if is_target:
                return jnp.where(row < 3, base, jnp.where(row == 3, h[b], jnp.where(row == 4, 1.0, 0.0)))
            return jnp.where(row < 3, base, jnp.where(row == 3, -1.0, jnp.where(row == 4, -h[b], 0.0)))

        extra = [0, 1, 2, None, None, None]
        ta = [0, 0, 1, 1, 0, 2]
        sa = [0, 1, 0, 1, 2, 0]
        for p in range(0, 6, 2):
            lt = jnp.concatenate([mix(ta[p], extra[p], True), mix(ta[p + 1], extra[p + 1], True)], axis=0)
            rt = jnp.concatenate([mix(sa[p], extra[p], False), mix(sa[p + 1], extra[p + 1], False)], axis=0)
            left[pl.ds(8 * p, 16), pl.ds(at, width)] = lt.astype(BF16)
            right[pl.ds(8 * p, 16), pl.ds(at, width)] = rt.astype(BF16)
        w = (2.0 * x - v) * (1.0 / 256.0)
        wh = w.astype(BF16).astype(F32)
        wl = w - wh
        w2 = jnp.concatenate([jnp.where(row == 3, 1.0, wh), wl], axis=0)
        stat[:, pl.ds(at, width)] = w2.astype(BF16)

    prepare(halo_lo[0:3, :], halo_lo[3:6, :], 0, HB * 128)
    prepare(halo_hi[0:3, :], halo_hi[3:6, :], (NB + HB) * 128, HB * 128)

    def prep(i, carry):
        at = pl.multiple_of(i * wide, wide)
        prepare(loc[:, pl.ds(at, wide)], vel[:, pl.ds(at, wide)], pl.multiple_of(at + HB * 128, 128), wide)
        return carry

    lax.fori_loop(0, NPART // wide, prep, 0)
    acc[...] = jnp.zeros_like(acc)
    live = cnt[0]

    def tiles(g, carry):
        outs = []
        for u in range(UNROLL):
            t = g * UNROLL + u
            a = tgt[t] & (NB - 1)
            b = a + (src[t] - tgt[t]) + HB
            lm = left[:, pl.ds(pl.multiple_of((a + HB) * 128, 128), 128)]
            rm = right[:, pl.ds(pl.multiple_of(b * 128, 128), 128)]
            arg = lax.dot_general(rm, lm, (((0,), (0,)), ((), ())), preferred_element_type=F32)
            g_mn = jnp.exp2(arg)
            gh = g_mn.astype(BF16)
            gl = (g_mn - gh.astype(F32)).astype(BF16)
            s = stat[:, pl.ds(pl.multiple_of(b * 128, 128), 128)]
            out = jnp.dot(
                jnp.concatenate([s, s], axis=1),
                jnp.concatenate([gh, gl], axis=0),
                preferred_element_type=F32,
            )
            home = jnp.where(t < live, a, NB)
            outs.append((home, out[0:8] + out[8:16]))
        for home, out in outs:
            at = pl.multiple_of(home * 8, 8)
            acc[pl.ds(at, 8), :] = acc[pl.ds(at, 8), :] + out
        return carry

    lax.fori_loop(0, (live + UNROLL - 1) // UNROLL, tiles, 0)

    def advance(i, carry):
        for u in range(8):
            b = i * 8 + u
            at = pl.multiple_of(b * 128, 128)
            x = loc[:, pl.ds(at, 128)]
            v = vel[:, pl.ds(at, 128)]
            f = acc[pl.ds(pl.multiple_of(b * 8, 8), 8), :]
            w = (2.0 * x - v) * (1.0 / 256.0)
            force = w * f[3:4] - f[0:3]
            nv = v + 0.5 * force
            nx = x + 0.5 * nv
            nvel[:, pl.ds(at, 128)] = nv
            nloc[:, pl.ds(at, 128)] = nx
            zrow[pl.ds(b, 1), :] = nx[2:3]
        return carry

    lax.fori_loop(0, NB // 8, advance, 0)

    charge = wb[...] * (1.0 + 0.5 * jnp.tanh(zrow[...]))
    keys = key[...]
    ks = [keys[8 * r : 8 * r + 8] for r in range(16)]
    cs = [charge[8 * r : 8 * r + 8] for r in range(16)]
    ks, cs = bitonic(ks, cs)
    last[...] = ks[15][7:8]
    kt = jnp.concatenate(ks, axis=0)
    ct = jnp.concatenate(cs, axis=0)
    kt = jnp.transpose(kt)
    ct = jnp.transpose(ct)
    skey[...] = kt
    schg[...] = ct
    for ref, at in ((send_lo, 0), (send_hi, 96)):
        kk = kt[at : at + 32]
        ref[0:32] = (kk >> 15).astype(F32)
        ref[32:64] = ((kk >> 6) & 511).astype(F32)
        ref[64:96] = (kk & 63).astype(F32)
        ref[96:128] = ct[at : at + 32]


def particles(tgt, src, cnt, loc, vel, halo_lo, halo_hi, key, wb):
    sd = jax.ShapeDtypeStruct
    return pl.pallas_call(
        particle_kernel,
        out_shape=(
            sd((3, NPART), F32), sd((3, NPART), F32),
            sd((128, 128), I32), sd((128, 128), F32), sd((1, 128), I32),
            sd((128, 128), F32), sd((128, 128), F32),
        ),
        in_specs=[SSPEC] * 3 + [VSPEC] * 6,
        out_specs=(VSPEC,) * 7,
        scratch_shapes=[
            pltpu.VMEM((48, NEXT * 128), BF16),
            pltpu.VMEM((48, NEXT * 128), BF16),
            pltpu.VMEM((16, NEXT * 128), BF16),
            pltpu.VMEM(((NB + 1) * 8, 128), F32),
            pltpu.VMEM((NB, 128), F32),
        ],
        compiler_params=pltpu.CompilerParams(vmem_limit_bytes=VMEM_LIMIT),
        name="particle_step",
    )(tgt, src, cnt, loc, vel, halo_lo, halo_hi, key, wb)


OWN, RECV = 128, 32
BATCHES = OWN + 2 * RECV
DUMMY = BATCHES


def deposit_kernel(
    last, last_lo, last_hi, skey, schg, recv_lo, recv_hi,
    share, row_lo, row_hi, col_lo, col_hi,
    cells, prof, pile,
):
    own = skey[...]
    cells[0:OWN] = (own >> 6) - G * CY
    for ref, at, shift in ((recv_lo, OWN, -(G + CX)), (recv_hi, OWN + RECV, CX - G)):
        x = ref[0:32].astype(I32) + shift
        cells[at : at + RECV] = x * CY + ref[32:64].astype(I32)
    cells[DUMMY : DUMMY + 8] = jnp.full((8, 128), -1, I32)
    prof[DUMMY] = jnp.zeros((128, 128), BF16)
    level = iota((DEPTH, 128), 0).astype(F32)
    scale = math.sqrt(LOG2E) / 12.0

    def profile(z, charge):
        d = (level - z) * scale
        p = jnp.exp2(-(d * d)) * charge
        hi = p.astype(BF16)
        lo = (p - hi.astype(F32)).astype(BF16)
        return jnp.concatenate([hi, lo], axis=0)

    def own_profiles(i, carry):
        for u in range(4):
            b = i * 4 + u
            z = (skey[pl.ds(b, 1), :] & 63).astype(F32)
            prof[b] = profile(z, schg[pl.ds(b, 1), :])
        return carry

    lax.fori_loop(0, OWN // 4, own_profiles, 0)

    def recv_profiles(i, carry):
        for ref, at in ((recv_lo, OWN), (recv_hi, OWN + RECV)):
            for u in range(2):
                b = i * 2 + u
                prof[at + b] = profile(ref[pl.ds(64 + b, 1), :], ref[pl.ds(96 + b, 1), :])
        return carry

    lax.fori_loop(0, RECV // 2, recv_profiles, 0)

    def clear(i, carry):
        pile[i] = jnp.zeros((DEPTH, BIN), F32)
        return carry

    lax.fori_loop(0, 2 * CX, clear, 0)
    spot = iota((BIN, 128), 0)

    def walk(base, count, last_bin, first_bin):
        def seek(i, s):
            b = last_bin(i)
            return s[0] + (b < first_bin).astype(I32), s[1] + (b < 2 * CX).astype(I32)

        start, stop = lax.fori_loop(0, count, seek, (jnp.int32(0), jnp.int32(0)))
        stop = jnp.minimum(stop, count - 1)
        steps = stop - start + 1 + (2 * CX - 1 - first_bin)

        def step(g, state):
            i, j = state
            work = []
            for u in range(UNROLL):
                ii = jnp.where(i <= stop, base + i, DUMMY)
                work.append((ii, j))
                more = jnp.logical_and(last_bin(jnp.minimum(i, count - 1)) > j, j < 2 * CX - 1)
                j = jnp.where(more, j + 1, j)
                i = jnp.where(more, i, jnp.minimum(i + 1, count))
            outs = []
            for ii, jj in work:
                row = cells[pl.ds(ii, 1), :] - jj * BIN
                hot = jnp.where(spot == row, 1.0, 0.0).astype(BF16)
                out = lax.dot_general(prof[ii], hot, (((1,), (1,)), ((), ())), preferred_element_type=F32)
                outs.append(out[:DEPTH] + out[DEPTH:])
            for (ii, jj), out in zip(work, outs):
                pile[jj] = pile[jj] + out
            return i, j

        @pl.when(start <= stop)
        def _():
            lax.fori_loop(0, (steps + UNROLL - 1) // UNROLL, step, (start, jnp.int32(first_bin)))

    walk(0, OWN, lambda i: (last[i] >> 14) - 2 * G, 0)
    walk(OWN, RECV, lambda i: last_lo[i], 0)
    walk(OWN + RECV, RECV, lambda i: last_hi[i], 2 * G)

    row_lo[:, :BIN] = pile[0]
    row_lo[:, BIN:] = pile[1]
    row_hi[:, :BIN] = pile[2 * CX - 2]
    row_hi[:, BIN:] = pile[2 * CX - 1]
    lane = iota((8, 128), 1)
    sub = iota((8, 512), 0)

    def flip(t, carry):
        xg = t // 8
        zg = lax.rem(t, 8)
        z0 = pl.multiple_of(zg * 8, 8)
        x0 = pl.multiple_of(xg * 8, 8)
        a = []
        for i in range(8):
            bin0 = (x0 + i) * 2
            a.append(jnp.concatenate([pile[bin0, pl.ds(z0, 8), :], pile[bin0 + 1, pl.ds(z0, 8), :]], axis=1))
        for d in (1, 2, 4):
            b = list(a)
            low = (sub & d) == 0
            for i in range(8):
                if i & d:
                    continue
                p, q = a[i], a[i | d]
                b[i] = jnp.where(low, p, pltpu.roll(q, d, 0))
                b[i | d] = jnp.where(low, pltpu.roll(p, 8 - d, 0), q)
            a = b
        c0 = jnp.where(zg == 0, jnp.zeros((8, 128), F32), col_lo[pl.ds(x0, 8), :])
        c1 = jnp.where(zg == 0, jnp.zeros((8, 128), F32), col_hi[pl.ds(x0, 8), :])
        for k in range(8):
            share[z0 + k, pl.ds(x0, 8), :] = a[k]
            z = z0 + k
            c0 = jnp.where(lane == z, pltpu.roll(a[k][:, :128], z, 1), c0)
            c1 = jnp.where(lane == z, pltpu.roll(a[k][:, 384:], z + 1, 1), c1)
        col_lo[pl.ds(x0, 8), :] = c0
        col_hi[pl.ds(x0, 8), :] = c1
        return carry

    lax.fori_loop(0, 32, flip, 0)


def deposit(last, last_lo, last_hi, skey, schg, recv_lo, recv_hi):
    sd = jax.ShapeDtypeStruct
    return pl.pallas_call(
        deposit_kernel,
        out_shape=(
            sd((DEPTH, CX, CY), F32),
            sd((DEPTH, CY), F32), sd((DEPTH, CY), F32),
            sd((CX, 128), F32), sd((CX, 128), F32),
        ),
        in_specs=[SSPEC] * 3 + [VSPEC] * 4,
        out_specs=(VSPEC,) * 5,
        scratch_shapes=[
            pltpu.VMEM((BATCHES + 8, 128), I32),
            pltpu.VMEM((BATCHES + 1, 128, 128), BF16),
            pltpu.VMEM((2 * CX, DEPTH, BIN), F32),
        ],
        compiler_params=pltpu.CompilerParams(vmem_limit_bytes=VMEM_LIMIT),
        name="deposit",
    )(last, last_lo, last_hi, skey, schg, recv_lo, recv_hi)


def edges_kernel(left, right, top, bottom, row_lo, row_hi, col_lo, col_hi):
    row_lo[...] = top[:, 0, :]
    row_hi[...] = bottom[:, 7, :]
    lane = iota((CX, 128), 1)
    c0 = jnp.zeros((CX, 128), F32)
    c1 = jnp.zeros((CX, 128), F32)
    for z in range(DEPTH):
        a = left[z] if z == 0 else pltpu.roll(left[z], z, 1)
        c0 = jnp.where(lane == z, a, c0)
        c1 = jnp.where(lane == z, pltpu.roll(right[z], z + 1, 1), c1)
    col_lo[...] = c0
    col_hi[...] = c1


def edges(cells):
    sd = jax.ShapeDtypeStruct
    return pl.pallas_call(
        edges_kernel,
        grid=(1,),
        out_shape=(
            sd((DEPTH, CY), F32), sd((DEPTH, CY), F32),
            sd((CX, 128), F32), sd((CX, 128), F32),
        ),
        in_specs=[
            pl.BlockSpec((DEPTH, CX, 128), lambda i: (0, 0, 0)),
            pl.BlockSpec((DEPTH, CX, 128), lambda i: (0, 0, CY // 128 - 1)),
            pl.BlockSpec((DEPTH, 8, CY), lambda i: (0, 0, 0)),
            pl.BlockSpec((DEPTH, 8, CY), lambda i: (0, CX // 8 - 1, 0)),
        ],
        out_specs=(
            pl.BlockSpec((DEPTH, CY), lambda i: (0, 0)), pl.BlockSpec((DEPTH, CY), lambda i: (0, 0)),
            pl.BlockSpec((CX, 128), lambda i: (0, 0)), pl.BlockSpec((CX, 128), lambda i: (0, 0)),
        ),
        compiler_params=pltpu.CompilerParams(vmem_limit_bytes=VMEM_LIMIT),
        name="temperature_edges",
    )(cells, cells, cells, cells)


def half_kappa(u, v):
    return 0.05 * (1.0 + 0.5 * jnp.tanh(u)) / (1.0 + v)


def heat_kernel(
    with_edges, beam, u_ref, v_ref, ur_lo, ur_hi, uc_lo, uc_hi, vr_lo, vr_hi, vc_lo, vc_hi, out, *rest
):
    if with_edges:
        row_lo, row_hi, col_lo, col_hi = rest[:4]
        rest = rest[4:]
    kr_lo, kr_hi, kc_lo, kc_hi, kz, fz = rest
    kr_lo[...] = half_kappa(ur_lo[...], vr_lo[...])
    kr_hi[...] = half_kappa(ur_hi[...], vr_hi[...])
    kc_lo[...] = half_kappa(uc_lo[...], vc_lo[...])
    kc_hi[...] = half_kappa(uc_hi[...], vc_hi[...])
    if with_edges:
        col_lo[...] = jnp.zeros_like(col_lo)
        col_hi[...] = jnp.zeros_like(col_hi)
    lane = iota((CX, 128), 1)
    row = iota((CX, CY), 0)
    rows = (iota((CX, 128), 0).astype(F32) + beam[0]) * (1.0 / BAND)
    glow = 0.5 * jnp.exp(-(rows * rows))
    glow = jnp.concatenate([glow] * (CY // 128), axis=1)
    k0 = half_kappa(u_ref[0], v_ref[0])
    kz[0] = k0
    fz[...] = (k0 + 0.05) * u_ref[0]

    def plane(z, is_last):
        u = u_ref[z]
        k = kz[z & 1]
        if is_last:
            up = (k + 0.05) * (0.0 - u)
        else:
            un = u_ref[z + 1]
            kn = half_kappa(un, v_ref[z + 1])
            kz[(z + 1) & 1] = kn
            up = (k + kn) * (un - u)
        total = up - fz[...]
        fz[...] = up
        at = pl.ds(z, 1)
        below_u = jnp.where(row == 0, ur_lo[at, :], pltpu.roll(u, 1, 0))
        below_k = jnp.where(row == 0, kr_lo[at, :], pltpu.roll(k, 1, 0))
        f = (k + below_k) * (u - below_u)
        top = (k[24:32] + kr_hi[at, :]) * (ur_hi[at, :] - u[24:32])
        shifted = pltpu.roll(f, CX - 1, 0)
        above = jnp.concatenate([shifted[:24], jnp.where(row[24:32] == CX - 1, top, shifted[24:32])], axis=0)
        total = total + (above - f)

        def put(wide, tile, first):
            if first:
                return jnp.concatenate([jnp.where(lane == 0, tile, wide[:, :128]), wide[:, 128:]], axis=1)
            return jnp.concatenate([wide[:, :384], jnp.where(lane == 127, tile, wide[:, 384:])], axis=1)

        back = (128 - z) & 127
        left_u = put(pltpu.roll(u, 1, 1), pltpu.roll(uc_lo[...], back, 1), True)
        left_k = put(pltpu.roll(k, 1, 1), pltpu.roll(kc_lo[...], back, 1), True)
        f = (k + left_k) * (u - left_u)
        end_u = pltpu.roll(uc_hi[...], 127 - z, 1)
        end_k = pltpu.roll(kc_hi[...], 127 - z, 1)
        end = (k[:, 384:] + end_k) * (end_u - u[:, 384:])
        total = total + (put(pltpu.roll(f, CY - 1, 1), end, False) - f)
        new = u + total + glow * v_ref[z]
        out[z] = new
        if with_edges:
            row_lo[at, :] = new[0:1]
            row_hi[at, :] = new[CX - 1 : CX]
            col_lo[...] = jnp.where(lane == z, pltpu.roll(new[:, :128], z, 1), col_lo[...])
            col_hi[...] = jnp.where(lane == z, pltpu.roll(new[:, 384:], z + 1, 1), col_hi[...])

    def body(z, carry):
        plane(z, False)
        return carry

    lax.fori_loop(0, DEPTH - 1, body, 0)
    plane(DEPTH - 1, True)


def heat(beam, u, v, u_halo, v_halo, with_edges):
    sd = jax.ShapeDtypeStruct
    outs = [sd((DEPTH, CX, CY), F32)]
    if with_edges:
        outs += [sd((DEPTH, CY), F32)] * 2 + [sd((CX, 128), F32)] * 2
    return pl.pallas_call(
        lambda *refs: heat_kernel(with_edges, *refs),
        out_shape=tuple(outs),
        in_specs=[SSPEC] + [VSPEC] * 10,
        out_specs=(VSPEC,) * len(outs),
        scratch_shapes=[
            pltpu.VMEM((DEPTH, CY), F32), pltpu.VMEM((DEPTH, CY), F32),
            pltpu.VMEM((CX, 128), F32), pltpu.VMEM((CX, 128), F32),
            pltpu.VMEM((2, CX, CY), F32), pltpu.VMEM((CX, CY), F32),
        ],
        compiler_params=pltpu.CompilerParams(vmem_limit_bytes=VMEM_LIMIT),
        name="heat_step_one" if with_edges else "heat_step_two",
    )(beam, u, v, *u_halo, *v_halo)


def shift(value, axis, steps):
    count = lax.axis_size(axis)
    first, stop = max(0, -steps), min(count, count - steps)
    return lax.ppermute(value, axis, [(i, i + steps) for i in range(first, stop)])


def exchange(edge):
    row_lo, row_hi, col_lo, col_hi = edge
    return (
        shift(row_hi, "gx", 1),
        shift(row_lo, "gx", -1),
        shift(col_hi, "gy", 1),
        shift(col_lo, "gy", -1),
    )


def body(
    particle_locations,
    particle_speeds,
    particle_bulk,
    receiving_group_per_pair,
    emitting_group_per_pair,
    active_pair_slots,
    landing_site_triple,
    landing_weight_octants,
    thermal_excess,
    molten_strip_midlines,
):
    states = jnp.concatenate([particle_locations, particle_speeds], axis=0)
    width = HB * 128
    halo_lo = shift(states[:, NPART - width :], ("gx", "gy"), 1)
    halo_hi = shift(states[:, :width], ("gx", "gy"), -1)
    u_halo = exchange(edges(thermal_excess))

    row_start = lax.axis_index("gx") * CX
    col_start = lax.axis_index("gy") * CY
    px = landing_site_triple[1] - row_start + G
    py = landing_site_triple[2] - col_start
    key = ((px * CY + py) * DEPTH + landing_site_triple[0]).reshape(128, 128)
    wb = (particle_bulk * landing_weight_octants.astype(F32) * 0.125).reshape(128, 128)

    nloc, nvel, skey, schg, last, send_lo, send_hi = particles(
        receiving_group_per_pair, emitting_group_per_pair, active_pair_slots,
        particle_locations, particle_speeds, halo_lo, halo_hi, key, wb,
    )
    from_lo = shift(send_hi, "gx", 1)
    from_hi = shift(send_lo, "gx", -1)

    def last_bins(got, by):
        cell = (got[0:32, 127].astype(I32) + by) * CY + got[32:64, 127].astype(I32)
        return cell >> 8

    v, *v_edge = deposit(
        last.reshape(128), last_bins(from_lo, -(G + CX)), last_bins(from_hi, CX - G),
        skey, schg, from_lo, from_hi,
    )
    v_halo = exchange(v_edge)
    beam = (row_start - molten_strip_midlines).astype(F32)
    mid, *mid_edge = heat(beam[0:1], thermal_excess, v, u_halo, v_halo, True)
    (final,) = heat(beam[1:2], mid, v, exchange(mid_edge), v_halo, False)
    return nloc, nvel, v, final


def solution(mesh):
    placed = (
        P(None, ("gx", "gy")),
        P(None, ("gx", "gy")),
        P(("gx", "gy")),
        P(("gx", "gy")),
        P(("gx", "gy")),
        P(("gx", "gy")),
        P(None, ("gx", "gy")),
        P(("gx", "gy")),
        P(None, "gx", "gy"),
        P(),
    )
    return jax.shard_map(
        body,
        mesh=mesh,
        in_specs=placed,
        out_specs=(
            P(None, ("gx", "gy")),
            P(None, ("gx", "gy")),
            P(None, "gx", "gy"),
            P(None, "gx", "gy"),
        ),
        check_vma=False,
    )
```

```python
import math

import jax
import jax.numpy as jnp
from jax import lax
from jax.experimental import pallas as pl
from jax.experimental.pallas import tpu as pltpu
from jax.sharding import PartitionSpec as P

F32 = jnp.float32
BF16 = jnp.bfloat16
I32 = jnp.int32

DEPTH = 64
CX = 32
CY = 512
NPART = 16384
G = 16
HB = 2
NB = 128
NEXT = NB + 2 * HB
SLOTS = 256
BAND = 64.0
BIN = 256
LOG2E = 1.4426950408889634
VMEM_LIMIT = 56 * 1024 * 1024
TILE_UNROLL = 32
WALK_UNROLL = 16
XW = CX + 4
BINS = 2 * XW
SEND = 128 + 8 * DEPTH

VSPEC = pl.BlockSpec(memory_space=pltpu.VMEM)
SSPEC = pl.BlockSpec(memory_space=pltpu.SMEM)
ASPEC = pl.BlockSpec(memory_space=pl.ANY)


def iota(shape, dim):
    return lax.broadcasted_iota(I32, shape, dim)


def partner(a, step, axis, low):
    size = a.shape[axis]
    return jnp.where(low, pltpu.roll(a, size - step, axis), pltpu.roll(a, step, axis))


def cross_stage(ks, cs, step, axis, low):
    nk, nc = [], []
    for k, c in zip(ks, cs):
        pk = partner(k, step, axis, low)
        pc = partner(c, step, axis, low)
        m = jnp.where(low, jnp.minimum(k, pk), jnp.maximum(k, pk))
        nk.append(m)
        nc.append(jnp.where(m != k, pc, c))
    return nk, nc


def vreg_stage(ks, cs, j, descending):
    ks, cs = list(ks), list(cs)
    for r in range(16):
        if r & (1 << j):
            continue
        a, b = r, r | (1 << j)
        if descending(r):
            a, b = b, a
        less = ks[b] < ks[a]
        ks[a], ks[b] = jnp.minimum(ks[a], ks[b]), jnp.maximum(ks[a], ks[b])
        cs[a], cs[b] = jnp.where(less, cs[b], cs[a]), jnp.where(less, cs[a], cs[b])
    return ks, cs


def bitonic(ks, cs):
    sub = iota((8, 128), 0)
    lane = iota((8, 128), 1)
    up = lambda r: False

    def low_stages(ks, cs, top):
        for j in range(top, 3, -1):
            step = 1 << (j - 4)
            ks, cs = cross_stage(ks, cs, step, 0, (sub & step) == 0)
        for j in range(min(top, 3), -1, -1):
            ks, cs = vreg_stage(ks, cs, j, up)
        return ks, cs

    for k in range(1, 4):
        for j in range(k - 1, -1, -1):
            ks, cs = vreg_stage(ks, cs, j, lambda r: bool(r & (1 << k)))
    for k in range(4, 7):
        flip = -((sub >> (k - 4)) & 1)
        ks = [a ^ flip for a in ks]
        ks, cs = low_stages(ks, cs, k - 1)
        ks = [a ^ flip for a in ks]

    def phase(k, carry):
        ks, cs = list(carry[:16]), list(carry[16:])
        flip = -((lane >> (k - 7)) & 1)
        ks = [a ^ flip for a in ks]

        def lane_step(t, inner):
            step = jnp.left_shift(jnp.int32(1), k - 8 - t)
            low = (lane & step) == 0
            nk, nc = cross_stage(list(inner[:16]), list(inner[16:]), step, 1, low)
            return tuple(nk) + tuple(nc)

        out = lax.fori_loop(0, k - 7, lane_step, tuple(ks) + tuple(cs))
        ks, cs = low_stages(list(out[:16]), list(out[16:]), 6)
        ks = [a ^ flip for a in ks]
        return tuple(ks) + tuple(cs)

    out = lax.fori_loop(7, 15, phase, tuple(ks) + tuple(cs))
    return list(out[:16]), list(out[16:])


def split3(a):
    h1 = a.astype(BF16)
    r = a - h1.astype(F32)
    h2 = r.astype(BF16)
    h3 = (r - h2.astype(F32)).astype(BF16)
    return h1, h2, h3


def particle_kernel(
    tgt, src, cnt, loc, vel, halo_lo, halo_hi, key, wb, urow,
    nloc, nvel, skey, schg, last, send_lo, send_hi,
    left, right, stat, acc, zrow,
):
    wide = 4 * 128

    def prepare(x3, v3, at, width):
        pad = jnp.zeros((5, width), F32)
        x = jnp.concatenate([x3, pad], axis=0)
        v = jnp.concatenate([v3, pad], axis=0)
        row = iota((8, width), 0)
        xs = x * math.sqrt(LOG2E)
        q = 0.5 * jnp.sum(xs * xs, axis=0, keepdims=True)
        full = jnp.where(row < 3, xs, jnp.where(row < 5, q, 0.0))
        h = [p.astype(F32) for p in split3(full)]

        def mix(a, b, is_target):
            base = h[a]
            if b is None:
                return jnp.where(row < 3, base, 0.0)
            if is_target:
                return jnp.where(row < 3, base, jnp.where(row == 3, h[b], jnp.where(row == 4, 1.0, 0.0)))
            return jnp.where(row < 3, base, jnp.where(row == 3, -1.0, jnp.where(row == 4, -h[b], 0.0)))

        extra = [0, 1, 2, None, None, None]
        ta = [0, 0, 1, 1, 0, 2]
        sa = [0, 1, 0, 1, 2, 0]
        for p in range(0, 6, 2):
            lt = jnp.concatenate([mix(ta[p], extra[p], True), mix(ta[p + 1], extra[p + 1], True)], axis=0)
            rt = jnp.concatenate([mix(sa[p], extra[p], False), mix(sa[p + 1], extra[p + 1], False)], axis=0)
            left[pl.ds(8 * p, 16), pl.ds(at, width)] = lt.astype(BF16)
            right[pl.ds(8 * p, 16), pl.ds(at, width)] = rt.astype(BF16)
        w = (2.0 * x - v) * (1.0 / 256.0)
        wh = w.astype(BF16).astype(F32)
        wl = w - wh
        w2 = jnp.concatenate([jnp.where(row == 3, 1.0, wh), wl], axis=0)
        stat[:, pl.ds(at, width)] = w2.astype(BF16)

    prepare(halo_lo[0:3, :], halo_lo[3:6, :], 0, HB * 128)
    prepare(halo_hi[0:3, :], halo_hi[3:6, :], (NB + HB) * 128, HB * 128)

    def prep(i, carry):
        at = pl.multiple_of(i * wide, wide)
        prepare(loc[:, pl.ds(at, wide)], vel[:, pl.ds(at, wide)], pl.multiple_of(at + HB * 128, 128), wide)
        return carry

    lax.fori_loop(0, NPART // wide, prep, 0)
    acc[...] = jnp.zeros_like(acc)
    live = cnt[0]

    def tiles(g, carry):
        outs = []
        for u in range(TILE_UNROLL):
            t = g * TILE_UNROLL + u
            a = tgt[t] & (NB - 1)
            b = a + (src[t] - tgt[t]) + HB
            lm = left[:, pl.ds(pl.multiple_of((a + HB) * 128, 128), 128)]
            rm = right[:, pl.ds(pl.multiple_of(b * 128, 128), 128)]
            arg = lax.dot_general(rm, lm, (((0,), (0,)), ((), ())), preferred_element_type=F32)
            g_mn = jnp.exp2(arg)
            gh = g_mn.astype(BF16)
            gl = (g_mn - gh.astype(F32)).astype(BF16)
            s = stat[:, pl.ds(pl.multiple_of(b * 128, 128), 128)]
            out = jnp.dot(
                jnp.concatenate([s, s], axis=1),
                jnp.concatenate([gh, gl], axis=0),
                preferred_element_type=F32,
            )
            home = jnp.where(t < live, a, NB)
            outs.append((home, out[0:8] + out[8:16]))
        for home, out in outs:
            at = pl.multiple_of(home * 8, 8)
            acc[pl.ds(at, 8), :] = acc[pl.ds(at, 8), :] + out
        return carry

    lax.fori_loop(0, (live + TILE_UNROLL - 1) // TILE_UNROLL, tiles, 0)

    def advance(i, carry):
        for u in range(8):
            b = i * 8 + u
            at = pl.multiple_of(b * 128, 128)
            x = loc[:, pl.ds(at, 128)]
            v = vel[:, pl.ds(at, 128)]
            f = acc[pl.ds(pl.multiple_of(b * 8, 8), 8), :]
            w = (2.0 * x - v) * (1.0 / 256.0)
            force = w * f[3:4] - f[0:3]
            nv = v + 0.5 * force
            nx = x + 0.5 * nv
            nvel[:, pl.ds(at, 128)] = nv
            nloc[:, pl.ds(at, 128)] = nx
            zrow[pl.ds(b, 1), :] = nx[2:3]
        return carry

    lax.fori_loop(0, NB // 8, advance, 0)

    charge = wb[...] * (1.0 + 0.5 * jnp.tanh(zrow[...]))
    keys = key[...]
    ks = [keys[8 * r : 8 * r + 8] for r in range(16)]
    cs = [charge[8 * r : 8 * r + 8] for r in range(16)]
    ks, cs = bitonic(ks, cs)
    last[...] = ks[15][7:8]
    kt = jnp.concatenate(ks, axis=0)
    ct = jnp.concatenate(cs, axis=0)
    kt = jnp.transpose(kt)
    ct = jnp.transpose(ct)
    skey[...] = kt
    schg[...] = ct
    for ref, at in ((send_lo, 0), (send_hi, 96)):
        kk = kt[at : at + 32]
        ref[0:32] = (kk >> 15).astype(F32)
        ref[32:64] = ((kk >> 6) & 511).astype(F32)
        ref[64:96] = (kk & 63).astype(F32)
        ref[96:128] = ct[at : at + 32]
    for r in range(4):
        ref = send_lo if r < 2 else send_hi
        for c in range(4):
            at = 128 + ((r % 2) * 4 + c) * DEPTH
            ref[at : at + DEPTH] = urow[r, :, 128 * c : 128 * c + 128]


def particles(tgt, src, cnt, loc, vel, halo_lo, halo_hi, key, wb, urow):
    sd = jax.ShapeDtypeStruct
    return pl.pallas_call(
        particle_kernel,
        out_shape=(
            sd((3, NPART), F32), sd((3, NPART), F32),
            sd((128, 128), I32), sd((128, 128), F32), sd((1, 128), I32),
            sd((SEND, 128), F32), sd((SEND, 128), F32),
        ),
        in_specs=[SSPEC] * 3 + [VSPEC] * 7,
        out_specs=(VSPEC,) * 7,
        scratch_shapes=[
            pltpu.VMEM((48, NEXT * 128), BF16),
            pltpu.VMEM((48, NEXT * 128), BF16),
            pltpu.VMEM((16, NEXT * 128), BF16),
            pltpu.VMEM(((NB + 1) * 8, 128), F32),
            pltpu.VMEM((NB, 128), F32),
        ],
        compiler_params=pltpu.CompilerParams(vmem_limit_bytes=VMEM_LIMIT),
        name="particle_step",
    )(tgt, src, cnt, loc, vel, halo_lo, halo_hi, key, wb, urow)


OWN, RECV = 128, 32


def profile(z, charge):
    level = iota((DEPTH, 128), 0).astype(F32)
    d = (level - z) * (math.sqrt(LOG2E) / 12.0)
    p = jnp.exp2(-(d * d)) * charge
    hi = p.astype(BF16)
    lo = (p - hi.astype(F32)).astype(BF16)
    return jnp.concatenate([hi, lo], axis=0)


def walk(pile, cells, prof, base, count, dummy, last_bin, first_bin, end_bin):
    spot = iota((BIN, 128), 0)

    def seek(i, s):
        b = last_bin(i)
        return s[0] + (b < first_bin).astype(I32), s[1] + (b <= end_bin).astype(I32)

    start, stop = lax.fori_loop(0, count, seek, (jnp.int32(0), jnp.int32(0)), unroll=8)
    stop = jnp.minimum(stop, count - 1)
    steps = stop - start + 1 + (end_bin - first_bin)

    def step(g, state):
        i, j = state
        work = []
        for u in range(WALK_UNROLL):
            work.append((jnp.where(i <= stop, base + i, dummy), j))
            more = jnp.logical_and(last_bin(jnp.minimum(i, count - 1)) > j, j < end_bin)
            j = jnp.where(more, j + 1, j)
            i = jnp.where(more, i, jnp.minimum(i + 1, count))
        outs = []
        for ii, jj in work:
            row = cells[pl.ds(ii, 1), :] - jj * BIN
            hot = jnp.where(spot == row, 1.0, 0.0).astype(BF16)
            out = lax.dot_general(prof[ii], hot, (((1,), (1,)), ((), ())), preferred_element_type=F32)
            outs.append(out[:DEPTH] + out[DEPTH:])
        for (ii, jj), out in zip(work, outs):
            pile[jj] = pile[jj] + out
        return i, j

    @pl.when(start <= stop)
    def _():
        lax.fori_loop(0, (steps + WALK_UNROLL - 1) // WALK_UNROLL, step, (start, jnp.int32(first_bin)))


def own_deposit_kernel(last, skey, schg, pile, row_lo, row_hi, cells, prof):
    own = skey[...]
    cells[0:OWN] = (own >> 6) - (G - HB) * CY
    cells[OWN : OWN + 8] = jnp.full((8, 128), -1, I32)
    prof[OWN] = jnp.zeros((128, 128), BF16)

    def profiles(i, carry):
        for u in range(8):
            b = i * 8 + u
            z = (skey[pl.ds(b, 1), :] & 63).astype(F32)
            prof[b] = profile(z, schg[pl.ds(b, 1), :])
        return carry

    lax.fori_loop(0, OWN // 8, profiles, 0)

    def clear(i, carry):
        pile[i] = jnp.zeros((DEPTH, BIN), F32)
        return carry

    lax.fori_loop(0, BINS, clear, 0)
    walk(pile, cells, prof, 0, OWN, OWN, lambda i: (last[i] >> 14) - 2 * (G - HB), 0, BINS - 1)
    for ref, x0 in ((row_lo, 0), (row_hi, CX - 2)):
        for r in range(2):
            for c in range(4):
                at = (r * 4 + c) * DEPTH
                ref[at : at + DEPTH] = pile[2 * (x0 + r + 2) + c // 2, :, 128 * (c % 2) : 128 * (c % 2) + 128]


def own_deposit(last, skey, schg):
    sd = jax.ShapeDtypeStruct
    return pl.pallas_call(
        own_deposit_kernel,
        out_shape=(sd((BINS, DEPTH, BIN), F32), sd((8 * DEPTH, 128), F32), sd((8 * DEPTH, 128), F32)),
        in_specs=[SSPEC, VSPEC, VSPEC],
        out_specs=(VSPEC,) * 3,
        scratch_shapes=[
            pltpu.VMEM((OWN + 8, 128), I32),
            pltpu.VMEM((OWN + 1, 128, 128), BF16),
        ],
        compiler_params=pltpu.CompilerParams(vmem_limit_bytes=VMEM_LIMIT),
        name="own_deposit",
    )(last, skey, schg)


def edge_deposit_kernel(
    last_lo, last_hi, meta, pile_in, recv_lo, recv_hi, part_lo, part_hi, ucol,
    pile_out, vrow, pay_lo, pay_hi,
    pile, cells, prof, packs, sems,
):
    load = pltpu.make_async_copy(pile_in, pile, sems.at[0])
    load.start()
    for ref, at, shift in ((recv_lo, 0, HB - G - CX), (recv_hi, RECV, HB + CX - G)):
        x = ref[0:32].astype(I32) + shift
        cells[at : at + RECV] = x * CY + ref[32:64].astype(I32)
    dummy = 2 * RECV
    cells[dummy : dummy + 8] = jnp.full((8, 128), -1, I32)
    prof[dummy] = jnp.zeros((128, 128), BF16)

    def profiles(i, carry):
        for ref, at in ((recv_lo, 0), (recv_hi, RECV)):
            for u in range(4):
                b = i * 4 + u
                prof[at + b] = profile(ref[pl.ds(64 + b, 1), :], ref[pl.ds(96 + b, 1), :])
        return carry

    lax.fori_loop(0, RECV // 4, profiles, 0)
    load.wait()
    half = 2 * (2 + G)
    walk(pile, cells, prof, 0, RECV, dummy, lambda i: last_lo[i], 4, half - 1)
    walk(pile, cells, prof, RECV, RECV, dummy, lambda i: last_hi[i], half, 2 * (2 + CX) - 1)
    for ref, x0, flag in ((part_lo, 0, meta[2]), (part_hi, CX + 2, meta[3])):
        for r in range(2):
            for c in range(4):
                at = (r * 4 + c) * DEPTH
                b = 2 * (x0 + r) + c // 2
                cols = slice(128 * (c % 2), 128 * (c % 2) + 128)
                pile[b, :, cols] = flag * (pile[b, :, cols] + ref[at : at + DEPTH])
    save = pltpu.make_async_copy(pile, pile_out, sems.at[0])
    save.start()
    for n, x in enumerate((0, 1, 2, CX + 1, CX + 2, CX + 3)):
        vrow[n, :, :BIN] = pile[2 * x]
        vrow[n, :, BIN:] = pile[2 * x + 1]
    lane = iota((DEPTH, 128), 1)
    packs[...] = jnp.zeros_like(packs)

    def pick(row, at):
        a = pile[2 * row, :, 0:128]
        b = pile[2 * row + 1, :, 128:256]
        for n, (t, by) in enumerate(((a, at), (a, at + 127), (b, at + 2), (b, at + 1))):
            packs[n] = jnp.where(lane == at, pltpu.roll(t, by & 127, 1), packs[n])

    def picks(x, carry):
        pick(x + 2, x)
        return carry

    lax.fori_loop(0, CX, picks, 0)
    pick(1, CX)
    pick(CX + 2, CX + 1)
    base = 128 + 4 * DEPTH
    for pay, recv_col, near, far in ((pay_lo, 0, 0, 1), (pay_hi, 3, 3, 2)):
        lo = recv_lo[base + recv_col * DEPTH : base + recv_col * DEPTH + DEPTH]
        hi = recv_hi[128 + recv_col * DEPTH : 128 + recv_col * DEPTH + DEPTH]
        by = 0 if recv_col == 0 else 1
        corner = jnp.where(lane == CX, pltpu.roll(lo, CX + by, 1), 0.0)
        corner = jnp.where(lane == CX + 1, pltpu.roll(hi, CX + 1 + by, 1), corner)
        t = jnp.transpose(jnp.concatenate([corner, packs[near]], axis=0))
        pay[0:CX] = t[0:CX] + ucol[near]
        pay[CX : CX + 8] = t[CX : CX + 8]
        t = jnp.transpose(jnp.concatenate([jnp.zeros((DEPTH, 128), F32), packs[far]], axis=0))
        pay[40 : 40 + CX] = t[0:CX] + ucol[far]
        pay[40 + CX : 80] = jnp.zeros((8, 128), F32)
    save.wait()


def edge_deposit(last_lo, last_hi, meta, pile, recv_lo, recv_hi, part_lo, part_hi, ucol):
    sd = jax.ShapeDtypeStruct
    return pl.pallas_call(
        edge_deposit_kernel,
        out_shape=(
            sd((BINS, DEPTH, BIN), F32), sd((6, DEPTH, CY), F32),
            sd((80, 128), F32), sd((80, 128), F32),
        ),
        in_specs=[SSPEC] * 3 + [ASPEC] + [VSPEC] * 5,
        out_specs=(ASPEC, VSPEC, VSPEC, VSPEC),
        scratch_shapes=[
            pltpu.VMEM((BINS, DEPTH, BIN), F32),
            pltpu.VMEM((2 * RECV + 8, 128), I32),
            pltpu.VMEM((2 * RECV + 1, 128, 128), BF16),
            pltpu.VMEM((4, DEPTH, 128), F32),
            pltpu.SemaphoreType.DMA((1,)),
        ],
        compiler_params=pltpu.CompilerParams(vmem_limit_bytes=VMEM_LIMIT),
        name="edge_deposit",
    )(last_lo, last_hi, meta, pile, recv_lo, recv_hi, part_lo, part_hi, ucol)


def share_kernel(pile, share):
    sub = iota((8, CY), 0)

    def turn(xg, carry):
        x0 = pl.multiple_of(xg * 8, 8)
        a = [
            jnp.concatenate([pile[2 * (x0 + i + 2)], pile[2 * (x0 + i + 2) + 1]], axis=1)
            for i in range(8)
        ]
        for d in (1, 2, 4):
            b = list(a)
            low = (sub & d) == 0
            for i in range(8):
                if i & d:
                    continue
                p, q = a[i], a[i | d]
                b[i] = jnp.where(low, p, pltpu.roll(q, d, 0))
                b[i | d] = jnp.where(low, pltpu.roll(p, 8 - d, 0), q)
            a = b
        for k in range(8):
            share[k, pl.ds(x0, 8), :] = a[k]
        return carry

    lax.fori_loop(0, CX // 8, turn, 0)


def share_layout(pile):
    return pl.pallas_call(
        share_kernel,
        grid=(DEPTH // 8,),
        out_shape=jax.ShapeDtypeStruct((DEPTH, CX, CY), F32),
        in_specs=[pl.BlockSpec((BINS, 8, BIN), lambda i: (0, i, 0))],
        out_specs=pl.BlockSpec((8, CX, CY), lambda i: (i, 0, 0)),
        compiler_params=pltpu.CompilerParams(vmem_limit_bytes=VMEM_LIMIT),
        cost_estimate=pl.CostEstimate(flops=1 << 23, bytes_accessed=1 << 23, transcendentals=0),
        name="share_layout",
    )(pile)


def edges_kernel(left, right, top, bottom, urow, ucol):
    urow[0] = top[:, 0, :]
    urow[1] = top[:, 1, :]
    urow[2] = bottom[:, 6, :]
    urow[3] = bottom[:, 7, :]
    lane = iota((CX, 128), 1)
    acc = [jnp.zeros((CX, 128), F32)] * 4
    for z in range(DEPTH):
        for n, (ref, by) in enumerate(((left, z), (left, z + 127), (right, z + 2), (right, z + 1))):
            by = by & 127
            a = ref[z] if by == 0 else pltpu.roll(ref[z], by, 1)
            acc[n] = jnp.where(lane == z, a, acc[n])
    for n in range(4):
        ucol[n] = acc[n]


def edges(cells):
    sd = jax.ShapeDtypeStruct
    return pl.pallas_call(
        edges_kernel,
        grid=(1,),
        out_shape=(sd((4, DEPTH, CY), F32), sd((4, CX, 128), F32)),
        in_specs=[
            pl.BlockSpec((DEPTH, CX, 128), lambda i: (0, 0, 0)),
            pl.BlockSpec((DEPTH, CX, 128), lambda i: (0, 0, CY // 128 - 1)),
            pl.BlockSpec((DEPTH, 8, CY), lambda i: (0, 0, 0)),
            pl.BlockSpec((DEPTH, 8, CY), lambda i: (0, CX // 8 - 1, 0)),
        ],
        out_specs=(
            pl.BlockSpec((4, DEPTH, CY), lambda i: (0, 0, 0)),
            pl.BlockSpec((4, CX, 128), lambda i: (0, 0, 0)),
        ),
        compiler_params=pltpu.CompilerParams(vmem_limit_bytes=VMEM_LIMIT),
        name="temperature_edges",
    )(cells, cells, cells, cells)


def half_kappa(u, v):
    return 0.05 * (1.0 + 0.5 * jnp.tanh(u)) / (1.0 + v)


def flux(k, kn, u, un):
    return (k + kn) * (un - u)


def heat_kernel(
    meta, u_hbm, v_hbm, urow, recv_lo, recv_hi, vrow, pay_lo, pay_hi, got_lo, got_hi, out_hbm,
    us, vs, ms, kz, fz, row1, row2, mrow, col1, col2, sems,
):
    chunks = DEPTH // 8

    def fetch(c):
        at = pl.ds(pl.multiple_of(c * 8, 8), 8)
        return (
            pltpu.make_async_copy(u_hbm.at[at], us.at[at], sems.at[0, c]),
            pltpu.make_async_copy(v_hbm.at[at], vs.at[at], sems.at[1, c]),
        )

    for c in range(chunks):
        for copy in fetch(c):
            copy.start()

    def glow_of(rows):
        d = rows * (1.0 / BAND)
        return 0.5 * jnp.exp(-(d * d))

    lane = iota((CX, 128), 1)
    sub = iota((CX, 128), 0)
    lo_half = lane < DEPTH
    side = jnp.where(lo_half, meta[4], meta[5])
    glow1 = glow_of(sub.astype(F32) + meta[0])

    def stacks(a, b, at, size):
        p, q = a[at : at + size], b[at : at + size]
        low = iota((size, 128), 1) < DEPTH
        return jnp.where(low, p, pltpu.roll(q, DEPTH, 1)), jnp.where(low, pltpu.roll(p, DEPTH, 1), q)

    def column_step(outer, here, inner, ends):
        (uo, vo), (uh, vh), (ui, vi), (ue, ve) = outer, here, inner, ends
        kh = half_kappa(uh, vh)
        ke = half_kappa(ue, ve)
        total = flux(kh, half_kappa(uo, vo), uh, uo) + flux(kh, half_kappa(ui, vi), uh, ui)

        def near(a, e, n, pad):
            below = jnp.where(sub == 0, e[0:1], pltpu.roll(a, 1, 0))
            above = jnp.where(sub == CX - 1, e[1:2], pltpu.roll(a, CX - 1, 0))
            up = jnp.where((lane & (DEPTH - 1)) == DEPTH - 1, pad, pltpu.roll(a, 127, 1))
            down = jnp.where((lane & (DEPTH - 1)) == 0, pad, pltpu.roll(a, 1, 1))
            return below, above, up, down

        for kn, un in zip(near(kh, ke, 0, 0.05), near(uh, ue, 0, 0.0)):
            total = total + flux(kh, kn, uh, un)
        return uh + total + glow1 * vh, kh

    outer = stacks(got_lo, got_hi, 40, CX)
    here = stacks(got_lo, got_hi, 0, CX)
    inner = stacks(pay_lo, pay_hi, 0, CX)
    next_in = stacks(pay_lo, pay_hi, 40, CX)
    corners = stacks(got_lo, got_hi, CX, 8)
    mid_out, k_out = column_step(outer, here, inner, corners)
    mid_in, k_in = column_step(here, inner, next_in, stacks(pay_lo, pay_hi, CX, 8))
    mid_out = mid_out * side
    sign = jnp.where(lo_half, 1.0, -1.0)
    col1[...] = sign * flux(k_out, k_in, here[0], inner[0])
    col2[...] = sign * flux(half_kappa(mid_out, here[1]), half_kappa(mid_in, inner[1]), mid_out, mid_in)

    lane_w = iota((DEPTH, CY), 1)
    sub_w = iota((DEPTH, CY), 0)
    tail = [jnp.transpose(jnp.concatenate([g[CX : CX + 8]] * 16, axis=0)) for g in (got_lo, got_hi)]
    for n in range(2):
        recv = recv_lo if n == 0 else recv_hi

        def got_row(r):
            base = 128 + r * 4 * DEPTH
            return jnp.concatenate([recv[base + c * DEPTH : base + (c + 1) * DEPTH] for c in range(4)], axis=1)

        uo, uh = (got_row(0), got_row(1)) if n == 0 else (got_row(1), got_row(0))
        ui = urow[0] if n == 0 else urow[3]
        vo, vh, vi = (vrow[0], vrow[1], vrow[2]) if n == 0 else (vrow[5], vrow[4], vrow[3])
        kh = half_kappa(uh, vh)
        ki = half_kappa(ui, vi)
        total = flux(kh, half_kappa(uo, vo), uh, uo) + flux(kh, ki, uh, ui)
        first_u = pltpu.roll(tail[0][:DEPTH], (128 - n) & 127, 1) if n else tail[0][:DEPTH]
        first_v = pltpu.roll(tail[0][DEPTH:], (128 - n) & 127, 1) if n else tail[0][DEPTH:]
        end_u = pltpu.roll(tail[1][:DEPTH], 127 - n, 1)
        end_v = pltpu.roll(tail[1][DEPTH:], 127 - n, 1)
        first_k, end_k = half_kappa(first_u, first_v), half_kappa(end_u, end_v)

        def near(a, first, end, pad):
            left = jnp.where(lane_w == 0, jnp.concatenate([first] * 4, axis=1), pltpu.roll(a, 1, 1))
            right = jnp.where(lane_w == CY - 1, jnp.concatenate([end] * 4, axis=1), pltpu.roll(a, CY - 1, 1))
            up = jnp.where(sub_w == DEPTH - 1, pad, pltpu.roll(a, DEPTH - 1, 0))
            down = jnp.where(sub_w == 0, pad, pltpu.roll(a, 1, 0))
            return left, right, up, down

        for kn, un in zip(near(kh, first_k, end_k, 0.05), near(uh, first_u, end_u, 0.0)):
            total = total + flux(kh, kn, uh, un)
        row_at = meta[0] + (-1.0 if n == 0 else float(CX))
        gl = glow_of(jnp.full((1, CY), 1.0, F32) * row_at)
        mrow[DEPTH * n : DEPTH * n + DEPTH] = (uh + total + gl * vh) * meta[2 + n]
        row1[DEPTH * n : DEPTH * n + DEPTH] = flux(kh, ki, uh, ui) if n == 0 else flux(ki, kh, ui, uh)

    glow2 = glow_of(sub.astype(F32) + meta[1])
    tiles = range(4)

    def load(ref, z):
        return [ref[z, :, 128 * c : 128 * c + 128] for c in tiles]

    def plane(src, dst, row_f, col_f, glow, z, is_last):
        u = load(src, z)
        k = load(kz, z & 1)
        v = load(vs, z)
        if is_last:
            up = [(k[c] + 0.05) * (0.0 - u[c]) for c in tiles]
        else:
            un = load(src, z + 1)
            vn = load(vs, z + 1)
            kn = [half_kappa(un[c], vn[c]) for c in tiles]
            for c in tiles:
                kz[(z + 1) & 1, :, 128 * c : 128 * c + 128] = kn[c]
            up = [flux(k[c], kn[c], u[c], un[c]) for c in tiles]
        cols = col_f[...]
        row_first = row_f[pl.ds(z, 1), :]
        row_end = row_f[pl.ds(z + DEPTH, 1), :]
        edge0 = pltpu.roll(cols, (128 - z) & 127, 1)
        edge1 = pltpu.roll(cols, 63 - z, 1)
        ru = [pltpu.roll(u[c], 1, 1) for c in tiles]
        rk = [pltpu.roll(k[c], 1, 1) for c in tiles]
        g = []
        for c in tiles:
            if c == 0:
                g.append(jnp.where(lane == 0, edge0, flux(k[0], rk[0], ru[0], u[0])))
            else:
                pu = jnp.where(lane == 0, ru[c - 1], ru[c])
                pk = jnp.where(lane == 0, rk[c - 1], rk[c])
                g.append(flux(k[c], pk, pu, u[c]))
        rg = [pltpu.roll(g[c], 127, 1) for c in tiles]
        for c in tiles:
            at = slice(128 * c, 128 * c + 128)
            gn = jnp.where(lane == 127, rg[c + 1] if c < 3 else edge1, rg[c])
            f = flux(k[c], pltpu.roll(k[c], 1, 0), pltpu.roll(u[c], 1, 0), u[c])
            f = jnp.where(sub == 0, row_first[:, at], f)
            fn = jnp.where(sub == CX - 1, row_end[:, at], pltpu.roll(f, CX - 1, 0))
            total = (up[c] - fz[:, at]) + (fn - f) + (gn - g[c])
            fz[:, at] = up[c]
            dst[z, :, at] = u[c] + total + glow * v[c]

    def begin(src):
        u = load(src, 0)
        v = load(vs, 0)
        for c in tiles:
            at = slice(128 * c, 128 * c + 128)
            k = half_kappa(u[c], v[c])
            kz[0, :, at] = k
            fz[:, at] = (k + 0.05) * u[c]

    for copy in fetch(0):
        copy.wait()
    begin(us)

    def one(z, carry):
        @pl.when((z & 7) == 7)
        def _():
            for copy in fetch((z >> 3) + 1):
                copy.wait()

        plane(us, ms, row1, col1, glow1, z, False)
        return carry

    lax.fori_loop(0, DEPTH - 1, one, 0)
    plane(us, ms, row1, col1, glow1, DEPTH - 1, True)

    for n in range(2):
        mh = mrow[DEPTH * n : DEPTH * n + DEPTH]
        kh = half_kappa(mh, vrow[1] if n == 0 else vrow[4])
        mi = ms[:, 0 if n == 0 else CX - 1, :]
        ki = half_kappa(mi, vrow[2] if n == 0 else vrow[3])
        row2[DEPTH * n : DEPTH * n + DEPTH] = flux(kh, ki, mh, mi) if n == 0 else flux(ki, kh, mi, mh)

    def store(c):
        at = pl.ds(pl.multiple_of(c * 8, 8), 8)
        return pltpu.make_async_copy(us.at[at], out_hbm.at[at], sems.at[0, c])

    begin(ms)

    def two(z, carry):
        plane(ms, us, row2, col2, glow2, z, False)

        @pl.when((z & 7) == 7)
        def _():
            store(z >> 3).start()

        return carry

    lax.fori_loop(0, DEPTH - 1, two, 0)
    plane(ms, us, row2, col2, glow2, DEPTH - 1, True)
    store(chunks - 1).start()
    for c in range(chunks):
        store(c).wait()


def heat(meta, u, v, urow, recv_lo, recv_hi, vrow, pay_lo, pay_hi, got_lo, got_hi):
    plane = pltpu.VMEM((DEPTH, CX, CY), F32)
    rows = pltpu.VMEM((2 * DEPTH, CY), F32)
    column = pltpu.VMEM((CX, 128), F32)
    return pl.pallas_call(
        heat_kernel,
        out_shape=jax.ShapeDtypeStruct((DEPTH, CX, CY), F32),
        in_specs=[SSPEC, ASPEC, ASPEC] + [VSPEC] * 8,
        out_specs=ASPEC,
        scratch_shapes=[
            plane, plane, plane,
            pltpu.VMEM((2, CX, CY), F32), pltpu.VMEM((CX, CY), F32),
            rows, rows, rows, column, column,
            pltpu.SemaphoreType.DMA((2, DEPTH // 8)),
        ],
        compiler_params=pltpu.CompilerParams(vmem_limit_bytes=VMEM_LIMIT),
        name="two_heat_steps",
    )(meta, u, v, urow, recv_lo, recv_hi, vrow, pay_lo, pay_hi, got_lo, got_hi)


def shift(value, axis, steps):
    count = lax.axis_size(axis)
    first, stop = max(0, -steps), min(count, count - steps)
    return lax.ppermute(value, axis, [(i, i + steps) for i in range(first, stop)])


def body(
    particle_locations,
    particle_speeds,
    particle_bulk,
    receiving_group_per_pair,
    emitting_group_per_pair,
    active_pair_slots,
    landing_site_triple,
    landing_weight_octants,
    thermal_excess,
    molten_strip_midlines,
):
    states = jnp.concatenate([particle_locations, particle_speeds], axis=0)
    width = HB * 128
    halo_lo = shift(states[:, NPART - width :], ("gx", "gy"), 1)
    halo_hi = shift(states[:, :width], ("gx", "gy"), -1)
    urow, ucol = edges(thermal_excess)

    gx, gy = lax.axis_index("gx"), lax.axis_index("gy")
    row_start, col_start = gx * CX, gy * CY
    beam = row_start - molten_strip_midlines
    inside = jnp.stack([gx > 0, gx < lax.axis_size("gx") - 1, gy > 0, gy < lax.axis_size("gy") - 1])
    meta = jnp.concatenate([beam.astype(F32), inside.astype(F32)])
    px = landing_site_triple[1] - row_start + G
    py = landing_site_triple[2] - col_start
    key = ((px * CY + py) * DEPTH + landing_site_triple[0]).reshape(128, 128)
    wb = (particle_bulk * landing_weight_octants.astype(F32) * 0.125).reshape(128, 128)

    nloc, nvel, skey, schg, last, send_lo, send_hi = particles(
        receiving_group_per_pair, emitting_group_per_pair, active_pair_slots,
        particle_locations, particle_speeds, halo_lo, halo_hi, key, wb, urow,
    )
    recv_lo = shift(send_hi, "gx", 1)
    recv_hi = shift(send_lo, "gx", -1)
    pile, row_lo, row_hi = own_deposit(last.reshape(128), skey, schg)
    part_lo = shift(row_hi, "gx", 1)
    part_hi = shift(row_lo, "gx", -1)

    def last_bins(got, by):
        cell = (got[0:32, 127].astype(I32) + by) * CY + got[32:64, 127].astype(I32)
        return cell >> 8

    pile, vrow, pay_lo, pay_hi = edge_deposit(
        last_bins(recv_lo, HB - G - CX), last_bins(recv_hi, HB + CX - G), meta,
        pile, recv_lo, recv_hi, part_lo, part_hi, ucol,
    )
    got_lo = shift(pay_hi, "gy", 1)
    got_hi = shift(pay_lo, "gy", -1)
    share = share_layout(pile)
    final = heat(meta, thermal_excess, share, urow, recv_lo, recv_hi, vrow, pay_lo, pay_hi, got_lo, got_hi)
    return nloc, nvel, share, final


def solution(mesh):
    placed = (
        P(None, ("gx", "gy")),
        P(None, ("gx", "gy")),
        P(("gx", "gy")),
        P(("gx", "gy")),
        P(("gx", "gy")),
        P(("gx", "gy")),
        P(None, ("gx", "gy")),
        P(("gx", "gy")),
        P(None, "gx", "gy"),
        P(),
    )
    return jax.shard_map(
        body,
        mesh=mesh,
        in_specs=placed,
        out_specs=(
            P(None, ("gx", "gy")),
            P(None, ("gx", "gy")),
            P(None, "gx", "gy"),
            P(None, "gx", "gy"),
        ),
        check_vma=False,
    )
```

```python
import math

import jax
import jax.numpy as jnp
from jax import lax
from jax.experimental import pallas as pl
from jax.experimental.pallas import tpu as pltpu
from jax.sharding import PartitionSpec as P

F32 = jnp.float32
BF16 = jnp.bfloat16
I32 = jnp.int32

DEPTH = 64
CX = 32
CY = 512
NPART = 16384
G = 16
HB = 2
NB = 128
NEXT = NB + 2 * HB
SLOTS = 256
BAND = 64.0
BIN = 256
LOG2E = 1.4426950408889634
VMEM_LIMIT = 56 * 1024 * 1024
TILE_UNROLL = 32
WALK_UNROLL = 32
PLANES = 4
XW = CX + 4
BINS = 2 * XW
SEND = 128 + 8 * DEPTH + 8

VSPEC = pl.BlockSpec(memory_space=pltpu.VMEM)
SSPEC = pl.BlockSpec(memory_space=pltpu.SMEM)
ASPEC = pl.BlockSpec(memory_space=pl.ANY)


def iota(shape, dim):
    return lax.broadcasted_iota(I32, shape, dim)


def cross_stage(ks, cs, step, axis):
    at = iota((8, 128), axis)
    other = at ^ step
    low = (at & step) == 0
    nk, nc = [], []
    for k, c in zip(ks, cs):
        pk = jnp.take_along_axis(k, other, axis=axis)
        pc = jnp.take_along_axis(c, other, axis=axis)
        m = jnp.where(low, jnp.minimum(k, pk), jnp.maximum(k, pk))
        nk.append(m)
        nc.append(jnp.where(m != k, pc, c))
    return nk, nc


def vreg_stage(ks, cs, j, descending):
    ks, cs = list(ks), list(cs)
    for r in range(16):
        if r & (1 << j):
            continue
        a, b = r, r | (1 << j)
        if descending(r):
            a, b = b, a
        less = ks[b] < ks[a]
        ks[a], ks[b] = jnp.minimum(ks[a], ks[b]), jnp.maximum(ks[a], ks[b])
        cs[a], cs[b] = jnp.where(less, cs[b], cs[a]), jnp.where(less, cs[a], cs[b])
    return ks, cs


def bitonic(ks, cs):
    sub = iota((8, 128), 0)
    lane = iota((8, 128), 1)
    up = lambda r: False

    def low_stages(ks, cs, top):
        for j in range(top, 3, -1):
            step = 1 << (j - 4)
            ks, cs = cross_stage(ks, cs, step, 0)
        for j in range(min(top, 3), -1, -1):
            ks, cs = vreg_stage(ks, cs, j, up)
        return ks, cs

    for k in range(1, 4):
        for j in range(k - 1, -1, -1):
            ks, cs = vreg_stage(ks, cs, j, lambda r: bool(r & (1 << k)))
    for k in range(4, 7):
        flip = -((sub >> (k - 4)) & 1)
        ks = [a ^ flip for a in ks]
        ks, cs = low_stages(ks, cs, k - 1)
        ks = [a ^ flip for a in ks]

    def phase(k, carry):
        ks, cs = list(carry[:16]), list(carry[16:])
        flip = -((lane >> (k - 7)) & 1)
        ks = [a ^ flip for a in ks]

        def lane_step(t, inner):
            step = jnp.left_shift(jnp.int32(1), k - 8 - t)
            nk, nc = cross_stage(list(inner[:16]), list(inner[16:]), step, 1)
            return tuple(nk) + tuple(nc)

        out = lax.fori_loop(0, k - 7, lane_step, tuple(ks) + tuple(cs))
        ks, cs = low_stages(list(out[:16]), list(out[16:]), 6)
        ks = [a ^ flip for a in ks]
        return tuple(ks) + tuple(cs)

    out = lax.fori_loop(7, 15, phase, tuple(ks) + tuple(cs))
    return list(out[:16]), list(out[16:])


def split3(a):
    h1 = a.astype(BF16)
    r = a - h1.astype(F32)
    h2 = r.astype(BF16)
    h3 = (r - h2.astype(F32)).astype(BF16)
    return h1, h2, h3


def particle_kernel(
    tgt, src, cnt, origin, loc, vel, halo_lo, halo_hi, site, bulk, octants, urow,
    nloc, nvel, skey, schg, last, send_lo, send_hi,
    left, right, stat, acc, zrow, key,
):
    wide = 4 * 128

    def prepare(x3, v3, at, width):
        pad = jnp.zeros((5, width), F32)
        x = jnp.concatenate([x3, pad], axis=0)
        v = jnp.concatenate([v3, pad], axis=0)
        row = iota((8, width), 0)
        xs = x * math.sqrt(LOG2E)
        q = 0.5 * jnp.sum(xs * xs, axis=0, keepdims=True)
        full = jnp.where(row < 3, xs, jnp.where(row < 5, q, 0.0))
        h = [p.astype(F32) for p in split3(full)]

        def mix(a, b, is_target):
            base = h[a]
            if b is None:
                return jnp.where(row < 3, base, 0.0)
            if is_target:
                return jnp.where(row < 3, base, jnp.where(row == 3, h[b], jnp.where(row == 4, 1.0, 0.0)))
            return jnp.where(row < 3, base, jnp.where(row == 3, -1.0, jnp.where(row == 4, -h[b], 0.0)))

        extra = [0, 1, 2, None, None, None]
        ta = [0, 0, 1, 1, 0, 2]
        sa = [0, 1, 0, 1, 2, 0]
        for p in range(0, 6, 2):
            lt = jnp.concatenate([mix(ta[p], extra[p], True), mix(ta[p + 1], extra[p + 1], True)], axis=0)
            rt = jnp.concatenate([mix(sa[p], extra[p], False), mix(sa[p + 1], extra[p + 1], False)], axis=0)
            left[pl.ds(8 * p, 16), pl.ds(at, width)] = lt.astype(BF16)
            right[pl.ds(8 * p, 16), pl.ds(at, width)] = rt.astype(BF16)
        w = (2.0 * x - v) * (1.0 / 256.0)
        wh = w.astype(BF16).astype(F32)
        wl = w - wh
        w2 = jnp.concatenate([jnp.where(row == 3, 1.0, wh), wl], axis=0)
        stat[:, pl.ds(at, width)] = w2.astype(BF16)

    prepare(halo_lo[0:3, :], halo_lo[3:6, :], 0, HB * 128)
    prepare(halo_hi[0:3, :], halo_hi[3:6, :], (NB + HB) * 128, HB * 128)

    def prep(i, carry):
        at = pl.multiple_of(i * wide, wide)
        prepare(loc[:, pl.ds(at, wide)], vel[:, pl.ds(at, wide)], pl.multiple_of(at + HB * 128, 128), wide)
        return carry

    lax.fori_loop(0, NPART // wide, prep, 0)
    acc[...] = jnp.zeros_like(acc)
    live = cnt[0]

    def tiles(g, carry):
        outs = []
        for u in range(TILE_UNROLL):
            t = g * TILE_UNROLL + u
            a = tgt[t] & (NB - 1)
            b = a + (src[t] - tgt[t]) + HB
            lm = left[:, pl.ds(pl.multiple_of((a + HB) * 128, 128), 128)]
            rm = right[:, pl.ds(pl.multiple_of(b * 128, 128), 128)]
            arg = lax.dot_general(rm, lm, (((0,), (0,)), ((), ())), preferred_element_type=F32)
            g_mn = jnp.exp2(arg)
            gh = g_mn.astype(BF16)
            gl = (g_mn - gh.astype(F32)).astype(BF16)
            s = stat[:, pl.ds(pl.multiple_of(b * 128, 128), 128)]
            out = jnp.dot(
                jnp.concatenate([s, s], axis=1),
                jnp.concatenate([gh, gl], axis=0),
                preferred_element_type=F32,
            )
            home = jnp.where(t < live, a, NB)
            outs.append((home, out[0:8] + out[8:16]))
        for home, out in outs:
            at = pl.multiple_of(home * 8, 8)
            acc[pl.ds(at, 8), :] = acc[pl.ds(at, 8), :] + out
        return carry

    lax.fori_loop(0, (live + TILE_UNROLL - 1) // TILE_UNROLL, tiles, 0)

    def advance(i, carry):
        for u in range(8):
            b = i * 8 + u
            at = pl.multiple_of(b * 128, 128)
            x = loc[:, pl.ds(at, 128)]
            v = vel[:, pl.ds(at, 128)]
            f = acc[pl.ds(pl.multiple_of(b * 8, 8), 8), :]
            w = (2.0 * x - v) * (1.0 / 256.0)
            force = w * f[3:4] - f[0:3]
            nv = v + 0.5 * force
            nx = x + 0.5 * nv
            nvel[:, pl.ds(at, 128)] = nv
            nloc[:, pl.ds(at, 128)] = nx
            zrow[pl.ds(b, 1), :] = nx[2:3]
            p = site[:, pl.ds(at, 128)]
            cell = (p[1:2] - origin[0]) * CY + (p[2:3] - origin[1])
            key[pl.ds(b, 1), :] = cell * DEPTH + p[0:1]
        return carry

    lax.fori_loop(0, NB // 8, advance, 0)

    charge = bulk[...] * octants[...].astype(F32) * 0.125 * (1.0 + 0.5 * jnp.tanh(zrow[...]))
    keys = key[...]
    ks = [keys[8 * r : 8 * r + 8] for r in range(16)]
    cs = [charge[8 * r : 8 * r + 8] for r in range(16)]
    ks, cs = bitonic(ks, cs)
    last[...] = ks[15][7:8]
    kt = jnp.concatenate(ks, axis=0)
    ct = jnp.concatenate(cs, axis=0)
    kt = jnp.transpose(kt)
    ct = jnp.transpose(ct)
    skey[...] = kt
    schg[...] = ct
    for ref, at in ((send_lo, 0), (send_hi, 96)):
        kk = kt[at : at + 32]
        ref[0:32] = (kk >> 15).astype(F32)
        ref[32:64] = ((kk >> 6) & 511).astype(F32)
        ref[64:96] = (kk & 63).astype(F32)
        ref[96:128] = ct[at : at + 32]
    for r in range(4):
        ref = send_lo if r < 2 else send_hi
        for c in range(4):
            at = 128 + ((r % 2) * 4 + c) * DEPTH
            ref[at : at + DEPTH] = urow[r, :, 128 * c : 128 * c + 128]
    for ref in (send_lo, send_hi):
        ref[SEND - 8 : SEND] = jnp.broadcast_to(last[...].astype(F32), (8, 128))


def particles(tgt, src, cnt, origin, loc, vel, halo_lo, halo_hi, site, bulk, octants, urow):
    sd = jax.ShapeDtypeStruct
    return pl.pallas_call(
        particle_kernel,
        out_shape=(
            sd((3, NPART), F32), sd((3, NPART), F32),
            sd((128, 128), I32), sd((128, 128), F32), sd((1, 128), I32),
            sd((SEND, 128), F32), sd((SEND, 128), F32),
        ),
        in_specs=[SSPEC] * 4 + [VSPEC] * 8,
        out_specs=(VSPEC,) * 7,
        scratch_shapes=[
            pltpu.VMEM((48, NEXT * 128), BF16),
            pltpu.VMEM((48, NEXT * 128), BF16),
            pltpu.VMEM((16, NEXT * 128), BF16),
            pltpu.VMEM(((NB + 1) * 8, 128), F32),
            pltpu.VMEM((NB, 128), F32),
            pltpu.VMEM((NB, 128), I32),
        ],
        compiler_params=pltpu.CompilerParams(vmem_limit_bytes=VMEM_LIMIT),
        name="particle_step",
    )(tgt, src, cnt, origin, loc, vel, halo_lo, halo_hi, site, bulk, octants, urow)


OWN, RECV = 128, 32


def profile(z, charge):
    level = iota((DEPTH, 128), 0).astype(F32)
    d = (level - z) * (math.sqrt(LOG2E) / 12.0)
    p = jnp.exp2(-(d * d)) * charge
    hi = p.astype(BF16)
    lo = (p - hi.astype(F32)).astype(BF16)
    return jnp.concatenate([hi, lo], axis=0)


def walk(pile, cells, prof, base, count, dummy, last_bin, first_bin, end_bin):
    spot = iota((BIN, 128), 0)

    def seek(i, s):
        b = last_bin(i)
        return s[0] + (b < first_bin).astype(I32), s[1] + (b <= end_bin).astype(I32)

    start, stop = lax.fori_loop(0, count, seek, (jnp.int32(0), jnp.int32(0)), unroll=8)
    stop = jnp.minimum(stop, count - 1)
    steps = stop - start + 1 + (end_bin - first_bin)

    def step(g, state):
        i, j = state
        work = []
        for u in range(WALK_UNROLL):
            work.append((jnp.where(i <= stop, base + i, dummy), j))
            more = jnp.logical_and(last_bin(jnp.minimum(i, count - 1)) > j, j < end_bin)
            j = jnp.where(more, j + 1, j)
            i = jnp.where(more, i, jnp.minimum(i + 1, count))
        outs = []
        for ii, jj in work:
            row = cells[pl.ds(ii, 1), :] - jj * BIN
            hot = jnp.where(spot == row, 1.0, 0.0).astype(BF16)
            out = lax.dot_general(prof[ii], hot, (((1,), (1,)), ((), ())), preferred_element_type=F32)
            outs.append(out[:DEPTH] + out[DEPTH:])
        for (ii, jj), out in zip(work, outs):
            pile[jj] = pile[jj] + out
        return i, j

    @pl.when(start <= stop)
    def _():
        lax.fori_loop(0, (steps + WALK_UNROLL - 1) // WALK_UNROLL, step, (start, jnp.int32(first_bin)))


def own_deposit_kernel(last, skey, schg, pile, row_lo, row_hi, cells, prof):
    own = skey[...]
    cells[0:OWN] = (own >> 6) - (G - HB) * CY
    cells[OWN : OWN + 8] = jnp.full((8, 128), -1, I32)
    prof[OWN] = jnp.zeros((128, 128), BF16)

    def profiles(i, carry):
        for u in range(8):
            b = i * 8 + u
            z = (skey[pl.ds(b, 1), :] & 63).astype(F32)
            prof[b] = profile(z, schg[pl.ds(b, 1), :])
        return carry

    lax.fori_loop(0, OWN // 8, profiles, 0)

    def clear(i, carry):
        pile[i] = jnp.zeros((DEPTH, BIN), F32)
        return carry

    lax.fori_loop(0, BINS, clear, 0)
    walk(pile, cells, prof, 0, OWN, OWN, lambda i: (last[i] >> 14) - 2 * (G - HB), 0, BINS - 1)
    for ref, x0 in ((row_lo, 0), (row_hi, CX - 2)):
        for r in range(2):
            for c in range(4):
                at = (r * 4 + c) * DEPTH
                ref[at : at + DEPTH] = pile[2 * (x0 + r + 2) + c // 2, :, 128 * (c % 2) : 128 * (c % 2) + 128]


def own_deposit(last, skey, schg):
    sd = jax.ShapeDtypeStruct
    return pl.pallas_call(
        own_deposit_kernel,
        out_shape=(sd((BINS, DEPTH, BIN), F32), sd((8 * DEPTH, 128), F32), sd((8 * DEPTH, 128), F32)),
        in_specs=[SSPEC, VSPEC, VSPEC],
        out_specs=(VSPEC,) * 3,
        scratch_shapes=[
            pltpu.VMEM((OWN + 8, 128), I32),
            pltpu.VMEM((OWN + 1, 128, 128), BF16),
        ],
        compiler_params=pltpu.CompilerParams(vmem_limit_bytes=VMEM_LIMIT),
        name="own_deposit",
    )(last, skey, schg)


def edge_deposit_kernel(
    meta, pile_in, recv_lo, recv_hi, part_lo, part_hi, ucol,
    share, vrow, pay_lo, pay_hi,
    pile, cells, prof, packs, last_v, last_s, sems,
):
    load = pltpu.make_async_copy(pile_in, pile, sems.at[0])
    load.start()
    last_v[0:1] = recv_lo[SEND - 8 : SEND - 7].astype(I32)
    last_v[1:2] = recv_hi[SEND - 8 : SEND - 7].astype(I32)
    lasts = pltpu.make_async_copy(last_v, last_s, sems.at[1])
    lasts.start()
    for ref, at, shift in ((recv_lo, 0, HB - G - CX), (recv_hi, RECV, HB + CX - G)):
        x = ref[0:32].astype(I32) + shift
        cells[at : at + RECV] = x * CY + ref[32:64].astype(I32)
    dummy = 2 * RECV
    cells[dummy : dummy + 8] = jnp.full((8, 128), -1, I32)
    prof[dummy] = jnp.zeros((128, 128), BF16)

    def profiles(i, carry):
        for ref, at in ((recv_lo, 0), (recv_hi, RECV)):
            for u in range(4):
                b = i * 4 + u
                prof[at + b] = profile(ref[pl.ds(64 + b, 1), :], ref[pl.ds(96 + b, 1), :])
        return carry

    lax.fori_loop(0, RECV // 4, profiles, 0)
    lasts.wait()
    load.wait()
    half = 2 * (2 + G)
    walk(pile, cells, prof, 0, RECV, dummy, lambda i: (last_s[0, OWN - RECV + i] >> 14) + 2 * (HB - G - CX), 4, half - 1)
    walk(pile, cells, prof, RECV, RECV, dummy, lambda i: (last_s[1, i] >> 14) + 2 * (HB + CX - G), half, 2 * (2 + CX) - 1)
    for ref, x0, flag in ((part_lo, 0, meta[2]), (part_hi, CX + 2, meta[3])):
        for r in range(2):
            for c in range(4):
                at = (r * 4 + c) * DEPTH
                b = 2 * (x0 + r) + c // 2
                cols = slice(128 * (c % 2), 128 * (c % 2) + 128)
                pile[b, :, cols] = flag * (pile[b, :, cols] + ref[at : at + DEPTH])

    def turn(t):
        x = t >> 1
        cols = pl.ds(pl.multiple_of((t & 1) * BIN, BIN), BIN)
        return pltpu.make_async_copy(pile.at[t + 2 * HB], share.at[:, x, cols], sems.at[2 + t])

    def turn_start(t, carry):
        turn(t).start()
        return carry

    lax.fori_loop(0, 2 * CX, turn_start, 0)
    for n, x in enumerate((0, 1, 2, CX + 1, CX + 2, CX + 3)):
        vrow[n, :, :BIN] = pile[2 * x]
        vrow[n, :, BIN:] = pile[2 * x + 1]
    lane = iota((DEPTH, 128), 1)
    packs[...] = jnp.zeros_like(packs)

    def pick(row, at):
        a = pile[2 * row, :, 0:128]
        b = pile[2 * row + 1, :, 128:256]
        for n, (t, by) in enumerate(((a, at), (a, at + 127), (b, at + 2), (b, at + 1))):
            packs[n] = jnp.where(lane == at, pltpu.roll(t, by & 127, 1), packs[n])

    def picks(x, carry):
        pick(x + 2, x)
        return carry

    lax.fori_loop(0, CX, picks, 0)
    pick(1, CX)
    pick(CX + 2, CX + 1)
    base = 128 + 4 * DEPTH
    for pay, recv_col, near, far in ((pay_lo, 0, 0, 1), (pay_hi, 3, 3, 2)):
        lo = recv_lo[base + recv_col * DEPTH : base + recv_col * DEPTH + DEPTH]
        hi = recv_hi[128 + recv_col * DEPTH : 128 + recv_col * DEPTH + DEPTH]
        by = 0 if recv_col == 0 else 1
        corner = jnp.where(lane == CX, pltpu.roll(lo, CX + by, 1), 0.0)
        corner = jnp.where(lane == CX + 1, pltpu.roll(hi, CX + 1 + by, 1), corner)
        t = jnp.transpose(jnp.concatenate([corner, packs[near]], axis=0))
        pay[0:CX] = t[0:CX] + ucol[near]
        pay[CX : CX + 8] = t[CX : CX + 8]
        t = jnp.transpose(jnp.concatenate([jnp.zeros((DEPTH, 128), F32), packs[far]], axis=0))
        pay[40 : 40 + CX] = t[0:CX] + ucol[far]
        pay[40 + CX : 80] = jnp.zeros((8, 128), F32)

    def turn_wait(t, carry):
        turn(t).wait()
        return carry

    lax.fori_loop(0, 2 * CX, turn_wait, 0)


def edge_deposit(meta, pile, recv_lo, recv_hi, part_lo, part_hi, ucol):
    sd = jax.ShapeDtypeStruct
    return pl.pallas_call(
        edge_deposit_kernel,
        out_shape=(
            sd((DEPTH, CX, CY), F32), sd((6, DEPTH, CY), F32),
            sd((80, 128), F32), sd((80, 128), F32),
        ),
        in_specs=[SSPEC, ASPEC] + [VSPEC] * 5,
        out_specs=(ASPEC, VSPEC, VSPEC, VSPEC),
        scratch_shapes=[
            pltpu.VMEM((BINS, DEPTH, BIN), F32),
            pltpu.VMEM((2 * RECV + 8, 128), I32),
            pltpu.VMEM((2 * RECV + 1, 128, 128), BF16),
            pltpu.VMEM((4, DEPTH, 128), F32),
            pltpu.VMEM((2, 128), I32),
            pltpu.SMEM((2, 128), I32),
            pltpu.SemaphoreType.DMA((2 + 2 * CX,)),
        ],
        compiler_params=pltpu.CompilerParams(vmem_limit_bytes=VMEM_LIMIT),
        name="edge_deposit",
    )(meta, pile, recv_lo, recv_hi, part_lo, part_hi, ucol)


def edges_kernel(cells, urow, ucol, left, right, sems):
    rows = [
        pltpu.make_async_copy(cells.at[:, x, :], urow.at[r], sems.at[2 + r])
        for r, x in enumerate((0, 1, CX - 2, CX - 1))
    ]
    cols = [
        pltpu.make_async_copy(cells.at[:, :, pl.ds(at, 128)], ref, sems.at[n])
        for n, (ref, at) in enumerate(((left, 0), (right, CY - 128)))
    ]
    for copy in cols + rows:
        copy.start()
    for copy in cols:
        copy.wait()
    lane = iota((CX, 128), 1)
    acc = [jnp.zeros((CX, 128), F32)] * 4
    for z in range(DEPTH):
        for n, (ref, by) in enumerate(((left, z), (left, z + 127), (right, z + 2), (right, z + 1))):
            by = by & 127
            a = ref[z] if by == 0 else pltpu.roll(ref[z], by, 1)
            acc[n] = jnp.where(lane == z, a, acc[n])
    for n in range(4):
        ucol[n] = acc[n]
    for copy in rows:
        copy.wait()


def edges(cells):
    sd = jax.ShapeDtypeStruct
    return pl.pallas_call(
        edges_kernel,
        out_shape=(sd((4, DEPTH, CY), F32), sd((4, CX, 128), F32)),
        in_specs=[ASPEC],
        out_specs=(VSPEC, VSPEC),
        scratch_shapes=[
            pltpu.VMEM((DEPTH, CX, 128), F32),
            pltpu.VMEM((DEPTH, CX, 128), F32),
            pltpu.SemaphoreType.DMA((6,)),
        ],
        compiler_params=pltpu.CompilerParams(vmem_limit_bytes=VMEM_LIMIT),
        name="temperature_edges",
    )(cells)


def half_kappa(u, v):
    return 0.05 * (1.0 + 0.5 * jnp.tanh(u)) / (1.0 + v)


def flux(k, kn, u, un):
    return (k + kn) * (un - u)


def heat_kernel(
    meta, u_hbm, v_hbm, urow, recv_lo, recv_hi, vrow, pay_lo, pay_hi, got_lo, got_hi, out_hbm,
    us, vs, ms, kz, fz, row1, row2, mrow, col1, col2, sems,
):
    chunks = DEPTH // 8

    def fetch(c):
        at = pl.ds(pl.multiple_of(c * 8, 8), 8)
        return (
            pltpu.make_async_copy(u_hbm.at[at], us.at[at], sems.at[0, c]),
            pltpu.make_async_copy(v_hbm.at[at], vs.at[at], sems.at[1, c]),
        )

    for c in range(chunks):
        for copy in fetch(c):
            copy.start()

    def glow_of(rows):
        d = rows * (1.0 / BAND)
        return 0.5 * jnp.exp(-(d * d))

    lane = iota((CX, 128), 1)
    sub = iota((CX, 128), 0)
    lo_half = lane < DEPTH
    side = jnp.where(lo_half, meta[4], meta[5])
    glow1 = glow_of(sub.astype(F32) + meta[0])

    def stacks(a, b, at, size):
        p, q = a[at : at + size], b[at : at + size]
        low = iota((size, 128), 1) < DEPTH
        return jnp.where(low, p, pltpu.roll(q, DEPTH, 1)), jnp.where(low, pltpu.roll(p, DEPTH, 1), q)

    def column_step(outer, here, inner, ends):
        (uo, vo), (uh, vh), (ui, vi), (ue, ve) = outer, here, inner, ends
        kh = half_kappa(uh, vh)
        ke = half_kappa(ue, ve)
        total = flux(kh, half_kappa(uo, vo), uh, uo) + flux(kh, half_kappa(ui, vi), uh, ui)

        def near(a, e, n, pad):
            below = jnp.where(sub == 0, e[0:1], pltpu.roll(a, 1, 0))
            above = jnp.where(sub == CX - 1, e[1:2], pltpu.roll(a, CX - 1, 0))
            up = jnp.where((lane & (DEPTH - 1)) == DEPTH - 1, pad, pltpu.roll(a, 127, 1))
            down = jnp.where((lane & (DEPTH - 1)) == 0, pad, pltpu.roll(a, 1, 1))
            return below, above, up, down

        for kn, un in zip(near(kh, ke, 0, 0.05), near(uh, ue, 0, 0.0)):
            total = total + flux(kh, kn, uh, un)
        return uh + total + glow1 * vh, kh

    outer = stacks(got_lo, got_hi, 40, CX)
    here = stacks(got_lo, got_hi, 0, CX)
    inner = stacks(pay_lo, pay_hi, 0, CX)
    next_in = stacks(pay_lo, pay_hi, 40, CX)
    corners = stacks(got_lo, got_hi, CX, 8)
    mid_out, k_out = column_step(outer, here, inner, corners)
    mid_in, k_in = column_step(here, inner, next_in, stacks(pay_lo, pay_hi, CX, 8))
    mid_out = mid_out * side
    sign = jnp.where(lo_half, 1.0, -1.0)
    col1[...] = sign * flux(k_out, k_in, here[0], inner[0])
    col2[...] = sign * flux(half_kappa(mid_out, here[1]), half_kappa(mid_in, inner[1]), mid_out, mid_in)

    lane_w = iota((DEPTH, CY), 1)
    sub_w = iota((DEPTH, CY), 0)
    tail = [jnp.transpose(jnp.concatenate([g[CX : CX + 8]] * 16, axis=0)) for g in (got_lo, got_hi)]
    for n in range(2):
        recv = recv_lo if n == 0 else recv_hi

        def got_row(r):
            base = 128 + r * 4 * DEPTH
            return jnp.concatenate([recv[base + c * DEPTH : base + (c + 1) * DEPTH] for c in range(4)], axis=1)

        uo, uh = (got_row(0), got_row(1)) if n == 0 else (got_row(1), got_row(0))
        ui = urow[0] if n == 0 else urow[3]
        vo, vh, vi = (vrow[0], vrow[1], vrow[2]) if n == 0 else (vrow[5], vrow[4], vrow[3])
        kh = half_kappa(uh, vh)
        ki = half_kappa(ui, vi)
        total = flux(kh, half_kappa(uo, vo), uh, uo) + flux(kh, ki, uh, ui)
        first_u = pltpu.roll(tail[0][:DEPTH], (128 - n) & 127, 1) if n else tail[0][:DEPTH]
        first_v = pltpu.roll(tail[0][DEPTH:], (128 - n) & 127, 1) if n else tail[0][DEPTH:]
        end_u = pltpu.roll(tail[1][:DEPTH], 127 - n, 1)
        end_v = pltpu.roll(tail[1][DEPTH:], 127 - n, 1)
        first_k, end_k = half_kappa(first_u, first_v), half_kappa(end_u, end_v)

        def near(a, first, end, pad):
            left = jnp.where(lane_w == 0, jnp.concatenate([first] * 4, axis=1), pltpu.roll(a, 1, 1))
            right = jnp.where(lane_w == CY - 1, jnp.concatenate([end] * 4, axis=1), pltpu.roll(a, CY - 1, 1))
            up = jnp.where(sub_w == DEPTH - 1, pad, pltpu.roll(a, DEPTH - 1, 0))
            down = jnp.where(sub_w == 0, pad, pltpu.roll(a, 1, 0))
            return left, right, up, down

        for kn, un in zip(near(kh, first_k, end_k, 0.05), near(uh, first_u, end_u, 0.0)):
            total = total + flux(kh, kn, uh, un)
        row_at = meta[0] + (-1.0 if n == 0 else float(CX))
        gl = glow_of(jnp.full((1, CY), 1.0, F32) * row_at)
        mrow[DEPTH * n : DEPTH * n + DEPTH] = (uh + total + gl * vh) * meta[2 + n]
        row1[DEPTH * n : DEPTH * n + DEPTH] = flux(kh, ki, uh, ui) if n == 0 else flux(ki, kh, ui, uh)

    glow2 = glow_of(sub.astype(F32) + meta[1])
    tiles = range(4)

    def load(ref, z):
        return [ref[z, :, 128 * c : 128 * c + 128] for c in tiles]

    def planes(src, dst, row_f, col_f, glow, z0, is_last):
        k = load2(kz)
        down = load2(fz)
        cols = col_f[...]
        for p in range(PLANES):
            z = z0 + p
            u = load(src, z)
            v = load(vs, z)
            if is_last and p == PLANES - 1:
                kn = k
                up = [(k[c] + 0.05) * (0.0 - u[c]) for c in tiles]
            else:
                un = load(src, z + 1)
                vn = load(vs, z + 1)
                kn = [half_kappa(un[c], vn[c]) for c in tiles]
                up = [flux(k[c], kn[c], u[c], un[c]) for c in tiles]
            row_first = row_f[pl.ds(z, 1), :]
            row_end = row_f[pl.ds(z + DEPTH, 1), :]
            edge0 = pltpu.roll(cols, (128 - z) & 127, 1)
            edge1 = pltpu.roll(cols, 63 - z, 1)
            ru = [pltpu.roll(u[c], 1, 1) for c in tiles]
            rk = [pltpu.roll(k[c], 1, 1) for c in tiles]
            g = []
            for c in tiles:
                if c == 0:
                    g.append(jnp.where(lane == 0, edge0, flux(k[0], rk[0], ru[0], u[0])))
                else:
                    pu = jnp.where(lane == 0, ru[c - 1], ru[c])
                    pk = jnp.where(lane == 0, rk[c - 1], rk[c])
                    g.append(flux(k[c], pk, pu, u[c]))
            rg = [pltpu.roll(g[c], 127, 1) for c in tiles]
            for c in tiles:
                at = slice(128 * c, 128 * c + 128)
                gn = jnp.where(lane == 127, rg[c + 1] if c < 3 else edge1, rg[c])
                f = flux(k[c], pltpu.roll(k[c], 1, 0), pltpu.roll(u[c], 1, 0), u[c])
                f = jnp.where(sub == 0, row_first[:, at], f)
                fn = jnp.where(sub == CX - 1, row_end[:, at], pltpu.roll(f, CX - 1, 0))
                total = (up[c] - down[c]) + (fn - f) + (gn - g[c])
                dst[z, :, at] = u[c] + total + glow * v[c]
            k, down = kn, up
        for c in tiles:
            at = slice(128 * c, 128 * c + 128)
            kz[:, at] = k[c]
            fz[:, at] = down[c]

    def load2(ref):
        return [ref[:, 128 * c : 128 * c + 128] for c in tiles]

    def begin(src):
        u = load(src, 0)
        v = load(vs, 0)
        for c in tiles:
            at = slice(128 * c, 128 * c + 128)
            k = half_kappa(u[c], v[c])
            kz[:, at] = k
            fz[:, at] = (k + 0.05) * u[c]

    groups = DEPTH // PLANES
    per = 8 // PLANES
    for copy in fetch(0):
        copy.wait()
    begin(us)

    def one(g, carry):
        @pl.when(lax.rem(g, per) == per - 1)
        def _():
            for copy in fetch((g + 1) // per):
                copy.wait()

        planes(us, ms, row1, col1, glow1, g * PLANES, False)
        return carry

    lax.fori_loop(0, groups - 1, one, 0)
    planes(us, ms, row1, col1, glow1, DEPTH - PLANES, True)

    for n in range(2):
        mh = mrow[DEPTH * n : DEPTH * n + DEPTH]
        kh = half_kappa(mh, vrow[1] if n == 0 else vrow[4])
        mi = ms[:, 0 if n == 0 else CX - 1, :]
        ki = half_kappa(mi, vrow[2] if n == 0 else vrow[3])
        row2[DEPTH * n : DEPTH * n + DEPTH] = flux(kh, ki, mh, mi) if n == 0 else flux(ki, kh, mi, mh)

    def store(c):
        at = pl.ds(pl.multiple_of(c * 8, 8), 8)
        return pltpu.make_async_copy(us.at[at], out_hbm.at[at], sems.at[0, c])

    begin(ms)

    def two(g, carry):
        planes(ms, us, row2, col2, glow2, g * PLANES, False)

        @pl.when(lax.rem(g, per) == per - 1)
        def _():
            store(g // per).start()

        return carry

    lax.fori_loop(0, groups - 1, two, 0)
    planes(ms, us, row2, col2, glow2, DEPTH - PLANES, True)
    store(chunks - 1).start()
    for c in range(chunks):
        store(c).wait()


def heat(meta, u, v, urow, recv_lo, recv_hi, vrow, pay_lo, pay_hi, got_lo, got_hi):
    plane = pltpu.VMEM((DEPTH, CX, CY), F32)
    rows = pltpu.VMEM((2 * DEPTH, CY), F32)
    column = pltpu.VMEM((CX, 128), F32)
    return pl.pallas_call(
        heat_kernel,
        out_shape=jax.ShapeDtypeStruct((DEPTH, CX, CY), F32),
        in_specs=[SSPEC, ASPEC, ASPEC] + [VSPEC] * 8,
        out_specs=ASPEC,
        scratch_shapes=[
            plane, plane, plane,
            pltpu.VMEM((CX, CY), F32), pltpu.VMEM((CX, CY), F32),
            rows, rows, rows, column, column,
            pltpu.SemaphoreType.DMA((2, DEPTH // 8)),
        ],
        compiler_params=pltpu.CompilerParams(vmem_limit_bytes=VMEM_LIMIT),
        name="two_heat_steps",
    )(meta, u, v, urow, recv_lo, recv_hi, vrow, pay_lo, pay_hi, got_lo, got_hi)


def shift(value, axis, steps):
    count = lax.axis_size(axis)
    first, stop = max(0, -steps), min(count, count - steps)
    return lax.ppermute(value, axis, [(i, i + steps) for i in range(first, stop)])


def body(
    particle_locations,
    particle_speeds,
    particle_bulk,
    receiving_group_per_pair,
    emitting_group_per_pair,
    active_pair_slots,
    landing_site_triple,
    landing_weight_octants,
    thermal_excess,
    molten_strip_midlines,
):
    states = jnp.concatenate([particle_locations, particle_speeds], axis=0)
    width = HB * 128
    halo_lo = shift(states[:, NPART - width :], ("gx", "gy"), 1)
    halo_hi = shift(states[:, :width], ("gx", "gy"), -1)
    urow, ucol = edges(thermal_excess)

    gx, gy = lax.axis_index("gx"), lax.axis_index("gy")
    row_start, col_start = gx * CX, gy * CY
    beam = row_start - molten_strip_midlines
    inside = jnp.stack([gx > 0, gx < lax.axis_size("gx") - 1, gy > 0, gy < lax.axis_size("gy") - 1])
    meta = jnp.concatenate([beam.astype(F32), inside.astype(F32)])
    origin = jnp.stack([row_start - G, col_start])

    nloc, nvel, skey, schg, last, send_lo, send_hi = particles(
        receiving_group_per_pair, emitting_group_per_pair, active_pair_slots, origin,
        particle_locations, particle_speeds, halo_lo, halo_hi, landing_site_triple,
        particle_bulk.reshape(128, 128), landing_weight_octants.reshape(128, 128), urow,
    )
    recv_lo = shift(send_hi, "gx", 1)
    recv_hi = shift(send_lo, "gx", -1)
    pile, row_lo, row_hi = own_deposit(last.reshape(128), skey, schg)
    part_lo = shift(row_hi, "gx", 1)
    part_hi = shift(row_lo, "gx", -1)

    share, vrow, pay_lo, pay_hi = edge_deposit(
        meta, pile, recv_lo, recv_hi, part_lo, part_hi, ucol,
    )
    got_lo = shift(pay_hi, "gy", 1)
    got_hi = shift(pay_lo, "gy", -1)
    final = heat(meta, thermal_excess, share, urow, recv_lo, recv_hi, vrow, pay_lo, pay_hi, got_lo, got_hi)
    return nloc, nvel, share, final


def solution(mesh):
    placed = (
        P(None, ("gx", "gy")),
        P(None, ("gx", "gy")),
        P(("gx", "gy")),
        P(("gx", "gy")),
        P(("gx", "gy")),
        P(("gx", "gy")),
        P(None, ("gx", "gy")),
        P(("gx", "gy")),
        P(None, "gx", "gy"),
        P(),
    )
    return jax.shard_map(
        body,
        mesh=mesh,
        in_specs=placed,
        out_specs=(
            P(None, ("gx", "gy")),
            P(None, ("gx", "gy")),
            P(None, "gx", "gy"),
            P(None, "gx", "gy"),
        ),
        check_vma=False,
    )
```

```python
import math

import jax
import jax.numpy as jnp
from jax import lax
from jax.experimental import pallas as pl
from jax.experimental.pallas import tpu as pltpu
from jax.sharding import PartitionSpec as P

F32 = jnp.float32
BF16 = jnp.bfloat16
I32 = jnp.int32

DEPTH = 64
CX = 32
CY = 512
NPART = 16384
G = 16
HB = 2
NB = 128
NEXT = NB + 2 * HB
SLOTS = 256
BAND = 64.0
BIN = 256
LOG2E = 1.4426950408889634
VMEM_LIMIT = 30 * 1024 * 1024
TILE_UNROLL = 32
WALK_UNROLL = 32
ROW_UNROLL = 16
PLANES = 4
XW = CX + 4
BINS = 2 * XW
PART = 128 + 8 * DEPTH
SEND = PART + 8 * DEPTH + 8

VSPEC = pl.BlockSpec(memory_space=pltpu.VMEM)
SSPEC = pl.BlockSpec(memory_space=pltpu.SMEM)
ASPEC = pl.BlockSpec(memory_space=pl.ANY)


def iota(shape, dim):
    return lax.broadcasted_iota(I32, shape, dim)


def cross_stage(ks, cs, step, axis):
    at = iota((8, 128), axis)
    other = at ^ step
    low = (at & step) == 0
    nk, nc = [], []
    for k, c in zip(ks, cs):
        pk = jnp.take_along_axis(k, other, axis=axis)
        pc = jnp.take_along_axis(c, other, axis=axis)
        m = jnp.where(low, jnp.minimum(k, pk), jnp.maximum(k, pk))
        nk.append(m)
        nc.append(jnp.where(m != k, pc, c))
    return nk, nc


def vreg_stage(ks, cs, j, descending):
    ks, cs = list(ks), list(cs)
    for r in range(16):
        if r & (1 << j):
            continue
        a, b = r, r | (1 << j)
        if descending(r):
            a, b = b, a
        less = ks[b] < ks[a]
        ks[a], ks[b] = jnp.minimum(ks[a], ks[b]), jnp.maximum(ks[a], ks[b])
        cs[a], cs[b] = jnp.where(less, cs[b], cs[a]), jnp.where(less, cs[a], cs[b])
    return ks, cs


def bitonic(ks, cs):
    sub = iota((8, 128), 0)
    lane = iota((8, 128), 1)
    up = lambda r: False

    def low_stages(ks, cs, top):
        for j in range(top, 3, -1):
            step = 1 << (j - 4)
            ks, cs = cross_stage(ks, cs, step, 0)
        for j in range(min(top, 3), -1, -1):
            ks, cs = vreg_stage(ks, cs, j, up)
        return ks, cs

    for k in range(1, 4):
        for j in range(k - 1, -1, -1):
            ks, cs = vreg_stage(ks, cs, j, lambda r: bool(r & (1 << k)))
    for k in range(4, 7):
        flip = -((sub >> (k - 4)) & 1)
        ks = [a ^ flip for a in ks]
        ks, cs = low_stages(ks, cs, k - 1)
        ks = [a ^ flip for a in ks]

    def phase(k, carry):
        ks, cs = list(carry[:16]), list(carry[16:])
        flip = -((lane >> (k - 7)) & 1)
        ks = [a ^ flip for a in ks]

        def lane_step(t, inner):
            step = jnp.left_shift(jnp.int32(1), k - 8 - t)
            nk, nc = cross_stage(list(inner[:16]), list(inner[16:]), step, 1)
            return tuple(nk) + tuple(nc)

        out = lax.fori_loop(0, k - 7, lane_step, tuple(ks) + tuple(cs))
        ks, cs = low_stages(list(out[:16]), list(out[16:]), 6)
        ks = [a ^ flip for a in ks]
        return tuple(ks) + tuple(cs)

    out = lax.fori_loop(7, 15, phase, tuple(ks) + tuple(cs))
    return list(out[:16]), list(out[16:])


OWN, RECV = 128, 32


def profile(z, charge):
    level = iota((DEPTH, 128), 0).astype(F32)
    d = (level - z) * (math.sqrt(LOG2E) / 12.0)
    p = jnp.exp2(-(d * d)) * charge
    hi = p.astype(BF16)
    lo = (p - hi.astype(F32)).astype(BF16)
    return jnp.concatenate([hi, lo], axis=0)


def walk(pile, cells, prof, count, last_bin, first_bin, end_bin, origin, unroll):
    spot = iota((BIN, 128), 0)

    def seek(i, s):
        b = last_bin(i)
        return s[0] + (b < first_bin).astype(I32), s[1] + (b <= end_bin).astype(I32)

    start, stop = lax.fori_loop(0, count, seek, (jnp.int32(0), jnp.int32(0)), unroll=8)
    stop = jnp.minimum(stop, count - 1)
    steps = stop - start + 1 + (end_bin - first_bin)

    def step(g, state):
        i, j = state
        work = []
        for u in range(unroll):
            inside = i <= stop
            ii = jnp.minimum(i, count - 1)
            work.append((ii, jnp.where(inside, j * BIN, -(1 << 20)), j - origin))
            more = jnp.logical_and(last_bin(ii) > j, j < end_bin)
            j = jnp.where(more, j + 1, j)
            i = jnp.where(more, i, jnp.minimum(i + 1, count))
        outs = []
        for ii, first, home in work:
            hot = jnp.where(spot == cells(ii) - first, 1.0, 0.0).astype(BF16)
            out = lax.dot_general(prof(ii), hot, (((1,), (1,)), ((), ())), preferred_element_type=F32)
            outs.append(out[:DEPTH] + out[DEPTH:])
        for (ii, first, home), out in zip(work, outs):
            pile[home] = pile[home] + out
        return i, j

    @pl.when(start <= stop)
    def _():
        lax.fori_loop(0, (steps + unroll - 1) // unroll, step, (start, jnp.int32(first_bin)))


def split3(a):
    h1 = a.astype(BF16)
    r = a - h1.astype(F32)
    h2 = r.astype(BF16)
    h3 = (r - h2.astype(F32)).astype(BF16)
    return h1, h2, h3


def particle_kernel(
    tgt, src, cnt, origin, loc, vel, halo_lo, halo_hi, site, bulk, octants, urow,
    nloc, nvel, skey, schg, last, send_lo, send_hi,
    left, right, stat, acc, zrow, key, last_v, last_s, rows, sem,
):
    wide = 4 * 128

    def prepare(x3, v3, at, width):
        pad = jnp.zeros((5, width), F32)
        x = jnp.concatenate([x3, pad], axis=0)
        v = jnp.concatenate([v3, pad], axis=0)
        row = iota((8, width), 0)
        xs = x * math.sqrt(LOG2E)
        q = 0.5 * jnp.sum(xs * xs, axis=0, keepdims=True)
        full = jnp.where(row < 3, xs, jnp.where(row < 5, q, 0.0))
        h = [p.astype(F32) for p in split3(full)]

        def mix(a, b, is_target):
            base = h[a]
            if b is None:
                return jnp.where(row < 3, base, 0.0)
            if is_target:
                return jnp.where(row < 3, base, jnp.where(row == 3, h[b], jnp.where(row == 4, 1.0, 0.0)))
            return jnp.where(row < 3, base, jnp.where(row == 3, -1.0, jnp.where(row == 4, -h[b], 0.0)))

        extra = [0, 1, 2, None, None, None]
        ta = [0, 0, 1, 1, 0, 2]
        sa = [0, 1, 0, 1, 2, 0]
        for p in range(0, 6, 2):
            lt = jnp.concatenate([mix(ta[p], extra[p], True), mix(ta[p + 1], extra[p + 1], True)], axis=0)
            rt = jnp.concatenate([mix(sa[p], extra[p], False), mix(sa[p + 1], extra[p + 1], False)], axis=0)
            left[pl.ds(8 * p, 16), pl.ds(at, width)] = lt.astype(BF16)
            right[pl.ds(8 * p, 16), pl.ds(at, width)] = rt.astype(BF16)
        w = (2.0 * x - v) * (1.0 / 256.0)
        wh = w.astype(BF16).astype(F32)
        wl = w - wh
        w2 = jnp.concatenate([jnp.where(row == 3, 1.0, wh), wl], axis=0)
        stat[:, pl.ds(at, width)] = w2.astype(BF16)

    prepare(halo_lo[0:3, :], halo_lo[3:6, :], 0, HB * 128)
    prepare(halo_hi[0:3, :], halo_hi[3:6, :], (NB + HB) * 128, HB * 128)

    def prep(i, carry):
        at = pl.multiple_of(i * wide, wide)
        prepare(loc[:, pl.ds(at, wide)], vel[:, pl.ds(at, wide)], pl.multiple_of(at + HB * 128, 128), wide)
        return carry

    lax.fori_loop(0, NPART // wide, prep, 0)
    acc[...] = jnp.zeros_like(acc)
    live = cnt[0]

    def tiles(g, carry):
        outs = []
        for u in range(TILE_UNROLL):
            t = g * TILE_UNROLL + u
            a = tgt[t] & (NB - 1)
            b = a + (src[t] - tgt[t]) + HB
            lm = left[:, pl.ds(pl.multiple_of((a + HB) * 128, 128), 128)]
            rm = right[:, pl.ds(pl.multiple_of(b * 128, 128), 128)]
            arg = lax.dot_general(rm, lm, (((0,), (0,)), ((), ())), preferred_element_type=F32)
            g_mn = jnp.exp2(arg)
            gh = g_mn.astype(BF16)
            gl = (g_mn - gh.astype(F32)).astype(BF16)
            s = stat[:, pl.ds(pl.multiple_of(b * 128, 128), 128)]
            out = jnp.dot(
                jnp.concatenate([s, s], axis=1),
                jnp.concatenate([gh, gl], axis=0),
                preferred_element_type=F32,
            )
            home = jnp.where(t < live, a, NB)
            outs.append((home, out[0:8] + out[8:16]))
        for home, out in outs:
            at = pl.multiple_of(home * 8, 8)
            acc[pl.ds(at, 8), :] = acc[pl.ds(at, 8), :] + out
        return carry

    lax.fori_loop(0, (live + TILE_UNROLL - 1) // TILE_UNROLL, tiles, 0)

    def advance(i, carry):
        for u in range(8):
            b = i * 8 + u
            at = pl.multiple_of(b * 128, 128)
            x = loc[:, pl.ds(at, 128)]
            v = vel[:, pl.ds(at, 128)]
            f = acc[pl.ds(pl.multiple_of(b * 8, 8), 8), :]
            w = (2.0 * x - v) * (1.0 / 256.0)
            force = w * f[3:4] - f[0:3]
            nv = v + 0.5 * force
            nx = x + 0.5 * nv
            nvel[:, pl.ds(at, 128)] = nv
            nloc[:, pl.ds(at, 128)] = nx
            zrow[pl.ds(b, 1), :] = nx[2:3]
            p = site[:, pl.ds(at, 128)]
            cell = (p[1:2] - origin[0]) * CY + (p[2:3] - origin[1])
            key[pl.ds(b, 1), :] = cell * DEPTH + p[0:1]
        return carry

    lax.fori_loop(0, NB // 8, advance, 0)

    charge = bulk[...] * octants[...].astype(F32) * 0.125 * (1.0 + 0.5 * jnp.tanh(zrow[...]))
    keys = key[...]
    ks = [keys[8 * r : 8 * r + 8] for r in range(16)]
    cs = [charge[8 * r : 8 * r + 8] for r in range(16)]
    ks, cs = bitonic(ks, cs)
    last[...] = ks[15][7:8]
    last_v[...] = ks[15]
    lasts = pltpu.make_async_copy(last_v, last_s, sem.at[0])
    lasts.start()
    kt = jnp.concatenate(ks, axis=0)
    ct = jnp.concatenate(cs, axis=0)
    kt = jnp.transpose(kt)
    ct = jnp.transpose(ct)
    skey[...] = kt
    schg[...] = ct
    for ref, at in ((send_lo, 0), (send_hi, 96)):
        kk = kt[at : at + 32]
        ref[0:32] = (kk >> 15).astype(F32)
        ref[32:64] = ((kk >> 6) & 511).astype(F32)
        ref[64:96] = (kk & 63).astype(F32)
        ref[96:128] = ct[at : at + 32]
    for r in range(4):
        ref = send_lo if r < 2 else send_hi
        for c in range(4):
            at = 128 + ((r % 2) * 4 + c) * DEPTH
            ref[at : at + DEPTH] = urow[r, :, 128 * c : 128 * c + 128]
    rows[...] = jnp.zeros_like(rows)
    lasts.wait()

    def cells(i):
        return skey[pl.ds(i, 1), :] >> 6

    def prof(i):
        return profile((skey[pl.ds(i, 1), :] & 63).astype(F32), schg[pl.ds(i, 1), :])

    for n, x in enumerate((G, G + CX - 2)):
        walk(
            rows, cells, prof, OWN, lambda i: last_s[7, i] >> 14,
            2 * x, 2 * x + 3, 2 * x - 4 * n, ROW_UNROLL,
        )
    for r in range(4):
        ref = send_lo if r < 2 else send_hi
        for c in range(4):
            at = PART + ((r % 2) * 4 + c) * DEPTH
            ref[at : at + DEPTH] = rows[2 * r + c // 2, :, 128 * (c % 2) : 128 * (c % 2) + 128]
    for ref in (send_lo, send_hi):
        ref[SEND - 8 : SEND] = jnp.broadcast_to(last[...].astype(F32), (8, 128))


def particles(tgt, src, cnt, origin, loc, vel, halo_lo, halo_hi, site, bulk, octants, urow):
    sd = jax.ShapeDtypeStruct
    return pl.pallas_call(
        particle_kernel,
        out_shape=(
            sd((3, NPART), F32), sd((3, NPART), F32),
            sd((128, 128), I32), sd((128, 128), F32), sd((1, 128), I32),
            sd((SEND, 128), F32), sd((SEND, 128), F32),
        ),
        in_specs=[SSPEC] * 4 + [VSPEC] * 8,
        out_specs=(VSPEC,) * 7,
        scratch_shapes=[
            pltpu.VMEM((48, NEXT * 128), BF16),
            pltpu.VMEM((48, NEXT * 128), BF16),
            pltpu.VMEM((16, NEXT * 128), BF16),
            pltpu.VMEM(((NB + 1) * 8, 128), F32),
            pltpu.VMEM((NB, 128), F32),
            pltpu.VMEM((NB, 128), I32),
            pltpu.VMEM((8, 128), I32),
            pltpu.SMEM((8, 128), I32),
            pltpu.VMEM((8, DEPTH, BIN), F32),
            pltpu.SemaphoreType.DMA((1,)),
        ],
        compiler_params=pltpu.CompilerParams(vmem_limit_bytes=VMEM_LIMIT),
        name="particle_step",
    )(tgt, src, cnt, origin, loc, vel, halo_lo, halo_hi, site, bulk, octants, urow)


def own_deposit_kernel(last, skey, schg, pile, cells, prof):
    own = skey[...]
    cells[0:OWN] = (own >> 6) - (G - HB) * CY

    def profiles(i, carry):
        for u in range(8):
            b = i * 8 + u
            z = (skey[pl.ds(b, 1), :] & 63).astype(F32)
            prof[b] = profile(z, schg[pl.ds(b, 1), :])
        return carry

    lax.fori_loop(0, OWN // 8, profiles, 0)

    def clear(i, carry):
        pile[i] = jnp.zeros((DEPTH, BIN), F32)
        return carry

    lax.fori_loop(0, BINS, clear, 0)
    walk(
        pile, lambda i: cells[pl.ds(i, 1), :], lambda i: prof[i], OWN,
        lambda i: (last[i] >> 14) - 2 * (G - HB), 0, BINS - 1, 0, WALK_UNROLL,
    )


def own_deposit(last, skey, schg):
    sd = jax.ShapeDtypeStruct
    return pl.pallas_call(
        own_deposit_kernel,
        out_shape=sd((BINS, DEPTH, BIN), F32),
        in_specs=[SSPEC, VSPEC, VSPEC],
        out_specs=VSPEC,
        scratch_shapes=[
            pltpu.VMEM((OWN, 128), I32),
            pltpu.VMEM((OWN, 128, 128), BF16),
        ],
        compiler_params=pltpu.CompilerParams(vmem_limit_bytes=VMEM_LIMIT),
        name="own_deposit",
    )(last, skey, schg)


def edge_deposit_kernel(
    meta, pile_in, recv_lo, recv_hi, ucol,
    share, here, vrow, pay_lo, pay_hi,
    pile, cells, prof, packs, last_v, last_s, sems,
):
    load = pltpu.make_async_copy(pile_in, pile, sems.at[0])
    load.start()
    last_v[0:1] = recv_lo[SEND - 8 : SEND - 7].astype(I32)
    last_v[1:2] = recv_hi[SEND - 8 : SEND - 7].astype(I32)
    lasts = pltpu.make_async_copy(last_v, last_s, sems.at[1])
    lasts.start()
    for ref, at, shift in ((recv_lo, 0, HB - G - CX), (recv_hi, RECV, HB + CX - G)):
        x = ref[0:32].astype(I32) + shift
        cells[at : at + RECV] = x * CY + ref[32:64].astype(I32)

    def profiles(i, carry):
        for ref, at in ((recv_lo, 0), (recv_hi, RECV)):
            for u in range(4):
                b = i * 4 + u
                prof[at + b] = profile(ref[pl.ds(64 + b, 1), :], ref[pl.ds(96 + b, 1), :])
        return carry

    lax.fori_loop(0, RECV // 4, profiles, 0)
    lasts.wait()
    load.wait()
    half = 2 * (2 + G)
    for n, (at, by, first, end) in enumerate((
        (OWN - RECV, HB - G - CX, 4, half - 1), (0, HB + CX - G, half, 2 * (2 + CX) - 1),
    )):
        walk(
            pile, lambda i: cells[pl.ds(n * RECV + i, 1), :], lambda i: prof[n * RECV + i], RECV,
            lambda i: (last_s[n, at + i] >> 14) + 2 * by, first, end, 0, WALK_UNROLL,
        )
    for ref, x0, flag in ((recv_lo, 0, meta[2]), (recv_hi, CX + 2, meta[3])):
        for r in range(2):
            for c in range(4):
                at = PART + (r * 4 + c) * DEPTH
                b = 2 * (x0 + r) + c // 2
                cols = slice(128 * (c % 2), 128 * (c % 2) + 128)
                pile[b, :, cols] = flag * (pile[b, :, cols] + ref[at : at + DEPTH])

    def turn(t):
        x = t >> 1
        cols = pl.ds(pl.multiple_of((t & 1) * BIN, BIN), BIN)
        return (
            pltpu.make_async_copy(pile.at[t + 2 * HB], here.at[:, x, cols], sems.at[2 + t]),
            pltpu.make_async_copy(pile.at[t + 2 * HB], share.at[:, x, cols], sems.at[2 + 2 * CX + t]),
        )

    def turn_start(t, carry):
        for copy in turn(t):
            copy.start()
        return carry

    lax.fori_loop(0, 2 * CX, turn_start, 0)
    for n, x in enumerate((0, 1, 2, CX + 1, CX + 2, CX + 3)):
        vrow[n, :, :BIN] = pile[2 * x]
        vrow[n, :, BIN:] = pile[2 * x + 1]
    lane = iota((DEPTH, 128), 1)
    packs[...] = jnp.zeros_like(packs)

    def pick(row, at):
        a = pile[2 * row, :, 0:128]
        b = pile[2 * row + 1, :, 128:256]
        for n, (t, by) in enumerate(((a, at), (a, at + 127), (b, at + 2), (b, at + 1))):
            packs[n] = jnp.where(lane == at, pltpu.roll(t, by & 127, 1), packs[n])

    def picks(x, carry):
        pick(x + 2, x)
        return carry

    lax.fori_loop(0, CX, picks, 0, unroll=4)
    pick(1, CX)
    pick(CX + 2, CX + 1)
    base = 128 + 4 * DEPTH
    for pay, recv_col, near, far in ((pay_lo, 0, 0, 1), (pay_hi, 3, 3, 2)):
        lo = recv_lo[base + recv_col * DEPTH : base + recv_col * DEPTH + DEPTH]
        hi = recv_hi[128 + recv_col * DEPTH : 128 + recv_col * DEPTH + DEPTH]
        by = 0 if recv_col == 0 else 1
        corner = jnp.where(lane == CX, pltpu.roll(lo, CX + by, 1), 0.0)
        corner = jnp.where(lane == CX + 1, pltpu.roll(hi, CX + 1 + by, 1), corner)
        t = jnp.transpose(jnp.concatenate([corner, packs[near]], axis=0))
        pay[0:CX] = t[0:CX] + ucol[near]
        pay[CX : CX + 8] = t[CX : CX + 8]
        t = jnp.transpose(jnp.concatenate([jnp.zeros((DEPTH, 128), F32), packs[far]], axis=0))
        pay[40 : 40 + CX] = t[0:CX] + ucol[far]
        pay[40 + CX : 80] = jnp.zeros((8, 128), F32)

    def turn_wait(t, carry):
        for copy in turn(t):
            copy.wait()
        return carry

    lax.fori_loop(0, 2 * CX, turn_wait, 0)


def edge_deposit(meta, pile, recv_lo, recv_hi, ucol):
    sd = jax.ShapeDtypeStruct
    return pl.pallas_call(
        edge_deposit_kernel,
        out_shape=(
            sd((DEPTH, CX, CY), F32), sd((DEPTH, CX, CY), F32), sd((6, DEPTH, CY), F32),
            sd((80, 128), F32), sd((80, 128), F32),
        ),
        in_specs=[SSPEC, ASPEC] + [VSPEC] * 3,
        out_specs=(ASPEC, VSPEC, VSPEC, VSPEC, VSPEC),
        scratch_shapes=[
            pltpu.VMEM((BINS, DEPTH, BIN), F32),
            pltpu.VMEM((2 * RECV, 128), I32),
            pltpu.VMEM((2 * RECV, 128, 128), BF16),
            pltpu.VMEM((4, DEPTH, 128), F32),
            pltpu.VMEM((2, 128), I32),
            pltpu.SMEM((2, 128), I32),
            pltpu.SemaphoreType.DMA((2 + 4 * CX,)),
        ],
        compiler_params=pltpu.CompilerParams(vmem_limit_bytes=VMEM_LIMIT),
        name="edge_deposit",
    )(meta, pile, recv_lo, recv_hi, ucol)


def edges_kernel(cells, urow, ucol, left, right, sems):
    rows = [
        pltpu.make_async_copy(cells.at[:, x, :], urow.at[r], sems.at[2 + r])
        for r, x in enumerate((0, 1, CX - 2, CX - 1))
    ]
    cols = [
        pltpu.make_async_copy(cells.at[:, :, pl.ds(at, 128)], ref, sems.at[n])
        for n, (ref, at) in enumerate(((left, 0), (right, CY - 128)))
    ]
    for copy in cols + rows:
        copy.start()
    for copy in cols:
        copy.wait()
    lane = iota((CX, 128), 1)
    acc = [jnp.zeros((CX, 128), F32)] * 4
    for z in range(DEPTH):
        for n, (ref, by) in enumerate(((left, z), (left, z + 127), (right, z + 2), (right, z + 1))):
            by = by & 127
            a = ref[z] if by == 0 else pltpu.roll(ref[z], by, 1)
            acc[n] = jnp.where(lane == z, a, acc[n])
    for n in range(4):
        ucol[n] = acc[n]
    for copy in rows:
        copy.wait()


def edges(cells):
    sd = jax.ShapeDtypeStruct
    return pl.pallas_call(
        edges_kernel,
        out_shape=(sd((4, DEPTH, CY), F32), sd((4, CX, 128), F32)),
        in_specs=[ASPEC],
        out_specs=(VSPEC, VSPEC),
        scratch_shapes=[
            pltpu.VMEM((DEPTH, CX, 128), F32),
            pltpu.VMEM((DEPTH, CX, 128), F32),
            pltpu.SemaphoreType.DMA((6,)),
        ],
        compiler_params=pltpu.CompilerParams(vmem_limit_bytes=VMEM_LIMIT),
        name="temperature_edges",
    )(cells)


def half_kappa(u, v):
    return 0.05 * (1.0 + 0.5 * jnp.tanh(u)) / (1.0 + v)


def flux(k, kn, u, un):
    return (k + kn) * (un - u)


def heat_kernel(
    meta, us, vs, urow, recv_lo, recv_hi, vrow, pay_lo, pay_hi, got_lo, got_hi, out_hbm,
    ms, os, kz, fz, row1, row2, mrow, col1, col2, sems,
):
    chunks = DEPTH // 8

    def glow_of(rows):
        d = rows * (1.0 / BAND)
        return 0.5 * jnp.exp(-(d * d))

    lane = iota((CX, 128), 1)
    sub = iota((CX, 128), 0)
    lo_half = lane < DEPTH
    side = jnp.where(lo_half, meta[4], meta[5])
    glow1 = glow_of(sub.astype(F32) + meta[0])

    def stacks(a, b, at, size):
        p, q = a[at : at + size], b[at : at + size]
        low = iota((size, 128), 1) < DEPTH
        return jnp.where(low, p, pltpu.roll(q, DEPTH, 1)), jnp.where(low, pltpu.roll(p, DEPTH, 1), q)

    def column_step(outer, here, inner, ends):
        (uo, vo), (uh, vh), (ui, vi), (ue, ve) = outer, here, inner, ends
        kh = half_kappa(uh, vh)
        ke = half_kappa(ue, ve)
        total = flux(kh, half_kappa(uo, vo), uh, uo) + flux(kh, half_kappa(ui, vi), uh, ui)

        def near(a, e, n, pad):
            below = jnp.where(sub == 0, e[0:1], pltpu.roll(a, 1, 0))
            above = jnp.where(sub == CX - 1, e[1:2], pltpu.roll(a, CX - 1, 0))
            up = jnp.where((lane & (DEPTH - 1)) == DEPTH - 1, pad, pltpu.roll(a, 127, 1))
            down = jnp.where((lane & (DEPTH - 1)) == 0, pad, pltpu.roll(a, 1, 1))
            return below, above, up, down

        for kn, un in zip(near(kh, ke, 0, 0.05), near(uh, ue, 0, 0.0)):
            total = total + flux(kh, kn, uh, un)
        return uh + total + glow1 * vh, kh

    outer = stacks(got_lo, got_hi, 40, CX)
    here = stacks(got_lo, got_hi, 0, CX)
    inner = stacks(pay_lo, pay_hi, 0, CX)
    next_in = stacks(pay_lo, pay_hi, 40, CX)
    corners = stacks(got_lo, got_hi, CX, 8)
    mid_out, k_out = column_step(outer, here, inner, corners)
    mid_in, k_in = column_step(here, inner, next_in, stacks(pay_lo, pay_hi, CX, 8))
    mid_out = mid_out * side
    sign = jnp.where(lo_half, 1.0, -1.0)
    col1[...] = sign * flux(k_out, k_in, here[0], inner[0])
    col2[...] = sign * flux(half_kappa(mid_out, here[1]), half_kappa(mid_in, inner[1]), mid_out, mid_in)

    lane_w = iota((DEPTH, CY), 1)
    sub_w = iota((DEPTH, CY), 0)
    tail = [jnp.transpose(jnp.concatenate([g[CX : CX + 8]] * 16, axis=0)) for g in (got_lo, got_hi)]
    for n in range(2):
        recv = recv_lo if n == 0 else recv_hi

        def got_row(r):
            base = 128 + r * 4 * DEPTH
            return jnp.concatenate([recv[base + c * DEPTH : base + (c + 1) * DEPTH] for c in range(4)], axis=1)

        uo, uh = (got_row(0), got_row(1)) if n == 0 else (got_row(1), got_row(0))
        ui = urow[0] if n == 0 else urow[3]
        vo, vh, vi = (vrow[0], vrow[1], vrow[2]) if n == 0 else (vrow[5], vrow[4], vrow[3])
        kh = half_kappa(uh, vh)
        ki = half_kappa(ui, vi)
        total = flux(kh, half_kappa(uo, vo), uh, uo) + flux(kh, ki, uh, ui)
        first_u = pltpu.roll(tail[0][:DEPTH], (128 - n) & 127, 1) if n else tail[0][:DEPTH]
        first_v = pltpu.roll(tail[0][DEPTH:], (128 - n) & 127, 1) if n else tail[0][DEPTH:]
        end_u = pltpu.roll(tail[1][:DEPTH], 127 - n, 1)
        end_v = pltpu.roll(tail[1][DEPTH:], 127 - n, 1)
        first_k, end_k = half_kappa(first_u, first_v), half_kappa(end_u, end_v)

        def near(a, first, end, pad):
            left = jnp.where(lane_w == 0, jnp.concatenate([first] * 4, axis=1), pltpu.roll(a, 1, 1))
            right = jnp.where(lane_w == CY - 1, jnp.concatenate([end] * 4, axis=1), pltpu.roll(a, CY - 1, 1))
            up = jnp.where(sub_w == DEPTH - 1, pad, pltpu.roll(a, DEPTH - 1, 0))
            down = jnp.where(sub_w == 0, pad, pltpu.roll(a, 1, 0))
            return left, right, up, down

        for kn, un in zip(near(kh, first_k, end_k, 0.05), near(uh, first_u, end_u, 0.0)):
            total = total + flux(kh, kn, uh, un)
        row_at = meta[0] + (-1.0 if n == 0 else float(CX))
        gl = glow_of(jnp.full((1, CY), 1.0, F32) * row_at)
        mrow[DEPTH * n : DEPTH * n + DEPTH] = (uh + total + gl * vh) * meta[2 + n]
        row1[DEPTH * n : DEPTH * n + DEPTH] = flux(kh, ki, uh, ui) if n == 0 else flux(ki, kh, ui, uh)

    glow2 = glow_of(sub.astype(F32) + meta[1])
    tiles = range(4)

    def load(ref, z):
        return [ref[z, :, 128 * c : 128 * c + 128] for c in tiles]

    def planes(src, dst, row_f, col_f, glow, z0, is_last):
        k = load2(kz)
        down = load2(fz)
        cols = col_f[...]
        for p in range(PLANES):
            z = z0 + p
            u = load(src, z)
            v = load(vs, z)
            if is_last and p == PLANES - 1:
                kn = k
                up = [(k[c] + 0.05) * (0.0 - u[c]) for c in tiles]
            else:
                un = load(src, z + 1)
                vn = load(vs, z + 1)
                kn = [half_kappa(un[c], vn[c]) for c in tiles]
                up = [flux(k[c], kn[c], u[c], un[c]) for c in tiles]
            row_first = row_f[pl.ds(z, 1), :]
            row_end = row_f[pl.ds(z + DEPTH, 1), :]
            edge0 = pltpu.roll(cols, (128 - z) & 127, 1)
            edge1 = pltpu.roll(cols, 63 - z, 1)
            ru = [pltpu.roll(u[c], 1, 1) for c in tiles]
            rk = [pltpu.roll(k[c], 1, 1) for c in tiles]
            g = []
            for c in tiles:
                if c == 0:
                    g.append(jnp.where(lane == 0, edge0, flux(k[0], rk[0], ru[0], u[0])))
                else:
                    pu = jnp.where(lane == 0, ru[c - 1], ru[c])
                    pk = jnp.where(lane == 0, rk[c - 1], rk[c])
                    g.append(flux(k[c], pk, pu, u[c]))
            rg = [pltpu.roll(g[c], 127, 1) for c in tiles]
            for c in tiles:
                at = slice(128 * c, 128 * c + 128)
                gn = jnp.where(lane == 127, rg[c + 1] if c < 3 else edge1, rg[c])
                f = flux(k[c], pltpu.roll(k[c], 1, 0), pltpu.roll(u[c], 1, 0), u[c])
                f = jnp.where(sub == 0, row_first[:, at], f)
                fn = jnp.where(sub == CX - 1, row_end[:, at], pltpu.roll(f, CX - 1, 0))
                total = (up[c] - down[c]) + (fn - f) + (gn - g[c])
                dst[z, :, at] = u[c] + total + glow * v[c]
            k, down = kn, up
        for c in tiles:
            at = slice(128 * c, 128 * c + 128)
            kz[:, at] = k[c]
            fz[:, at] = down[c]

    def load2(ref):
        return [ref[:, 128 * c : 128 * c + 128] for c in tiles]

    def begin(src):
        u = load(src, 0)
        v = load(vs, 0)
        for c in tiles:
            at = slice(128 * c, 128 * c + 128)
            k = half_kappa(u[c], v[c])
            kz[:, at] = k
            fz[:, at] = (k + 0.05) * u[c]

    groups = DEPTH // PLANES
    per = 8 // PLANES
    begin(us)

    def one(g, carry):
        planes(us, ms, row1, col1, glow1, g * PLANES, False)
        return carry

    lax.fori_loop(0, groups - 1, one, 0)
    planes(us, ms, row1, col1, glow1, DEPTH - PLANES, True)

    for n in range(2):
        mh = mrow[DEPTH * n : DEPTH * n + DEPTH]
        kh = half_kappa(mh, vrow[1] if n == 0 else vrow[4])
        mi = ms[:, 0 if n == 0 else CX - 1, :]
        ki = half_kappa(mi, vrow[2] if n == 0 else vrow[3])
        row2[DEPTH * n : DEPTH * n + DEPTH] = flux(kh, ki, mh, mi) if n == 0 else flux(ki, kh, mi, mh)

    def store(c):
        at = pl.ds(pl.multiple_of(c * 8, 8), 8)
        return pltpu.make_async_copy(os.at[at], out_hbm.at[at], sems.at[c])

    begin(ms)

    def two(g, carry):
        planes(ms, os, row2, col2, glow2, g * PLANES, False)

        @pl.when(lax.rem(g, per) == per - 1)
        def _():
            store(g // per).start()

        return carry

    lax.fori_loop(0, groups - 1, two, 0)
    planes(ms, os, row2, col2, glow2, DEPTH - PLANES, True)
    store(chunks - 1).start()
    for c in range(chunks):
        store(c).wait()


def heat(meta, u, v, urow, recv_lo, recv_hi, vrow, pay_lo, pay_hi, got_lo, got_hi):
    plane = pltpu.VMEM((DEPTH, CX, CY), F32)
    rows = pltpu.VMEM((2 * DEPTH, CY), F32)
    column = pltpu.VMEM((CX, 128), F32)
    return pl.pallas_call(
        heat_kernel,
        out_shape=jax.ShapeDtypeStruct((DEPTH, CX, CY), F32),
        in_specs=[SSPEC] + [VSPEC] * 10,
        out_specs=ASPEC,
        scratch_shapes=[
            plane, plane,
            pltpu.VMEM((CX, CY), F32), pltpu.VMEM((CX, CY), F32),
            rows, rows, rows, column, column,
            pltpu.SemaphoreType.DMA((DEPTH // 8,)),
        ],
        compiler_params=pltpu.CompilerParams(vmem_limit_bytes=VMEM_LIMIT),
        name="two_heat_steps",
    )(meta, u, v, urow, recv_lo, recv_hi, vrow, pay_lo, pay_hi, got_lo, got_hi)


def shift(value, axis, steps):
    count = lax.axis_size(axis)
    first, stop = max(0, -steps), min(count, count - steps)
    return lax.ppermute(value, axis, [(i, i + steps) for i in range(first, stop)])


def body(
    particle_locations,
    particle_speeds,
    particle_bulk,
    receiving_group_per_pair,
    emitting_group_per_pair,
    active_pair_slots,
    landing_site_triple,
    landing_weight_octants,
    thermal_excess,
    molten_strip_midlines,
):
    states = jnp.concatenate([particle_locations, particle_speeds], axis=0)
    width = HB * 128
    halo_lo = shift(states[:, NPART - width :], ("gx", "gy"), 1)
    halo_hi = shift(states[:, :width], ("gx", "gy"), -1)
    urow, ucol = edges(thermal_excess)

    gx, gy = lax.axis_index("gx"), lax.axis_index("gy")
    row_start, col_start = gx * CX, gy * CY
    beam = row_start - molten_strip_midlines
    inside = jnp.stack([gx > 0, gx < lax.axis_size("gx") - 1, gy > 0, gy < lax.axis_size("gy") - 1])
    meta = jnp.concatenate([beam.astype(F32), inside.astype(F32)])
    origin = jnp.stack([row_start - G, col_start])

    nloc, nvel, skey, schg, last, send_lo, send_hi = particles(
        receiving_group_per_pair, emitting_group_per_pair, active_pair_slots, origin,
        particle_locations, particle_speeds, halo_lo, halo_hi, landing_site_triple,
        particle_bulk.reshape(128, 128), landing_weight_octants.reshape(128, 128), urow,
    )
    recv_lo = shift(send_hi, "gx", 1)
    recv_hi = shift(send_lo, "gx", -1)
    pile = own_deposit(last.reshape(128), skey, schg)
    share, here, vrow, pay_lo, pay_hi = edge_deposit(meta, pile, recv_lo, recv_hi, ucol)
    got_lo = shift(pay_hi, "gy", 1)
    got_hi = shift(pay_lo, "gy", -1)
    final = heat(meta, thermal_excess, here, urow, recv_lo, recv_hi, vrow, pay_lo, pay_hi, got_lo, got_hi)
    return nloc, nvel, share, final


def solution(mesh):
    placed = (
        P(None, ("gx", "gy")),
        P(None, ("gx", "gy")),
        P(("gx", "gy")),
        P(("gx", "gy")),
        P(("gx", "gy")),
        P(("gx", "gy")),
        P(None, ("gx", "gy")),
        P(("gx", "gy")),
        P(None, "gx", "gy"),
        P(),
    )
    return jax.shard_map(
        body,
        mesh=mesh,
        in_specs=placed,
        out_specs=(
            P(None, ("gx", "gy")),
            P(None, ("gx", "gy")),
            P(None, "gx", "gy"),
            P(None, "gx", "gy"),
        ),
        check_vma=False,
    )
```

```python
import math

import jax
import jax.numpy as jnp
from jax import lax
from jax.experimental import pallas as pl
from jax.experimental.pallas import tpu as pltpu
from jax.sharding import PartitionSpec as P

F32 = jnp.float32
BF16 = jnp.bfloat16
I32 = jnp.int32

DEPTH = 64
CX = 32
CY = 512
NPART = 16384
G = 16
HB = 2
NB = 128
NEXT = NB + 2 * HB
SLOTS = 256
BAND = 64.0
BIN = 256
LOG2E = 1.4426950408889634
VMEM_LIMIT = 30 * 1024 * 1024
TILE_UNROLL = 32
WALK_UNROLL = 32
ROW_UNROLL = 16
PLANES = 4
XW = CX + 4
BINS = 2 * XW
PART = 128 + 8 * DEPTH
SEND = PART + 8 * DEPTH + 8

VSPEC = pl.BlockSpec(memory_space=pltpu.VMEM)
SSPEC = pl.BlockSpec(memory_space=pltpu.SMEM)
ASPEC = pl.BlockSpec(memory_space=pl.ANY)


def iota(shape, dim):
    return lax.broadcasted_iota(I32, shape, dim)


def cross_stage(ks, cs, step, axis):
    at = iota((8, 128), axis)
    other = at ^ step
    low = (at & step) == 0
    nk, nc = [], []
    for k, c in zip(ks, cs):
        pk = jnp.take_along_axis(k, other, axis=axis)
        pc = jnp.take_along_axis(c, other, axis=axis)
        m = jnp.where(low, jnp.minimum(k, pk), jnp.maximum(k, pk))
        nk.append(m)
        nc.append(jnp.where(m != k, pc, c))
    return nk, nc


def vreg_stage(ks, cs, j, descending):
    ks, cs = list(ks), list(cs)
    for r in range(16):
        if r & (1 << j):
            continue
        a, b = r, r | (1 << j)
        if descending(r):
            a, b = b, a
        less = ks[b] < ks[a]
        ks[a], ks[b] = jnp.minimum(ks[a], ks[b]), jnp.maximum(ks[a], ks[b])
        cs[a], cs[b] = jnp.where(less, cs[b], cs[a]), jnp.where(less, cs[a], cs[b])
    return ks, cs


def bitonic(ks, cs):
    sub = iota((8, 128), 0)
    lane = iota((8, 128), 1)
    up = lambda r: False

    def low_stages(ks, cs, top):
        for j in range(top, 3, -1):
            step = 1 << (j - 4)
            ks, cs = cross_stage(ks, cs, step, 0)
        for j in range(min(top, 3), -1, -1):
            ks, cs = vreg_stage(ks, cs, j, up)
        return ks, cs

    for k in range(1, 4):
        for j in range(k - 1, -1, -1):
            ks, cs = vreg_stage(ks, cs, j, lambda r: bool(r & (1 << k)))
    for k in range(4, 7):
        flip = -((sub >> (k - 4)) & 1)
        ks = [a ^ flip for a in ks]
        ks, cs = low_stages(ks, cs, k - 1)
        ks = [a ^ flip for a in ks]

    def phase(k, carry):
        ks, cs = list(carry[:16]), list(carry[16:])
        flip = -((lane >> (k - 7)) & 1)
        ks = [a ^ flip for a in ks]

        def lane_step(t, inner):
            step = jnp.left_shift(jnp.int32(1), k - 8 - t)
            nk, nc = cross_stage(list(inner[:16]), list(inner[16:]), step, 1)
            return tuple(nk) + tuple(nc)

        out = lax.fori_loop(0, k - 7, lane_step, tuple(ks) + tuple(cs))
        ks, cs = low_stages(list(out[:16]), list(out[16:]), 6)
        ks = [a ^ flip for a in ks]
        return tuple(ks) + tuple(cs)

    out = lax.fori_loop(7, 15, phase, tuple(ks) + tuple(cs))
    return list(out[:16]), list(out[16:])


OWN, RECV = 128, 32


def profile(z, charge):
    level = iota((DEPTH, 128), 0).astype(F32)
    d = (level - z) * (math.sqrt(LOG2E) / 12.0)
    p = jnp.exp2(-(d * d)) * charge
    hi = p.astype(BF16)
    lo = (p - hi.astype(F32)).astype(BF16)
    return jnp.concatenate([hi, lo], axis=0)


def count_below(bins, limit):
    return jnp.sum(jnp.where(bins < limit, 1.0, 0.0)).astype(I32)


def walk(pile, cells, prof, count, bins, last_bin, first_bin, end_bin, origin, unroll):
    spot = iota((BIN, 128), 0)
    start = count_below(bins, float(first_bin))
    stop = jnp.minimum(count_below(bins, float(end_bin + 1)), count - 1)
    steps = stop - start + 1 + (end_bin - first_bin)

    def step(g, state):
        i, j = state
        work = []
        for u in range(unroll):
            inside = i <= stop
            ii = jnp.minimum(i, count - 1)
            work.append((ii, jnp.where(inside, j * BIN, -(1 << 20)), j - origin))
            more = jnp.logical_and(last_bin(ii) > j, j < end_bin)
            j = jnp.where(more, j + 1, j)
            i = jnp.where(more, i, jnp.minimum(i + 1, count))
        outs = []
        for ii, first, home in work:
            hot = jnp.where(spot == cells(ii) - first, 1.0, 0.0).astype(BF16)
            out = lax.dot_general(prof(ii), hot, (((1,), (1,)), ((), ())), preferred_element_type=F32)
            outs.append(out[:DEPTH] + out[DEPTH:])
        for (ii, first, home), out in zip(work, outs):
            x, at = home >> 1, pl.ds(pl.multiple_of((home & 1) * BIN, BIN), BIN)
            pile[x, :, at] = pile[x, :, at] + out
        return i, j

    @pl.when(start <= stop)
    def _():
        lax.fori_loop(0, (steps + unroll - 1) // unroll, step, (start, jnp.int32(first_bin)))


def split3(a):
    h1 = a.astype(BF16)
    r = a - h1.astype(F32)
    h2 = r.astype(BF16)
    h3 = (r - h2.astype(F32)).astype(BF16)
    return h1, h2, h3


def particle_kernel(
    tgt, src, cnt, origin, loc, vel, halo_lo, halo_hi, site, bulk, octants, urow,
    nloc, nvel, skey, schg, last, send_lo, send_hi,
    left, right, stat, acc, zrow, key, last_v, last_s, rows, sem,
):
    wide = 4 * 128

    def prepare(x3, v3, at, width):
        pad = jnp.zeros((5, width), F32)
        x = jnp.concatenate([x3, pad], axis=0)
        v = jnp.concatenate([v3, pad], axis=0)
        row = iota((8, width), 0)
        xs = x * math.sqrt(LOG2E)
        q = 0.5 * jnp.sum(xs * xs, axis=0, keepdims=True)
        full = jnp.where(row < 3, xs, jnp.where(row < 5, q, 0.0))
        h = [p.astype(F32) for p in split3(full)]

        def mix(a, b, is_target):
            base = h[a]
            if b is None:
                return jnp.where(row < 3, base, 0.0)
            if is_target:
                return jnp.where(row < 3, base, jnp.where(row == 3, h[b], jnp.where(row == 4, 1.0, 0.0)))
            return jnp.where(row < 3, base, jnp.where(row == 3, -1.0, jnp.where(row == 4, -h[b], 0.0)))

        extra = [0, 1, 2, None, None, None]
        ta = [0, 0, 1, 1, 0, 2]
        sa = [0, 1, 0, 1, 2, 0]
        for p in range(0, 6, 2):
            lt = jnp.concatenate([mix(ta[p], extra[p], True), mix(ta[p + 1], extra[p + 1], True)], axis=0)
            rt = jnp.concatenate([mix(sa[p], extra[p], False), mix(sa[p + 1], extra[p + 1], False)], axis=0)
            left[pl.ds(8 * p, 16), pl.ds(at, width)] = lt.astype(BF16)
            right[pl.ds(8 * p, 16), pl.ds(at, width)] = rt.astype(BF16)
        w = (2.0 * x - v) * (1.0 / 256.0)
        wh = w.astype(BF16).astype(F32)
        wl = w - wh
        w2 = jnp.concatenate([jnp.where(row == 3, 1.0, wh), wl], axis=0)
        stat[:, pl.ds(at, width)] = w2.astype(BF16)

    prepare(halo_lo[0:3, :], halo_lo[3:6, :], 0, HB * 128)
    prepare(halo_hi[0:3, :], halo_hi[3:6, :], (NB + HB) * 128, HB * 128)

    def prep(i, carry):
        at = pl.multiple_of(i * wide, wide)
        prepare(loc[:, pl.ds(at, wide)], vel[:, pl.ds(at, wide)], pl.multiple_of(at + HB * 128, 128), wide)
        return carry

    lax.fori_loop(0, NPART // wide, prep, 0)
    acc[...] = jnp.zeros_like(acc)
    live = cnt[0]

    def tiles(g, carry):
        outs = []
        for u in range(TILE_UNROLL):
            t = g * TILE_UNROLL + u
            a = tgt[t] & (NB - 1)
            b = a + (src[t] - tgt[t]) + HB
            lm = left[:, pl.ds(pl.multiple_of((a + HB) * 128, 128), 128)]
            rm = right[:, pl.ds(pl.multiple_of(b * 128, 128), 128)]
            arg = lax.dot_general(rm, lm, (((0,), (0,)), ((), ())), preferred_element_type=F32)
            g_mn = jnp.exp2(arg)
            gh = g_mn.astype(BF16)
            gl = (g_mn - gh.astype(F32)).astype(BF16)
            s = stat[:, pl.ds(pl.multiple_of(b * 128, 128), 128)]
            out = jnp.dot(
                jnp.concatenate([s, s], axis=1),
                jnp.concatenate([gh, gl], axis=0),
                preferred_element_type=F32,
            )
            home = jnp.where(t < live, a, NB)
            outs.append((home, out[0:8] + out[8:16]))
        for home, out in outs:
            at = pl.multiple_of(home * 8, 8)
            acc[pl.ds(at, 8), :] = acc[pl.ds(at, 8), :] + out
        return carry

    lax.fori_loop(0, (live + TILE_UNROLL - 1) // TILE_UNROLL, tiles, 0)

    def advance(i, carry):
        for u in range(8):
            b = i * 8 + u
            at = pl.multiple_of(b * 128, 128)
            x = loc[:, pl.ds(at, 128)]
            v = vel[:, pl.ds(at, 128)]
            f = acc[pl.ds(pl.multiple_of(b * 8, 8), 8), :]
            w = (2.0 * x - v) * (1.0 / 256.0)
            force = w * f[3:4] - f[0:3]
            nv = v + 0.5 * force
            nx = x + 0.5 * nv
            nvel[:, pl.ds(at, 128)] = nv
            nloc[:, pl.ds(at, 128)] = nx
            zrow[pl.ds(b, 1), :] = nx[2:3]
            p = site[:, pl.ds(at, 128)]
            cell = (p[1:2] - origin[0]) * CY + (p[2:3] - origin[1])
            key[pl.ds(b, 1), :] = cell * DEPTH + p[0:1]
        return carry

    lax.fori_loop(0, NB // 8, advance, 0)

    charge = bulk[...] * octants[...].astype(F32) * 0.125 * (1.0 + 0.5 * jnp.tanh(zrow[...]))
    keys = key[...]
    ks = [keys[8 * r : 8 * r + 8] for r in range(16)]
    cs = [charge[8 * r : 8 * r + 8] for r in range(16)]
    ks, cs = bitonic(ks, cs)
    last[...] = ks[15][7:8]
    last_v[...] = ks[15]
    lasts = pltpu.make_async_copy(last_v, last_s, sem.at[0])
    lasts.start()
    kt = jnp.concatenate(ks, axis=0)
    ct = jnp.concatenate(cs, axis=0)
    kt = jnp.transpose(kt)
    ct = jnp.transpose(ct)
    skey[...] = kt
    schg[...] = ct
    for ref, at in ((send_lo, 0), (send_hi, 96)):
        kk = kt[at : at + 32]
        ref[0:32] = (kk >> 15).astype(F32)
        ref[32:64] = ((kk >> 6) & 511).astype(F32)
        ref[64:96] = (kk & 63).astype(F32)
        ref[96:128] = ct[at : at + 32]
    for r in range(4):
        ref = send_lo if r < 2 else send_hi
        for c in range(4):
            at = 128 + ((r % 2) * 4 + c) * DEPTH
            ref[at : at + DEPTH] = urow[r, :, 128 * c : 128 * c + 128]
    rows[...] = jnp.zeros_like(rows)
    lasts.wait()

    def cells(i):
        return skey[pl.ds(i, 1), :] >> 6

    def prof(i):
        return profile((skey[pl.ds(i, 1), :] & 63).astype(F32), schg[pl.ds(i, 1), :])

    for n, x in enumerate((G, G + CX - 2)):
        walk(
            rows, cells, prof, OWN, (ks[15][7:8] >> 14).astype(F32), lambda i: last_s[7, i] >> 14,
            2 * x, 2 * x + 3, 2 * x - 4 * n, ROW_UNROLL,
        )
    for r in range(4):
        ref = send_lo if r < 2 else send_hi
        for c in range(4):
            at = PART + ((r % 2) * 4 + c) * DEPTH
            ref[at : at + DEPTH] = rows[r, :, 128 * c : 128 * c + 128]
    for ref in (send_lo, send_hi):
        ref[SEND - 8 : SEND] = jnp.broadcast_to(last[...].astype(F32), (8, 128))


def particles(tgt, src, cnt, origin, loc, vel, halo_lo, halo_hi, site, bulk, octants, urow):
    sd = jax.ShapeDtypeStruct
    return pl.pallas_call(
        particle_kernel,
        out_shape=(
            sd((3, NPART), F32), sd((3, NPART), F32),
            sd((128, 128), I32), sd((128, 128), F32), sd((1, 128), I32),
            sd((SEND, 128), F32), sd((SEND, 128), F32),
        ),
        in_specs=[SSPEC] * 4 + [VSPEC] * 8,
        out_specs=(VSPEC,) * 7,
        scratch_shapes=[
            pltpu.VMEM((48, NEXT * 128), BF16),
            pltpu.VMEM((48, NEXT * 128), BF16),
            pltpu.VMEM((16, NEXT * 128), BF16),
            pltpu.VMEM(((NB + 1) * 8, 128), F32),
            pltpu.VMEM((NB, 128), F32),
            pltpu.VMEM((NB, 128), I32),
            pltpu.VMEM((8, 128), I32),
            pltpu.SMEM((8, 128), I32),
            pltpu.VMEM((4, DEPTH, CY), F32),
            pltpu.SemaphoreType.DMA((1,)),
        ],
        compiler_params=pltpu.CompilerParams(vmem_limit_bytes=VMEM_LIMIT),
        name="particle_step",
    )(tgt, src, cnt, origin, loc, vel, halo_lo, halo_hi, site, bulk, octants, urow)


def own_deposit_kernel(last, last_v, skey, schg, pile, cells, prof):
    own = skey[...]
    cells[0:OWN] = (own >> 6) - (G - HB) * CY

    def profiles(i, carry):
        for u in range(8):
            b = i * 8 + u
            z = (skey[pl.ds(b, 1), :] & 63).astype(F32)
            prof[b] = profile(z, schg[pl.ds(b, 1), :])
        return carry

    lax.fori_loop(0, OWN // 8, profiles, 0)

    def clear(i, carry):
        pile[i] = jnp.zeros((DEPTH, CY), F32)
        return carry

    lax.fori_loop(0, XW, clear, 0)
    walk(
        pile, lambda i: cells[pl.ds(i, 1), :], lambda i: prof[i], OWN,
        ((last_v[...] >> 14) - 2 * (G - HB)).astype(F32),
        lambda i: (last[i] >> 14) - 2 * (G - HB), 0, BINS - 1, 0, WALK_UNROLL,
    )


def own_deposit(last, last_v, skey, schg):
    sd = jax.ShapeDtypeStruct
    return pl.pallas_call(
        own_deposit_kernel,
        out_shape=sd((XW, DEPTH, CY), F32),
        in_specs=[SSPEC, VSPEC, VSPEC, VSPEC],
        out_specs=VSPEC,
        scratch_shapes=[
            pltpu.VMEM((OWN, 128), I32),
            pltpu.VMEM((OWN, 128, 128), BF16),
        ],
        compiler_params=pltpu.CompilerParams(vmem_limit_bytes=VMEM_LIMIT),
        name="own_deposit",
    )(last, last_v, skey, schg)


def edge_deposit_kernel(
    meta, pile_in, recv_lo, recv_hi, ucol,
    here, vrow, pay_lo, pay_hi,
    pile, cells, prof, packs, last_v, last_s, sems,
):
    load = pltpu.make_async_copy(pile_in, pile, sems.at[0])
    load.start()
    last_v[0:1] = recv_lo[SEND - 8 : SEND - 7].astype(I32)
    last_v[1:2] = recv_hi[SEND - 8 : SEND - 7].astype(I32)
    lasts = pltpu.make_async_copy(last_v, last_s, sems.at[1])
    lasts.start()
    for ref, at, shift in ((recv_lo, 0, HB - G - CX), (recv_hi, RECV, HB + CX - G)):
        x = ref[0:32].astype(I32) + shift
        cells[at : at + RECV] = x * CY + ref[32:64].astype(I32)

    def profiles(i, carry):
        for ref, at in ((recv_lo, 0), (recv_hi, RECV)):
            for u in range(4):
                b = i * 4 + u
                prof[at + b] = profile(ref[pl.ds(64 + b, 1), :], ref[pl.ds(96 + b, 1), :])
        return carry

    lax.fori_loop(0, RECV // 4, profiles, 0)
    lasts.wait()
    load.wait()
    half = 2 * (2 + G)
    slot = iota((1, 128), 1)
    for n, (at, by, first, end) in enumerate((
        (OWN - RECV, HB - G - CX, 4, half - 1), (0, HB + CX - G, half, 2 * (2 + CX) - 1),
    )):
        sent = jnp.logical_and(slot >= at, slot < at + RECV)
        bins = jnp.where(sent, (last_v[n : n + 1] >> 14) + 2 * by, 4 * BINS).astype(F32)
        walk(
            pile, lambda i: cells[pl.ds(n * RECV + i, 1), :], lambda i: prof[n * RECV + i], RECV, bins,
            lambda i: (last_s[n, at + i] >> 14) + 2 * by, first, end, 0, WALK_UNROLL,
        )

    def turn(x):
        return pltpu.make_async_copy(pile.at[x + HB], here.at[:, x, :], sems.at[2 + x])

    def turn_start(x, carry):
        turn(x).start()
        return carry

    lax.fori_loop(0, CX, turn_start, 0)
    for ref, x0, flag in ((recv_lo, 0, meta[2]), (recv_hi, CX + 2, meta[3])):
        for r in range(2):
            for c in range(4):
                at = PART + (r * 4 + c) * DEPTH
                cols = slice(128 * c, 128 * c + 128)
                pile[x0 + r, :, cols] = flag * (pile[x0 + r, :, cols] + ref[at : at + DEPTH])
    for n, x in enumerate((0, 1, 2, CX + 1, CX + 2, CX + 3)):
        vrow[n] = pile[x]
    lane = iota((DEPTH, 128), 1)
    packs[...] = jnp.zeros_like(packs)

    def pick(row, at):
        a = pile[row, :, 0:128]
        b = pile[row, :, 384:512]
        for n, (t, by) in enumerate(((a, at), (a, at + 127), (b, at + 2), (b, at + 1))):
            packs[n] = jnp.where(lane == at, pltpu.roll(t, by & 127, 1), packs[n])

    def picks(x, carry):
        pick(x + 2, x)
        return carry

    lax.fori_loop(0, CX, picks, 0, unroll=4)
    pick(1, CX)
    pick(CX + 2, CX + 1)
    base = 128 + 4 * DEPTH
    for pay, recv_col, near, far in ((pay_lo, 0, 0, 1), (pay_hi, 3, 3, 2)):
        lo = recv_lo[base + recv_col * DEPTH : base + recv_col * DEPTH + DEPTH]
        hi = recv_hi[128 + recv_col * DEPTH : 128 + recv_col * DEPTH + DEPTH]
        by = 0 if recv_col == 0 else 1
        corner = jnp.where(lane == CX, pltpu.roll(lo, CX + by, 1), 0.0)
        corner = jnp.where(lane == CX + 1, pltpu.roll(hi, CX + 1 + by, 1), corner)
        t = jnp.transpose(jnp.concatenate([corner, packs[near]], axis=0))
        pay[0:CX] = t[0:CX] + ucol[near]
        pay[CX : CX + 8] = t[CX : CX + 8]
        t = jnp.transpose(jnp.concatenate([jnp.zeros((DEPTH, 128), F32), packs[far]], axis=0))
        pay[40 : 40 + CX] = t[0:CX] + ucol[far]
        pay[40 + CX : 80] = jnp.zeros((8, 128), F32)

    def turn_wait(x, carry):
        turn(x).wait()
        return carry

    lax.fori_loop(0, CX, turn_wait, 0)


def edge_deposit(meta, pile, recv_lo, recv_hi, ucol):
    sd = jax.ShapeDtypeStruct
    return pl.pallas_call(
        edge_deposit_kernel,
        out_shape=(
            sd((DEPTH, CX, CY), F32), sd((6, DEPTH, CY), F32),
            sd((80, 128), F32), sd((80, 128), F32),
        ),
        in_specs=[SSPEC, ASPEC] + [VSPEC] * 3,
        out_specs=(VSPEC,) * 4,
        scratch_shapes=[
            pltpu.VMEM((XW, DEPTH, CY), F32),
            pltpu.VMEM((2 * RECV, 128), I32),
            pltpu.VMEM((2 * RECV, 128, 128), BF16),
            pltpu.VMEM((4, DEPTH, 128), F32),
            pltpu.VMEM((2, 128), I32),
            pltpu.SMEM((2, 128), I32),
            pltpu.SemaphoreType.DMA((2 + CX,)),
        ],
        compiler_params=pltpu.CompilerParams(vmem_limit_bytes=VMEM_LIMIT),
        name="edge_deposit",
    )(meta, pile, recv_lo, recv_hi, ucol)


def edges_kernel(cells, urow, ucol, left, right, sems):
    rows = [
        pltpu.make_async_copy(cells.at[:, x, :], urow.at[r], sems.at[2 + r])
        for r, x in enumerate((0, 1, CX - 2, CX - 1))
    ]
    cols = [
        pltpu.make_async_copy(cells.at[:, :, pl.ds(at, 128)], ref, sems.at[n])
        for n, (ref, at) in enumerate(((left, 0), (right, CY - 128)))
    ]
    for copy in cols + rows:
        copy.start()
    for copy in cols:
        copy.wait()
    lane = iota((CX, 128), 1)
    acc = [jnp.zeros((CX, 128), F32)] * 4
    for z in range(DEPTH):
        for n, (ref, by) in enumerate(((left, z), (left, z + 127), (right, z + 2), (right, z + 1))):
            by = by & 127
            a = ref[z] if by == 0 else pltpu.roll(ref[z], by, 1)
            acc[n] = jnp.where(lane == z, a, acc[n])
    for n in range(4):
        ucol[n] = acc[n]
    for copy in rows:
        copy.wait()


def edges(cells):
    sd = jax.ShapeDtypeStruct
    return pl.pallas_call(
        edges_kernel,
        out_shape=(sd((4, DEPTH, CY), F32), sd((4, CX, 128), F32)),
        in_specs=[ASPEC],
        out_specs=(VSPEC, VSPEC),
        scratch_shapes=[
            pltpu.VMEM((DEPTH, CX, 128), F32),
            pltpu.VMEM((DEPTH, CX, 128), F32),
            pltpu.SemaphoreType.DMA((6,)),
        ],
        compiler_params=pltpu.CompilerParams(vmem_limit_bytes=VMEM_LIMIT),
        name="temperature_edges",
    )(cells)


def half_kappa(u, v):
    return 0.05 * (1.0 + 0.5 * jnp.tanh(u)) / (1.0 + v)


def flux(k, kn, u, un):
    return (k + kn) * (un - u)


def glow_of(rows):
    d = rows * (1.0 / BAND)
    return 0.5 * jnp.exp(-(d * d))


TILES = range(CY // 128)


def tile(c):
    return slice(128 * c, 128 * c + 128)


def load(ref, z):
    return [ref[z, :, tile(c)] for c in TILES]


def heat_planes(src, dst, vs, kz, fz, row_f, col_f, fix, glow, after):
    lane = iota((CX, 128), 1)
    sub = iota((CX, 128), 0)

    def fetch(z):
        u = load(src, z)
        if fix is not None:
            u[0] = jnp.where(lane == 0, pltpu.roll(fix[...], (128 - z) & 127, 1), u[0])
            u[3] = jnp.where(lane == 127, pltpu.roll(fix[...], 63 - z, 1), u[3])
        return u

    u0 = fetch(0)
    v0 = load(vs, 0)
    for c in TILES:
        k = half_kappa(u0[c], v0[c])
        kz[:, tile(c)] = k
        fz[:, tile(c)] = (k + 0.05) * u0[c]

    def planes(z0, is_last):
        k = [kz[:, tile(c)] for c in TILES]
        down = [fz[:, tile(c)] for c in TILES]
        u = fetch(z0)
        for p in range(PLANES):
            z = z0 + p
            v = load(vs, z)
            if is_last and p == PLANES - 1:
                un, kn = u, k
                up = [(k[c] + 0.05) * (0.0 - u[c]) for c in TILES]
            else:
                un = fetch(z + 1)
                vn = load(vs, z + 1)
                kn = [half_kappa(un[c], vn[c]) for c in TILES]
                up = [flux(k[c], kn[c], u[c], un[c]) for c in TILES]
            row_first = row_f[pl.ds(z, 1), :]
            row_end = row_f[pl.ds(z + DEPTH, 1), :]
            ru = [pltpu.roll(u[c], 1, 1) for c in TILES]
            rk = [pltpu.roll(k[c], 1, 1) for c in TILES]
            g = []
            for c in TILES:
                if c == 0:
                    f = flux(k[0], rk[0], ru[0], u[0])
                    if col_f is not None:
                        f = jnp.where(lane == 0, pltpu.roll(col_f[...], (128 - z) & 127, 1), f)
                else:
                    pu = jnp.where(lane == 0, ru[c - 1], ru[c])
                    pk = jnp.where(lane == 0, rk[c - 1], rk[c])
                    f = flux(k[c], pk, pu, u[c])
                g.append(f)
            rg = [pltpu.roll(g[c], 127, 1) for c in TILES]
            for c in TILES:
                if c < 3:
                    gn = jnp.where(lane == 127, rg[c + 1], rg[c])
                elif col_f is not None:
                    gn = jnp.where(lane == 127, pltpu.roll(col_f[...], 63 - z, 1), rg[c])
                else:
                    gn = rg[c]
                f = flux(k[c], pltpu.roll(k[c], 1, 0), pltpu.roll(u[c], 1, 0), u[c])
                f = jnp.where(sub == 0, row_first[:, tile(c)], f)
                fn = jnp.where(sub == CX - 1, row_end[:, tile(c)], pltpu.roll(f, CX - 1, 0))
                total = (up[c] - down[c]) + (fn - f) + (gn - g[c])
                dst[z, :, tile(c)] = u[c] + total + glow * v[c]
            k, down, u = kn, up, un
        for c in TILES:
            kz[:, tile(c)] = k[c]
            fz[:, tile(c)] = down[c]

    groups = DEPTH // PLANES

    def group(g, carry):
        planes(g * PLANES, False)
        after(g)
        return carry

    lax.fori_loop(0, groups - 1, group, 0)
    planes(DEPTH - PLANES, True)


def heat_one_kernel(meta, us, vs, urow, recv_lo, recv_hi, vrow, mid, mrow, share, kz, fz, row1, sem):
    save = pltpu.make_async_copy(vs, share, sem.at[0])
    save.start()
    lane_w = iota((DEPTH, CY), 1)
    sub_w = iota((DEPTH, CY), 0)
    for n in range(2):
        recv = recv_lo if n == 0 else recv_hi

        def got_row(r):
            base = 128 + r * 4 * DEPTH
            return jnp.concatenate([recv[base + c * DEPTH : base + (c + 1) * DEPTH] for c in range(4)], axis=1)

        uo, uh = (got_row(0), got_row(1)) if n == 0 else (got_row(1), got_row(0))
        ui = urow[0] if n == 0 else urow[3]
        vo, vh, vi = (vrow[0], vrow[1], vrow[2]) if n == 0 else (vrow[5], vrow[4], vrow[3])
        kh = half_kappa(uh, vh)
        ki = half_kappa(ui, vi)
        total = flux(kh, half_kappa(uo, vo), uh, uo) + flux(kh, ki, uh, ui)

        def near(a, pad):
            left = jnp.where(lane_w == 0, a, pltpu.roll(a, 1, 1))
            right = jnp.where(lane_w == CY - 1, a, pltpu.roll(a, CY - 1, 1))
            up = jnp.where(sub_w == DEPTH - 1, pad, pltpu.roll(a, DEPTH - 1, 0))
            down = jnp.where(sub_w == 0, pad, pltpu.roll(a, 1, 0))
            return left, right, up, down

        for kn, un in zip(near(kh, 0.05), near(uh, 0.0)):
            total = total + flux(kh, kn, uh, un)
        row_at = meta[0] + (-1.0 if n == 0 else float(CX))
        gl = glow_of(jnp.full((1, CY), 1.0, F32) * row_at)
        mrow[n] = uh + total + gl * vh
        row1[DEPTH * n : DEPTH * n + DEPTH] = flux(kh, ki, uh, ui) if n == 0 else flux(ki, kh, ui, uh)
    glow = glow_of(iota((CX, 128), 0).astype(F32) + meta[0])
    heat_planes(us, mid, vs, kz, fz, row1, None, None, glow, lambda g: None)
    save.wait()


def heat_one(meta, u, v, urow, recv_lo, recv_hi, vrow):
    sd = jax.ShapeDtypeStruct
    return pl.pallas_call(
        heat_one_kernel,
        out_shape=(sd((DEPTH, CX, CY), F32), sd((2, DEPTH, CY), F32), sd((DEPTH, CX, CY), F32)),
        in_specs=[SSPEC] + [VSPEC] * 6,
        out_specs=(VSPEC, VSPEC, ASPEC),
        scratch_shapes=[
            pltpu.VMEM((CX, CY), F32), pltpu.VMEM((CX, CY), F32),
            pltpu.VMEM((2 * DEPTH, CY), F32),
            pltpu.SemaphoreType.DMA((1,)),
        ],
        compiler_params=pltpu.CompilerParams(vmem_limit_bytes=VMEM_LIMIT),
        cost_estimate=pl.CostEstimate(flops=1 << 25, bytes_accessed=1 << 24, transcendentals=1 << 21),
        name="heat_step_one",
    )(meta, u, v, urow, recv_lo, recv_hi, vrow)


def heat_two_kernel(
    meta, mid, vs, mpart, recv_lo, recv_hi, vrow, pay_lo, pay_hi, got_lo, got_hi, out_hbm,
    os, kz, fz, row2, fix, col2, sems,
):
    lane = iota((CX, 128), 1)
    sub = iota((CX, 128), 0)
    lo_half = lane < DEPTH
    side = jnp.where(lo_half, meta[4], meta[5])
    glow1 = glow_of(sub.astype(F32) + meta[0])

    def stacks(a, b, at, size):
        p, q = a[at : at + size], b[at : at + size]
        low = iota((size, 128), 1) < DEPTH
        return jnp.where(low, p, pltpu.roll(q, DEPTH, 1)), jnp.where(low, pltpu.roll(p, DEPTH, 1), q)

    def column_step(outer, here, inner, ends):
        (uo, vo), (uh, vh), (ui, vi), (ue, ve) = outer, here, inner, ends
        kh = half_kappa(uh, vh)
        ke = half_kappa(ue, ve)
        total = flux(kh, half_kappa(uo, vo), uh, uo) + flux(kh, half_kappa(ui, vi), uh, ui)

        def near(a, e, pad):
            below = jnp.where(sub == 0, e[0:1], pltpu.roll(a, 1, 0))
            above = jnp.where(sub == CX - 1, e[1:2], pltpu.roll(a, CX - 1, 0))
            up = jnp.where((lane & (DEPTH - 1)) == DEPTH - 1, pad, pltpu.roll(a, 127, 1))
            down = jnp.where((lane & (DEPTH - 1)) == 0, pad, pltpu.roll(a, 1, 1))
            return below, above, up, down

        for kn, un in zip(near(kh, ke, 0.05), near(uh, ue, 0.0)):
            total = total + flux(kh, kn, uh, un)
        return uh + total + glow1 * vh

    outer = stacks(got_lo, got_hi, 40, CX)
    here = stacks(got_lo, got_hi, 0, CX)
    inner = stacks(pay_lo, pay_hi, 0, CX)
    next_in = stacks(pay_lo, pay_hi, 40, CX)
    mid_out = column_step(outer, here, inner, stacks(got_lo, got_hi, CX, 8)) * side
    mid_in = column_step(here, inner, next_in, stacks(pay_lo, pay_hi, CX, 8))
    sign = jnp.where(lo_half, 1.0, -1.0)
    fix[...] = mid_in
    col2[...] = sign * flux(half_kappa(mid_out, here[1]), half_kappa(mid_in, inner[1]), mid_out, mid_in)

    tail = [jnp.transpose(jnp.concatenate([g[CX : CX + 8]] * 16, axis=0)) for g in (got_lo, got_hi)]
    ends = jnp.transpose(jnp.concatenate([mid_in] * 4, axis=0))
    lane_t = iota((DEPTH, 128), 1)

    def turned(a, by):
        return pltpu.roll(a, by & 127, 1) if by & 127 else a

    for n in range(2):
        x = 0 if n == 0 else CX - 1
        recv, r, vh = (recv_lo, 1, vrow[1]) if n == 0 else (recv_hi, 0, vrow[4])
        mh = [mpart[n, :, tile(c)] for c in TILES]
        mi = [mid[:, x, tile(c)] for c in TILES]
        for c, at, half, g, e in ((0, 0, 0, 0, 0), (3, 127, DEPTH, 1, 127)):
            base = 128 + (r * 4 + c) * DEPTH
            uc = recv[base : base + DEPTH]
            kc = half_kappa(uc, vh[:, tile(c)])
            ue = turned(tail[g][:DEPTH], e - n)
            ke = half_kappa(ue, turned(tail[g][DEPTH:], e - n))
            mh[c] = mh[c] + jnp.where(lane_t == at, flux(kc, ke, uc, ue), 0.0)
            mi[c] = jnp.where(lane_t == at, turned(ends[half : half + DEPTH], e - x), mi[c])
        vi = vrow[2] if n == 0 else vrow[3]
        for c in TILES:
            m = mh[c] * meta[2 + n]
            kh = half_kappa(m, vh[:, tile(c)])
            ki = half_kappa(mi[c], vi[:, tile(c)])
            row2[DEPTH * n : DEPTH * n + DEPTH, tile(c)] = flux(kh, ki, m, mi[c]) if n == 0 else flux(ki, kh, mi[c], m)

    per = 8 // PLANES

    def store(c):
        at = pl.ds(pl.multiple_of(c * 8, 8), 8)
        return pltpu.make_async_copy(os.at[at], out_hbm.at[at], sems.at[c])

    def after(g):
        @pl.when(lax.rem(g, per) == per - 1)
        def _():
            store(g // per).start()

    glow = glow_of(sub.astype(F32) + meta[1])
    heat_planes(mid, os, vs, kz, fz, row2, col2, fix, glow, after)
    store(DEPTH // 8 - 1).start()
    for c in range(DEPTH // 8):
        store(c).wait()


def heat_two(meta, mid, v, mpart, recv_lo, recv_hi, vrow, pay_lo, pay_hi, got_lo, got_hi):
    return pl.pallas_call(
        heat_two_kernel,
        out_shape=jax.ShapeDtypeStruct((DEPTH, CX, CY), F32),
        in_specs=[SSPEC] + [VSPEC] * 10,
        out_specs=ASPEC,
        scratch_shapes=[
            pltpu.VMEM((DEPTH, CX, CY), F32),
            pltpu.VMEM((CX, CY), F32), pltpu.VMEM((CX, CY), F32),
            pltpu.VMEM((2 * DEPTH, CY), F32),
            pltpu.VMEM((CX, 128), F32), pltpu.VMEM((CX, 128), F32),
            pltpu.SemaphoreType.DMA((DEPTH // 8,)),
        ],
        compiler_params=pltpu.CompilerParams(vmem_limit_bytes=VMEM_LIMIT),
        name="heat_step_two",
    )(meta, mid, v, mpart, recv_lo, recv_hi, vrow, pay_lo, pay_hi, got_lo, got_hi)


def shift(value, axis, steps):
    count = lax.axis_size(axis)
    first, stop = max(0, -steps), min(count, count - steps)
    return lax.ppermute(value, axis, [(i, i + steps) for i in range(first, stop)])


def body(
    particle_locations,
    particle_speeds,
    particle_bulk,
    receiving_group_per_pair,
    emitting_group_per_pair,
    active_pair_slots,
    landing_site_triple,
    landing_weight_octants,
    thermal_excess,
    molten_strip_midlines,
):
    states = jnp.concatenate([particle_locations, particle_speeds], axis=0)
    width = HB * 128
    halo_lo = shift(states[:, NPART - width :], ("gx", "gy"), 1)
    halo_hi = shift(states[:, :width], ("gx", "gy"), -1)
    urow, ucol = edges(thermal_excess)

    gx, gy = lax.axis_index("gx"), lax.axis_index("gy")
    row_start, col_start = gx * CX, gy * CY
    beam = row_start - molten_strip_midlines
    inside = jnp.stack([gx > 0, gx < lax.axis_size("gx") - 1, gy > 0, gy < lax.axis_size("gy") - 1])
    meta = jnp.concatenate([beam.astype(F32), inside.astype(F32)])
    origin = jnp.stack([row_start - G, col_start])

    nloc, nvel, skey, schg, last, send_lo, send_hi = particles(
        receiving_group_per_pair, emitting_group_per_pair, active_pair_slots, origin,
        particle_locations, particle_speeds, halo_lo, halo_hi, landing_site_triple,
        particle_bulk.reshape(128, 128), landing_weight_octants.reshape(128, 128), urow,
    )
    recv_lo = shift(send_hi, "gx", 1)
    recv_hi = shift(send_lo, "gx", -1)
    pile = own_deposit(last.reshape(128), last, skey, schg)
    here, vrow, pay_lo, pay_hi = edge_deposit(meta, pile, recv_lo, recv_hi, ucol)
    got_lo = shift(pay_hi, "gy", 1)
    got_hi = shift(pay_lo, "gy", -1)
    mid, mpart, share = heat_one(meta, thermal_excess, here, urow, recv_lo, recv_hi, vrow)
    final = heat_two(meta, mid, here, mpart, recv_lo, recv_hi, vrow, pay_lo, pay_hi, got_lo, got_hi)
    return nloc, nvel, share, final


def solution(mesh):
    placed = (
        P(None, ("gx", "gy")),
        P(None, ("gx", "gy")),
        P(("gx", "gy")),
        P(("gx", "gy")),
        P(("gx", "gy")),
        P(("gx", "gy")),
        P(None, ("gx", "gy")),
        P(("gx", "gy")),
        P(None, "gx", "gy"),
        P(),
    )
    return jax.shard_map(
        body,
        mesh=mesh,
        in_specs=placed,
        out_specs=(
            P(None, ("gx", "gy")),
            P(None, ("gx", "gy")),
            P(None, "gx", "gy"),
            P(None, "gx", "gy"),
        ),
        check_vma=False,
    )
```

```python
import math

import jax
import jax.numpy as jnp
from jax import lax
from jax.experimental import pallas as pl
from jax.experimental.pallas import tpu as pltpu
from jax.sharding import PartitionSpec as P

F32 = jnp.float32
BF16 = jnp.bfloat16
I32 = jnp.int32

DEPTH = 64
CX = 32
CY = 512
NPART = 16384
G = 16
HB = 2
NB = 128
NEXT = NB + 2 * HB
SLOTS = 256
BAND = 64.0
BIN = 256
LOG2E = 1.4426950408889634
VMEM_LIMIT = 30 * 1024 * 1024
TILE_UNROLL = 32
WALK_UNROLL = 32
ROW_UNROLL = 16
PLANES = 8
CHUNK = 8
XW = CX + 4
BINS = 2 * XW
PART = 128 + 8 * DEPTH
SEND = PART + 8 * DEPTH + 8

VSPEC = pl.BlockSpec(memory_space=pltpu.VMEM)
SSPEC = pl.BlockSpec(memory_space=pltpu.SMEM)
ASPEC = pl.BlockSpec(memory_space=pl.ANY)
HSPEC = pl.BlockSpec(memory_space=pltpu.HBM)


def iota(shape, dim):
    return lax.broadcasted_iota(I32, shape, dim)


def cross_stage(ks, cs, step, axis):
    at = iota((8, 128), axis)
    other = at ^ step
    low = (at & step) == 0
    nk, nc = [], []
    for k, c in zip(ks, cs):
        pk = jnp.take_along_axis(k, other, axis=axis)
        pc = jnp.take_along_axis(c, other, axis=axis)
        m = jnp.where(low, jnp.minimum(k, pk), jnp.maximum(k, pk))
        nk.append(m)
        nc.append(jnp.where(m != k, pc, c))
    return nk, nc


def vreg_stage(ks, cs, j, descending):
    ks, cs = list(ks), list(cs)
    for r in range(16):
        if r & (1 << j):
            continue
        a, b = r, r | (1 << j)
        if descending(r):
            a, b = b, a
        less = ks[b] < ks[a]
        ks[a], ks[b] = jnp.minimum(ks[a], ks[b]), jnp.maximum(ks[a], ks[b])
        cs[a], cs[b] = jnp.where(less, cs[b], cs[a]), jnp.where(less, cs[a], cs[b])
    return ks, cs


def bitonic(ks, cs):
    sub = iota((8, 128), 0)
    lane = iota((8, 128), 1)
    up = lambda r: False

    def low_stages(ks, cs, top):
        for j in range(top, 3, -1):
            step = 1 << (j - 4)
            ks, cs = cross_stage(ks, cs, step, 0)
        for j in range(min(top, 3), -1, -1):
            ks, cs = vreg_stage(ks, cs, j, up)
        return ks, cs

    for k in range(1, 4):
        for j in range(k - 1, -1, -1):
            ks, cs = vreg_stage(ks, cs, j, lambda r: bool(r & (1 << k)))
    for k in range(4, 7):
        flip = -((sub >> (k - 4)) & 1)
        ks = [a ^ flip for a in ks]
        ks, cs = low_stages(ks, cs, k - 1)
        ks = [a ^ flip for a in ks]

    def phase(k, carry):
        ks, cs = list(carry[:16]), list(carry[16:])
        flip = -((lane >> (k - 7)) & 1)
        ks = [a ^ flip for a in ks]

        def lane_step(t, inner):
            step = jnp.left_shift(jnp.int32(1), k - 8 - t)
            nk, nc = cross_stage(list(inner[:16]), list(inner[16:]), step, 1)
            return tuple(nk) + tuple(nc)

        out = lax.fori_loop(0, k - 7, lane_step, tuple(ks) + tuple(cs))
        ks, cs = low_stages(list(out[:16]), list(out[16:]), 6)
        ks = [a ^ flip for a in ks]
        return tuple(ks) + tuple(cs)

    out = lax.fori_loop(7, 15, phase, tuple(ks) + tuple(cs))
    return list(out[:16]), list(out[16:])


OWN, RECV = 128, 32


def profile(z, charge):
    level = iota((DEPTH, 128), 0).astype(F32)
    d = (level - z) * (math.sqrt(LOG2E) / 12.0)
    p = jnp.exp2(-(d * d)) * charge
    hi = p.astype(BF16)
    lo = (p - hi.astype(F32)).astype(BF16)
    return jnp.concatenate([hi, lo], axis=0)


def count_below(bins, limit):
    return jnp.sum(jnp.where(bins < limit, 1.0, 0.0)).astype(I32)


def walk(pile, cells, prof, count, bins, last_bin, first_bin, end_bin, origin, unroll):
    spot = iota((BIN, 128), 0).astype(F32).astype(BF16)
    one, zero = jnp.ones((), BF16), jnp.zeros((), BF16)
    start = count_below(bins, float(first_bin))
    stop = jnp.minimum(count_below(bins, float(end_bin + 1)), count - 1)
    steps = stop - start + 1 + (end_bin - first_bin)

    def step(g, state):
        i, j = state
        work = []
        for u in range(unroll):
            inside = i <= stop
            ii = jnp.minimum(i, count - 1)
            work.append((ii, jnp.where(inside, j * BIN, -(1 << 20)), j - origin))
            more = jnp.logical_and(last_bin(ii) > j, j < end_bin)
            j = jnp.where(more, j + 1, j)
            i = jnp.where(more, i, jnp.minimum(i + 1, count))
        outs = []
        for ii, first, home in work:
            col = cells(ii) - first
            col = jnp.where(jnp.logical_and(col >= 0, col < BIN), col, 300).astype(F32).astype(BF16)
            hot = jnp.where(spot == col, one, zero)
            out = lax.dot_general(prof(ii), hot, (((1,), (1,)), ((), ())), preferred_element_type=F32)
            outs.append(out[:DEPTH] + out[DEPTH:])
        for (ii, first, home), out in zip(work, outs):
            x, at = home >> 1, pl.ds(pl.multiple_of((home & 1) * BIN, BIN), BIN)
            pile[x, :, at] = pile[x, :, at] + out
        return i, j

    @pl.when(start <= stop)
    def _():
        lax.fori_loop(0, (steps + unroll - 1) // unroll, step, (start, jnp.int32(first_bin)))


def split3(a):
    h1 = a.astype(BF16)
    r = a - h1.astype(F32)
    h2 = r.astype(BF16)
    h3 = (r - h2.astype(F32)).astype(BF16)
    return h1, h2, h3


def particle_kernel(
    tgt, src, cnt, origin, loc, vel, halo_lo, halo_hi, site, bulk, octants, urow,
    nloc, nvel, skey, schg, last, send_lo, send_hi,
    left, right, stat, acc, zrow, key, last_v, last_s, rows, sem,
):
    wide = 4 * 128

    def prepare(x3, v3, at, width):
        pad = jnp.zeros((5, width), F32)
        x = jnp.concatenate([x3, pad], axis=0)
        v = jnp.concatenate([v3, pad], axis=0)
        row = iota((8, width), 0)
        xs = x * math.sqrt(LOG2E)
        q = 0.5 * jnp.sum(xs * xs, axis=0, keepdims=True)
        full = jnp.where(row < 3, xs, jnp.where(row < 5, q, 0.0))
        h = [p.astype(F32) for p in split3(full)]

        def mix(a, b, is_target):
            base = h[a]
            if b is None:
                return jnp.where(row < 3, base, 0.0)
            if is_target:
                return jnp.where(row < 3, base, jnp.where(row == 3, h[b], jnp.where(row == 4, 1.0, 0.0)))
            return jnp.where(row < 3, base, jnp.where(row == 3, -1.0, jnp.where(row == 4, -h[b], 0.0)))

        extra = [0, 1, 2, None, None, None]
        ta = [0, 0, 1, 1, 0, 2]
        sa = [0, 1, 0, 1, 2, 0]
        for p in range(0, 6, 2):
            lt = jnp.concatenate([mix(ta[p], extra[p], True), mix(ta[p + 1], extra[p + 1], True)], axis=0)
            rt = jnp.concatenate([mix(sa[p], extra[p], False), mix(sa[p + 1], extra[p + 1], False)], axis=0)
            left[pl.ds(8 * p, 16), pl.ds(at, width)] = lt.astype(BF16)
            right[pl.ds(8 * p, 16), pl.ds(at, width)] = rt.astype(BF16)
        w = (2.0 * x - v) * (1.0 / 256.0)
        wh = w.astype(BF16).astype(F32)
        wl = w - wh
        w2 = jnp.concatenate([jnp.where(row == 3, 1.0, wh), wl], axis=0)
        stat[:, pl.ds(at, width)] = w2.astype(BF16)

    prepare(halo_lo[0:3, :], halo_lo[3:6, :], 0, HB * 128)
    prepare(halo_hi[0:3, :], halo_hi[3:6, :], (NB + HB) * 128, HB * 128)

    def prep(i, carry):
        at = pl.multiple_of(i * wide, wide)
        prepare(loc[:, pl.ds(at, wide)], vel[:, pl.ds(at, wide)], pl.multiple_of(at + HB * 128, 128), wide)
        return carry

    lax.fori_loop(0, NPART // wide, prep, 0)
    acc[...] = jnp.zeros_like(acc)
    live = cnt[0]

    def tiles(g, carry):
        outs = []
        for u in range(TILE_UNROLL):
            t = g * TILE_UNROLL + u
            a = tgt[t] & (NB - 1)
            b = a + (src[t] - tgt[t]) + HB
            lm = left[:, pl.ds(pl.multiple_of((a + HB) * 128, 128), 128)]
            rm = right[:, pl.ds(pl.multiple_of(b * 128, 128), 128)]
            arg = lax.dot_general(rm, lm, (((0,), (0,)), ((), ())), preferred_element_type=F32)
            g_mn = jnp.exp2(arg)
            gh = g_mn.astype(BF16)
            gl = (g_mn - gh.astype(F32)).astype(BF16)
            s = stat[:, pl.ds(pl.multiple_of(b * 128, 128), 128)]
            out = jnp.dot(
                jnp.concatenate([s, s], axis=1),
                jnp.concatenate([gh, gl], axis=0),
                preferred_element_type=F32,
            )
            home = jnp.where(t < live, a, NB)
            outs.append((home, out[0:8] + out[8:16]))
        for home, out in outs:
            at = pl.multiple_of(home * 8, 8)
            acc[pl.ds(at, 8), :] = acc[pl.ds(at, 8), :] + out
        return carry

    lax.fori_loop(0, (live + TILE_UNROLL - 1) // TILE_UNROLL, tiles, 0)

    def advance(i, carry):
        for u in range(8):
            b = i * 8 + u
            at = pl.multiple_of(b * 128, 128)
            x = loc[:, pl.ds(at, 128)]
            v = vel[:, pl.ds(at, 128)]
            f = acc[pl.ds(pl.multiple_of(b * 8, 8), 8), :]
            w = (2.0 * x - v) * (1.0 / 256.0)
            force = w * f[3:4] - f[0:3]
            nv = v + 0.5 * force
            nx = x + 0.5 * nv
            nvel[:, pl.ds(at, 128)] = nv
            nloc[:, pl.ds(at, 128)] = nx
            zrow[pl.ds(b, 1), :] = nx[2:3]
            p = site[:, pl.ds(at, 128)]
            cell = (p[1:2] - origin[0]) * CY + (p[2:3] - origin[1])
            key[pl.ds(b, 1), :] = cell * DEPTH + p[0:1]
        return carry

    lax.fori_loop(0, NB // 8, advance, 0)

    charge = bulk[...] * octants[...].astype(F32) * 0.125 * (1.0 + 0.5 * jnp.tanh(zrow[...]))
    keys = key[...]
    ks = [keys[8 * r : 8 * r + 8] for r in range(16)]
    cs = [charge[8 * r : 8 * r + 8] for r in range(16)]
    ks, cs = bitonic(ks, cs)
    last[...] = ks[15][7:8]
    last_v[...] = ks[15]
    lasts = pltpu.make_async_copy(last_v, last_s, sem.at[0])
    lasts.start()
    kt = jnp.concatenate(ks, axis=0)
    ct = jnp.concatenate(cs, axis=0)
    kt = jnp.transpose(kt)
    ct = jnp.transpose(ct)
    skey[...] = kt
    schg[...] = ct
    for ref, at in ((send_lo, 0), (send_hi, 96)):
        kk = kt[at : at + 32]
        ref[0:32] = (kk >> 15).astype(F32)
        ref[32:64] = ((kk >> 6) & 511).astype(F32)
        ref[64:96] = (kk & 63).astype(F32)
        ref[96:128] = ct[at : at + 32]
    for r in range(4):
        ref = send_lo if r < 2 else send_hi
        for c in range(4):
            at = 128 + ((r % 2) * 4 + c) * DEPTH
            ref[at : at + DEPTH] = urow[r, :, 128 * c : 128 * c + 128]
    rows[...] = jnp.zeros_like(rows)
    lasts.wait()

    def cells(i):
        return skey[pl.ds(i, 1), :] >> 6

    def prof(i):
        return profile((skey[pl.ds(i, 1), :] & 63).astype(F32), schg[pl.ds(i, 1), :])

    for n, x in enumerate((G, G + CX - 2)):
        walk(
            rows, cells, prof, OWN, (ks[15][7:8] >> 14).astype(F32), lambda i: last_s[7, i] >> 14,
            2 * x, 2 * x + 3, 2 * x - 4 * n, ROW_UNROLL,
        )
    for r in range(4):
        ref = send_lo if r < 2 else send_hi
        for c in range(4):
            at = PART + ((r % 2) * 4 + c) * DEPTH
            ref[at : at + DEPTH] = rows[r, :, 128 * c : 128 * c + 128]
    for ref in (send_lo, send_hi):
        ref[SEND - 8 : SEND] = jnp.broadcast_to(last[...].astype(F32), (8, 128))


def particles(tgt, src, cnt, origin, loc, vel, halo_lo, halo_hi, site, bulk, octants, urow):
    sd = jax.ShapeDtypeStruct
    return pl.pallas_call(
        particle_kernel,
        out_shape=(
            sd((3, NPART), F32), sd((3, NPART), F32),
            sd((128, 128), I32), sd((128, 128), F32), sd((1, 128), I32),
            sd((SEND, 128), F32), sd((SEND, 128), F32),
        ),
        in_specs=[SSPEC] * 4 + [VSPEC] * 8,
        out_specs=(VSPEC,) * 7,
        scratch_shapes=[
            pltpu.VMEM((48, NEXT * 128), BF16),
            pltpu.VMEM((48, NEXT * 128), BF16),
            pltpu.VMEM((16, NEXT * 128), BF16),
            pltpu.VMEM(((NB + 1) * 8, 128), F32),
            pltpu.VMEM((NB, 128), F32),
            pltpu.VMEM((NB, 128), I32),
            pltpu.VMEM((8, 128), I32),
            pltpu.SMEM((8, 128), I32),
            pltpu.VMEM((4, DEPTH, CY), F32),
            pltpu.SemaphoreType.DMA((1,)),
        ],
        compiler_params=pltpu.CompilerParams(vmem_limit_bytes=VMEM_LIMIT),
        name="particle_step",
    )(tgt, src, cnt, origin, loc, vel, halo_lo, halo_hi, site, bulk, octants, urow)


def own_deposit_kernel(last, last_v, skey, schg, pile, cells, prof):
    own = skey[...]
    cells[0:OWN] = (own >> 6) - (G - HB) * CY

    def profiles(i, carry):
        for u in range(8):
            b = i * 8 + u
            z = (skey[pl.ds(b, 1), :] & 63).astype(F32)
            prof[b] = profile(z, schg[pl.ds(b, 1), :])
        return carry

    lax.fori_loop(0, OWN // 8, profiles, 0)

    def clear(i, carry):
        pile[i] = jnp.zeros((DEPTH, CY), F32)
        return carry

    lax.fori_loop(0, XW, clear, 0)
    walk(
        pile, lambda i: cells[pl.ds(i, 1), :], lambda i: prof[i], OWN,
        ((last_v[...] >> 14) - 2 * (G - HB)).astype(F32),
        lambda i: (last[i] >> 14) - 2 * (G - HB), 0, BINS - 1, 0, WALK_UNROLL,
    )


def own_deposit(last, last_v, skey, schg):
    sd = jax.ShapeDtypeStruct
    return pl.pallas_call(
        own_deposit_kernel,
        out_shape=sd((XW, DEPTH, CY), F32),
        in_specs=[SSPEC, VSPEC, VSPEC, VSPEC],
        out_specs=VSPEC,
        scratch_shapes=[
            pltpu.VMEM((OWN, 128), I32),
            pltpu.VMEM((OWN, 128, 128), BF16),
        ],
        compiler_params=pltpu.CompilerParams(vmem_limit_bytes=VMEM_LIMIT),
        name="own_deposit",
    )(last, last_v, skey, schg)


def edge_deposit_kernel(
    meta, pile_in, recv_lo, recv_hi, ucol,
    share, vrow, pay_lo, pay_hi,
    pile, cells, prof, packs, last_v, last_s, sems,
):
    load = pltpu.make_async_copy(pile_in, pile, sems.at[0])
    load.start()
    last_v[0:1] = recv_lo[SEND - 8 : SEND - 7].astype(I32)
    last_v[1:2] = recv_hi[SEND - 8 : SEND - 7].astype(I32)
    lasts = pltpu.make_async_copy(last_v, last_s, sems.at[1])
    lasts.start()
    for ref, at, shift in ((recv_lo, 0, HB - G - CX), (recv_hi, RECV, HB + CX - G)):
        x = ref[0:32].astype(I32) + shift
        cells[at : at + RECV] = x * CY + ref[32:64].astype(I32)

    def profiles(i, carry):
        for ref, at in ((recv_lo, 0), (recv_hi, RECV)):
            for u in range(4):
                b = i * 4 + u
                prof[at + b] = profile(ref[pl.ds(64 + b, 1), :], ref[pl.ds(96 + b, 1), :])
        return carry

    lax.fori_loop(0, RECV // 4, profiles, 0)
    lasts.wait()
    load.wait()
    half = 2 * (2 + G)
    slot = iota((1, 128), 1)
    for n, (at, by, first, end) in enumerate((
        (OWN - RECV, HB - G - CX, 4, half - 1), (0, HB + CX - G, half, 2 * (2 + CX) - 1),
    )):
        sent = jnp.logical_and(slot >= at, slot < at + RECV)
        bins = jnp.where(sent, (last_v[n : n + 1] >> 14) + 2 * by, 4 * BINS).astype(F32)
        walk(
            pile, lambda i: cells[pl.ds(n * RECV + i, 1), :], lambda i: prof[n * RECV + i], RECV, bins,
            lambda i: (last_s[n, at + i] >> 14) + 2 * by, first, end, 0, WALK_UNROLL,
        )

    def turn(x):
        return pltpu.make_async_copy(pile.at[x + HB], share.at[:, x, :], sems.at[2 + x])

    def turn_start(x, carry):
        turn(x).start()
        return carry

    lax.fori_loop(0, CX, turn_start, 0)
    for ref, x0, flag in ((recv_lo, 0, meta[2]), (recv_hi, CX + 2, meta[3])):
        for r in range(2):
            for c in range(4):
                at = PART + (r * 4 + c) * DEPTH
                cols = slice(128 * c, 128 * c + 128)
                pile[x0 + r, :, cols] = flag * (pile[x0 + r, :, cols] + ref[at : at + DEPTH])
    for n, x in enumerate((0, 1, 2, CX + 1, CX + 2, CX + 3)):
        vrow[n] = pile[x]
    lane = iota((DEPTH, 128), 1)
    packs[...] = jnp.zeros_like(packs)

    def pick(row, at):
        a = pile[row, :, 0:128]
        b = pile[row, :, 384:512]
        for n, (t, by) in enumerate(((a, at), (a, at + 127), (b, at + 2), (b, at + 1))):
            packs[n] = jnp.where(lane == at, pltpu.roll(t, by & 127, 1), packs[n])

    def picks(x, carry):
        pick(x + 2, x)
        return carry

    lax.fori_loop(0, CX, picks, 0, unroll=4)
    pick(1, CX)
    pick(CX + 2, CX + 1)
    base = 128 + 4 * DEPTH
    for pay, recv_col, near, far in ((pay_lo, 0, 0, 1), (pay_hi, 3, 3, 2)):
        lo = recv_lo[base + recv_col * DEPTH : base + recv_col * DEPTH + DEPTH]
        hi = recv_hi[128 + recv_col * DEPTH : 128 + recv_col * DEPTH + DEPTH]
        by = 0 if recv_col == 0 else 1
        corner = jnp.where(lane == CX, pltpu.roll(lo, CX + by, 1), 0.0)
        corner = jnp.where(lane == CX + 1, pltpu.roll(hi, CX + 1 + by, 1), corner)
        t = jnp.transpose(jnp.concatenate([corner, packs[near]], axis=0))
        pay[0:CX] = t[0:CX] + ucol[near]
        pay[CX : CX + 8] = t[CX : CX + 8]
        t = jnp.transpose(jnp.concatenate([jnp.zeros((DEPTH, 128), F32), packs[far]], axis=0))
        pay[40 : 40 + CX] = t[0:CX] + ucol[far]
        pay[40 + CX : 80] = jnp.zeros((8, 128), F32)

    def turn_wait(x, carry):
        turn(x).wait()
        return carry

    lax.fori_loop(0, CX, turn_wait, 0)


def edge_deposit(meta, pile, recv_lo, recv_hi, ucol):
    sd = jax.ShapeDtypeStruct
    return pl.pallas_call(
        edge_deposit_kernel,
        out_shape=(
            sd((DEPTH, CX, CY), F32), sd((6, DEPTH, CY), F32),
            sd((80, 128), F32), sd((80, 128), F32),
        ),
        in_specs=[SSPEC, ASPEC] + [VSPEC] * 3,
        out_specs=(HSPEC, VSPEC, VSPEC, VSPEC),
        scratch_shapes=[
            pltpu.VMEM((XW, DEPTH, CY), F32),
            pltpu.VMEM((2 * RECV, 128), I32),
            pltpu.VMEM((2 * RECV, 128, 128), BF16),
            pltpu.VMEM((4, DEPTH, 128), F32),
            pltpu.VMEM((2, 128), I32),
            pltpu.SMEM((2, 128), I32),
            pltpu.SemaphoreType.DMA((2 + CX,)),
        ],
        compiler_params=pltpu.CompilerParams(vmem_limit_bytes=VMEM_LIMIT),
        name="edge_deposit",
    )(meta, pile, recv_lo, recv_hi, ucol)


def edges_kernel(cells, urow, ucol, left, right, sems):
    rows = [
        pltpu.make_async_copy(cells.at[:, x, :], urow.at[r], sems.at[2 + r])
        for r, x in enumerate((0, 1, CX - 2, CX - 1))
    ]
    cols = [
        pltpu.make_async_copy(cells.at[:, :, pl.ds(at, 128)], ref, sems.at[n])
        for n, (ref, at) in enumerate(((left, 0), (right, CY - 128)))
    ]
    for copy in cols + rows:
        copy.start()
    for copy in cols:
        copy.wait()
    lane = iota((CX, 128), 1)
    acc = [jnp.zeros((CX, 128), F32)] * 4
    for z in range(DEPTH):
        for n, (ref, by) in enumerate(((left, z), (left, z + 127), (right, z + 2), (right, z + 1))):
            by = by & 127
            a = ref[z] if by == 0 else pltpu.roll(ref[z], by, 1)
            acc[n] = jnp.where(lane == z, a, acc[n])
    for n in range(4):
        ucol[n] = acc[n]
    for copy in rows:
        copy.wait()


def edges(cells):
    sd = jax.ShapeDtypeStruct
    return pl.pallas_call(
        edges_kernel,
        out_shape=(sd((4, DEPTH, CY), F32), sd((4, CX, 128), F32)),
        in_specs=[ASPEC],
        out_specs=(VSPEC, VSPEC),
        scratch_shapes=[
            pltpu.VMEM((DEPTH, CX, 128), F32),
            pltpu.VMEM((DEPTH, CX, 128), F32),
            pltpu.SemaphoreType.DMA((6,)),
        ],
        compiler_params=pltpu.CompilerParams(vmem_limit_bytes=VMEM_LIMIT),
        name="temperature_edges",
    )(cells)


def half_kappa(u, v):
    return 0.05 * (1.0 + 0.5 * jnp.tanh(u)) / (1.0 + v)


def flux(k, kn, u, un):
    return (k + kn) * (un - u)


def glow_of(rows):
    d = rows * (1.0 / BAND)
    return 0.5 * jnp.exp(-(d * d))


TILES = range(CY // 128)


def tile(c):
    return slice(128 * c, 128 * c + 128)


def load(ref, z):
    return [ref[z, :, tile(c)] for c in TILES]


def heat_planes(src, dst, vs, kz, fz, row_f, col_f, fix, glow, before, after):
    lane = iota((CX, 128), 1)
    sub = iota((CX, 128), 0)

    def both(ref, z):
        return pltpu.roll(ref[...], (128 - 2 * z) & 127, 1)

    def fetch(z):
        u = load(src, z)
        if fix is not None:
            ends = both(fix, z)
            u[0] = jnp.where(lane == 0, ends, u[0])
            u[3] = jnp.where(lane == 127, ends, u[3])
        return u

    u0 = fetch(0)
    v0 = load(vs, 0)
    for c in TILES:
        k = half_kappa(u0[c], v0[c])
        kz[:, tile(c)] = k
        fz[:, tile(c)] = (k + 0.05) * u0[c]

    def planes(z0, is_last):
        k = [kz[:, tile(c)] for c in TILES]
        down = [fz[:, tile(c)] for c in TILES]
        u = fetch(z0)
        for p in range(PLANES):
            z = z0 + p
            v = load(vs, z)
            if is_last and p == PLANES - 1:
                un, kn = u, k
                up = [(k[c] + 0.05) * (0.0 - u[c]) for c in TILES]
            else:
                un = fetch(z + 1)
                vn = load(vs, z + 1)
                kn = [half_kappa(un[c], vn[c]) for c in TILES]
                up = [flux(k[c], kn[c], u[c], un[c]) for c in TILES]
            row_first = row_f[pl.ds(z, 1), :]
            row_end = row_f[pl.ds(z + DEPTH, 1), :]
            ru = [pltpu.roll(u[c], 1, 1) for c in TILES]
            rk = [pltpu.roll(k[c], 1, 1) for c in TILES]
            ends = None if col_f is None else both(col_f, z)
            g = []
            for c in TILES:
                if c == 0:
                    f = flux(k[0], rk[0], ru[0], u[0])
                    if col_f is not None:
                        f = jnp.where(lane == 0, ends, f)
                else:
                    pu = jnp.where(lane == 0, ru[c - 1], ru[c])
                    pk = jnp.where(lane == 0, rk[c - 1], rk[c])
                    f = flux(k[c], pk, pu, u[c])
                g.append(f)
            rg = [pltpu.roll(g[c], 127, 1) for c in TILES]
            for c in TILES:
                if c < 3:
                    gn = jnp.where(lane == 127, rg[c + 1], rg[c])
                elif col_f is not None:
                    gn = jnp.where(lane == 127, ends, rg[c])
                else:
                    gn = rg[c]
                f = flux(k[c], pltpu.roll(k[c], 1, 0), pltpu.roll(u[c], 1, 0), u[c])
                f = jnp.where(sub == 0, row_first[:, tile(c)], f)
                fn = jnp.where(sub == CX - 1, row_end[:, tile(c)], pltpu.roll(f, CX - 1, 0))
                total = (up[c] - down[c]) + (fn - f) + (gn - g[c])
                dst[z, :, tile(c)] = u[c] + total + glow * v[c]
            k, down, u = kn, up, un
        for c in TILES:
            kz[:, tile(c)] = k[c]
            fz[:, tile(c)] = down[c]

    groups = DEPTH // PLANES

    def group(g, carry):
        before(g)
        planes(g * PLANES, False)
        after(g)
        return carry

    lax.fori_loop(0, groups - 1, group, 0)
    planes(DEPTH - PLANES, True)


def heat_one_kernel(meta, us, share, urow, recv_lo, recv_hi, vrow, mid, mrow, vs, kz, fz, row1, sems):
    def bring(c):
        at = pl.ds(pl.multiple_of(c * CHUNK, CHUNK), CHUNK)
        return pltpu.make_async_copy(share.at[at], vs.at[at], sems.at[c])

    for c in range(2):
        bring(c).start()
    lane_w = iota((DEPTH, CY), 1)
    sub_w = iota((DEPTH, CY), 0)
    for n in range(2):
        recv = recv_lo if n == 0 else recv_hi

        def got_row(r):
            base = 128 + r * 4 * DEPTH
            return jnp.concatenate([recv[base + c * DEPTH : base + (c + 1) * DEPTH] for c in range(4)], axis=1)

        uo, uh = (got_row(0), got_row(1)) if n == 0 else (got_row(1), got_row(0))
        ui = urow[0] if n == 0 else urow[3]
        vo, vh, vi = (vrow[0], vrow[1], vrow[2]) if n == 0 else (vrow[5], vrow[4], vrow[3])
        kh = half_kappa(uh, vh)
        ki = half_kappa(ui, vi)
        total = flux(kh, half_kappa(uo, vo), uh, uo) + flux(kh, ki, uh, ui)

        def near(a, pad):
            left = jnp.where(lane_w == 0, a, pltpu.roll(a, 1, 1))
            right = jnp.where(lane_w == CY - 1, a, pltpu.roll(a, CY - 1, 1))
            up = jnp.where(sub_w == DEPTH - 1, pad, pltpu.roll(a, DEPTH - 1, 0))
            down = jnp.where(sub_w == 0, pad, pltpu.roll(a, 1, 0))
            return left, right, up, down

        for kn, un in zip(near(kh, 0.05), near(uh, 0.0)):
            total = total + flux(kh, kn, uh, un)
        row_at = meta[0] + (-1.0 if n == 0 else float(CX))
        gl = glow_of(jnp.full((1, CY), 1.0, F32) * row_at)
        mrow[n] = uh + total + gl * vh
        row1[DEPTH * n : DEPTH * n + DEPTH] = flux(kh, ki, uh, ui) if n == 0 else flux(ki, kh, ui, uh)
    glow = glow_of(iota((CX, 128), 0).astype(F32) + meta[0])

    def before(g):
        per = CHUNK // PLANES

        @pl.when(lax.rem(g, per) == per - 1)
        def _():
            c = (g + 1) // per
            bring(c).wait()

            @pl.when(c + 1 < DEPTH // CHUNK)
            def _():
                bring(c + 1).start()

    bring(0).wait()
    heat_planes(us, mid, vs, kz, fz, row1, None, None, glow, before, lambda g: None)


def heat_one(meta, u, v, urow, recv_lo, recv_hi, vrow):
    sd = jax.ShapeDtypeStruct
    return pl.pallas_call(
        heat_one_kernel,
        out_shape=(sd((DEPTH, CX, CY), F32), sd((2, DEPTH, CY), F32), sd((DEPTH, CX, CY), F32)),
        in_specs=[SSPEC, VSPEC, HSPEC] + [VSPEC] * 4,
        out_specs=(VSPEC,) * 3,
        scratch_shapes=[
            pltpu.VMEM((CX, CY), F32), pltpu.VMEM((CX, CY), F32),
            pltpu.VMEM((2 * DEPTH, CY), F32),
            pltpu.SemaphoreType.DMA((DEPTH // CHUNK,)),
        ],
        compiler_params=pltpu.CompilerParams(vmem_limit_bytes=VMEM_LIMIT),
        cost_estimate=pl.CostEstimate(flops=1 << 25, bytes_accessed=1 << 24, transcendentals=1 << 21),
        name="heat_step_one",
    )(meta, u, v, urow, recv_lo, recv_hi, vrow)


def heat_two_kernel(
    meta, mid, vs, mpart, recv_lo, recv_hi, vrow, pay_lo, pay_hi, got_lo, got_hi, out_hbm,
    os, kz, fz, row2, fix, col2, sems,
):
    lane = iota((CX, 128), 1)
    sub = iota((CX, 128), 0)
    lo_half = lane < DEPTH
    side = jnp.where(lo_half, meta[4], meta[5])
    glow1 = glow_of(sub.astype(F32) + meta[0])

    def stacks(a, b, at, size):
        p, q = a[at : at + size], b[at : at + size]
        low = iota((size, 128), 1) < DEPTH
        return jnp.where(low, p, pltpu.roll(q, DEPTH, 1)), jnp.where(low, pltpu.roll(p, DEPTH, 1), q)

    def column_step(outer, here, inner, ends):
        (uo, vo), (uh, vh), (ui, vi), (ue, ve) = outer, here, inner, ends
        kh = half_kappa(uh, vh)
        ke = half_kappa(ue, ve)
        total = flux(kh, half_kappa(uo, vo), uh, uo) + flux(kh, half_kappa(ui, vi), uh, ui)

        def near(a, e, pad):
            below = jnp.where(sub == 0, e[0:1], pltpu.roll(a, 1, 0))
            above = jnp.where(sub == CX - 1, e[1:2], pltpu.roll(a, CX - 1, 0))
            up = jnp.where((lane & (DEPTH - 1)) == DEPTH - 1, pad, pltpu.roll(a, 127, 1))
            down = jnp.where((lane & (DEPTH - 1)) == 0, pad, pltpu.roll(a, 1, 1))
            return below, above, up, down

        for kn, un in zip(near(kh, ke, 0.05), near(uh, ue, 0.0)):
            total = total + flux(kh, kn, uh, un)
        return uh + total + glow1 * vh

    outer = stacks(got_lo, got_hi, 40, CX)
    here = stacks(got_lo, got_hi, 0, CX)
    inner = stacks(pay_lo, pay_hi, 0, CX)
    next_in = stacks(pay_lo, pay_hi, 40, CX)
    mid_out = column_step(outer, here, inner, stacks(got_lo, got_hi, CX, 8)) * side
    mid_in = column_step(here, inner, next_in, stacks(pay_lo, pay_hi, CX, 8))
    sign = jnp.where(lo_half, 1.0, -1.0)
    lane8 = iota((8, 128), 1)
    source = ((lane8 + 1) >> 1) & (DEPTH - 1)
    source = jnp.where((lane8 & 1) == 0, source, source + DEPTH)

    def weave(ref, a):
        for i in range(0, CX, 8):
            ref[i : i + 8] = jnp.take_along_axis(a[i : i + 8], source, axis=1)

    weave(fix, mid_in)
    weave(col2, sign * flux(half_kappa(mid_out, here[1]), half_kappa(mid_in, inner[1]), mid_out, mid_in))

    tail = [jnp.transpose(jnp.concatenate([g[CX : CX + 8]] * 16, axis=0)) for g in (got_lo, got_hi)]
    ends = jnp.transpose(jnp.concatenate([mid_in] * 4, axis=0))
    lane_t = iota((DEPTH, 128), 1)

    def turned(a, by):
        return pltpu.roll(a, by & 127, 1) if by & 127 else a

    for n in range(2):
        x = 0 if n == 0 else CX - 1
        recv, r, vh = (recv_lo, 1, vrow[1]) if n == 0 else (recv_hi, 0, vrow[4])
        mh = [mpart[n, :, tile(c)] for c in TILES]
        mi = [mid[:, x, tile(c)] for c in TILES]
        for c, at, half, g, e in ((0, 0, 0, 0, 0), (3, 127, DEPTH, 1, 127)):
            base = 128 + (r * 4 + c) * DEPTH
            uc = recv[base : base + DEPTH]
            kc = half_kappa(uc, vh[:, tile(c)])
            ue = turned(tail[g][:DEPTH], e - n)
            ke = half_kappa(ue, turned(tail[g][DEPTH:], e - n))
            mh[c] = mh[c] + jnp.where(lane_t == at, flux(kc, ke, uc, ue), 0.0)
            mi[c] = jnp.where(lane_t == at, turned(ends[half : half + DEPTH], e - x), mi[c])
        vi = vrow[2] if n == 0 else vrow[3]
        for c in TILES:
            m = mh[c] * meta[2 + n]
            kh = half_kappa(m, vh[:, tile(c)])
            ki = half_kappa(mi[c], vi[:, tile(c)])
            row2[DEPTH * n : DEPTH * n + DEPTH, tile(c)] = flux(kh, ki, m, mi[c]) if n == 0 else flux(ki, kh, mi[c], m)

    per = 8 // PLANES

    def store(c):
        at = pl.ds(pl.multiple_of(c * 8, 8), 8)
        return pltpu.make_async_copy(os.at[at], out_hbm.at[at], sems.at[c])

    def after(g):
        @pl.when(lax.rem(g, per) == per - 1)
        def _():
            store(g // per).start()

    glow = glow_of(sub.astype(F32) + meta[1])
    heat_planes(mid, os, vs, kz, fz, row2, col2, fix, glow, lambda g: None, after)
    store(DEPTH // 8 - 1).start()
    for c in range(DEPTH // 8):
        store(c).wait()


def heat_two(meta, mid, v, mpart, recv_lo, recv_hi, vrow, pay_lo, pay_hi, got_lo, got_hi):
    return pl.pallas_call(
        heat_two_kernel,
        out_shape=jax.ShapeDtypeStruct((DEPTH, CX, CY), F32),
        in_specs=[SSPEC] + [VSPEC] * 10,
        out_specs=ASPEC,
        scratch_shapes=[
            pltpu.VMEM((DEPTH, CX, CY), F32),
            pltpu.VMEM((CX, CY), F32), pltpu.VMEM((CX, CY), F32),
            pltpu.VMEM((2 * DEPTH, CY), F32),
            pltpu.VMEM((CX, 128), F32), pltpu.VMEM((CX, 128), F32),
            pltpu.SemaphoreType.DMA((DEPTH // 8,)),
        ],
        compiler_params=pltpu.CompilerParams(vmem_limit_bytes=VMEM_LIMIT),
        name="heat_step_two",
    )(meta, mid, v, mpart, recv_lo, recv_hi, vrow, pay_lo, pay_hi, got_lo, got_hi)


def shift(value, axis, steps):
    count = lax.axis_size(axis)
    first, stop = max(0, -steps), min(count, count - steps)
    return lax.ppermute(value, axis, [(i, i + steps) for i in range(first, stop)])


def body(
    particle_locations,
    particle_speeds,
    particle_bulk,
    receiving_group_per_pair,
    emitting_group_per_pair,
    active_pair_slots,
    landing_site_triple,
    landing_weight_octants,
    thermal_excess,
    molten_strip_midlines,
):
    states = jnp.concatenate([particle_locations, particle_speeds], axis=0)
    width = HB * 128
    halo_lo = shift(states[:, NPART - width :], ("gx", "gy"), 1)
    halo_hi = shift(states[:, :width], ("gx", "gy"), -1)
    urow, ucol = edges(thermal_excess)

    gx, gy = lax.axis_index("gx"), lax.axis_index("gy")
    row_start, col_start = gx * CX, gy * CY
    beam = row_start - molten_strip_midlines
    inside = jnp.stack([gx > 0, gx < lax.axis_size("gx") - 1, gy > 0, gy < lax.axis_size("gy") - 1])
    meta = jnp.concatenate([beam.astype(F32), inside.astype(F32)])
    origin = jnp.stack([row_start - G, col_start])

    nloc, nvel, skey, schg, last, send_lo, send_hi = particles(
        receiving_group_per_pair, emitting_group_per_pair, active_pair_slots, origin,
        particle_locations, particle_speeds, halo_lo, halo_hi, landing_site_triple,
        particle_bulk.reshape(128, 128), landing_weight_octants.reshape(128, 128), urow,
    )
    recv_lo = shift(send_hi, "gx", 1)
    recv_hi = shift(send_lo, "gx", -1)
    pile = own_deposit(last.reshape(128), last, skey, schg)
    share, vrow, pay_lo, pay_hi = edge_deposit(meta, pile, recv_lo, recv_hi, ucol)
    got_lo = shift(pay_hi, "gy", 1)
    got_hi = shift(pay_lo, "gy", -1)
    mid, mpart, here = heat_one(meta, thermal_excess, pltpu.with_memory_space_constraint(share, pltpu.HBM), urow, recv_lo, recv_hi, vrow)
    final = heat_two(meta, mid, here, mpart, recv_lo, recv_hi, vrow, pay_lo, pay_hi, got_lo, got_hi)
    return nloc, nvel, share, final


def solution(mesh):
    placed = (
        P(None, ("gx", "gy")),
        P(None, ("gx", "gy")),
        P(("gx", "gy")),
        P(("gx", "gy")),
        P(("gx", "gy")),
        P(("gx", "gy")),
        P(None, ("gx", "gy")),
        P(("gx", "gy")),
        P(None, "gx", "gy"),
        P(),
    )
    return jax.shard_map(
        body,
        mesh=mesh,
        in_specs=placed,
        out_specs=(
            P(None, ("gx", "gy")),
            P(None, ("gx", "gy")),
            P(None, "gx", "gy"),
            P(None, "gx", "gy"),
        ),
        check_vma=False,
    )
```

```python
import math

import jax
import jax.numpy as jnp
from jax import lax
from jax.experimental import pallas as pl
from jax.experimental.pallas import tpu as pltpu
from jax.sharding import PartitionSpec as P

F32 = jnp.float32
BF16 = jnp.bfloat16
I32 = jnp.int32

DEPTH = 64
CX = 32
CY = 512
NPART = 16384
G = 16
HB = 2
NB = 128
NEXT = NB + 2 * HB
SLOTS = 256
BAND = 64.0
BIN = 256
LOG2E = 1.4426950408889634
VMEM_LIMIT = 30 * 1024 * 1024
TILE_UNROLL = 64
WALK_UNROLL = 32
ROW_UNROLL = 16
PLANES = 8
CHUNK = 8
AHEAD = 5
XW = CX + 4
BINS = 2 * XW
PART = 128 + 8 * DEPTH
SEND = PART + 8 * DEPTH + 8

VSPEC = pl.BlockSpec(memory_space=pltpu.VMEM)
SSPEC = pl.BlockSpec(memory_space=pltpu.SMEM)
ASPEC = pl.BlockSpec(memory_space=pl.ANY)
HSPEC = pl.BlockSpec(memory_space=pltpu.HBM)


def iota(shape, dim):
    return lax.broadcasted_iota(I32, shape, dim)


def cross_stage(ks, cs, step, axis):
    at = iota((8, 128), axis)
    other = at ^ step
    low = (at & step) == 0
    nk, nc = [], []
    for k, c in zip(ks, cs):
        pk = jnp.take_along_axis(k, other, axis=axis)
        pc = jnp.take_along_axis(c, other, axis=axis)
        m = jnp.where(low, jnp.minimum(k, pk), jnp.maximum(k, pk))
        nk.append(m)
        nc.append(jnp.where(m != k, pc, c))
    return nk, nc


def vreg_stage(ks, cs, j, descending):
    ks, cs = list(ks), list(cs)
    for r in range(16):
        if r & (1 << j):
            continue
        a, b = r, r | (1 << j)
        if descending(r):
            a, b = b, a
        less = ks[b] < ks[a]
        ks[a], ks[b] = jnp.minimum(ks[a], ks[b]), jnp.maximum(ks[a], ks[b])
        cs[a], cs[b] = jnp.where(less, cs[b], cs[a]), jnp.where(less, cs[a], cs[b])
    return ks, cs


def bitonic(ks, cs):
    sub = iota((8, 128), 0)
    lane = iota((8, 128), 1)
    up = lambda r: False

    def low_stages(ks, cs, top):
        for j in range(top, 3, -1):
            step = 1 << (j - 4)
            ks, cs = cross_stage(ks, cs, step, 0)
        for j in range(min(top, 3), -1, -1):
            ks, cs = vreg_stage(ks, cs, j, up)
        return ks, cs

    for k in range(1, 4):
        for j in range(k - 1, -1, -1):
            ks, cs = vreg_stage(ks, cs, j, lambda r: bool(r & (1 << k)))
    for k in range(4, 7):
        flip = -((sub >> (k - 4)) & 1)
        ks = [a ^ flip for a in ks]
        ks, cs = low_stages(ks, cs, k - 1)
        ks = [a ^ flip for a in ks]

    def phase(k, carry):
        ks, cs = list(carry[:16]), list(carry[16:])
        flip = -((lane >> (k - 7)) & 1)
        ks = [a ^ flip for a in ks]

        def lane_step(t, inner):
            step = jnp.left_shift(jnp.int32(1), k - 8 - t)
            nk, nc = cross_stage(list(inner[:16]), list(inner[16:]), step, 1)
            return tuple(nk) + tuple(nc)

        out = lax.fori_loop(0, k - 7, lane_step, tuple(ks) + tuple(cs))
        ks, cs = low_stages(list(out[:16]), list(out[16:]), 6)
        ks = [a ^ flip for a in ks]
        return tuple(ks) + tuple(cs)

    out = lax.fori_loop(7, 15, phase, tuple(ks) + tuple(cs))
    return list(out[:16]), list(out[16:])


OWN, RECV = 128, 32


def profile(z, charge):
    level = iota((DEPTH, 128), 0).astype(F32)
    d = (level - z) * (math.sqrt(LOG2E) / 12.0)
    p = jnp.exp2(-(d * d)) * charge
    hi = p.astype(BF16)
    lo = (p - hi.astype(F32)).astype(BF16)
    return jnp.concatenate([hi, lo], axis=0)


def count_below(bins, limit):
    return jnp.sum(jnp.where(bins < limit, 1.0, 0.0)).astype(I32)


def walk(pile, cells, prof, count, bins, last_bin, first_bin, end_bin, origin, unroll):
    spot = iota((BIN, 128), 0).astype(F32).astype(BF16)
    one, zero = jnp.ones((), BF16), jnp.zeros((), BF16)
    start = count_below(bins, float(first_bin))
    stop = jnp.minimum(count_below(bins, float(end_bin + 1)), count - 1)
    steps = stop - start + 1 + (end_bin - first_bin)

    def step(g, state):
        i, j = state
        work = []
        for u in range(unroll):
            inside = i <= stop
            ii = jnp.minimum(i, count - 1)
            work.append((ii, jnp.where(inside, j * BIN, -(1 << 20)), j - origin))
            more = jnp.logical_and(last_bin(ii) > j, j < end_bin)
            j = jnp.where(more, j + 1, j)
            i = jnp.where(more, i, jnp.minimum(i + 1, count))
        outs = []
        for ii, first, home in work:
            col = cells(ii) - first
            col = jnp.where(jnp.logical_and(col >= 0, col < BIN), col, 300).astype(F32).astype(BF16)
            hot = jnp.where(spot == col, one, zero)
            out = lax.dot_general(prof(ii), hot, (((1,), (1,)), ((), ())), preferred_element_type=F32)
            outs.append(out[:DEPTH] + out[DEPTH:])
        for (ii, first, home), out in zip(work, outs):
            x, at = home >> 1, pl.ds(pl.multiple_of((home & 1) * BIN, BIN), BIN)
            pile[x, :, at] = pile[x, :, at] + out
        return i, j

    @pl.when(start <= stop)
    def _():
        lax.fori_loop(0, (steps + unroll - 1) // unroll, step, (start, jnp.int32(first_bin)))


def split3(a):
    h1 = a.astype(BF16)
    r = a - h1.astype(F32)
    h2 = r.astype(BF16)
    h3 = (r - h2.astype(F32)).astype(BF16)
    return h1, h2, h3


def particle_kernel(
    tgt, src, cnt, origin, loc, vel, halo_lo, halo_hi, site, bulk, octants, urow,
    nloc, nvel, skey, schg, last, send_lo, send_hi,
    left, right, stat, acc, zrow, key, last_v, last_s, rows, sem,
):
    wide = 4 * 128

    def prepare(x3, v3, at, width):
        pad = jnp.zeros((5, width), F32)
        x = jnp.concatenate([x3, pad], axis=0)
        v = jnp.concatenate([v3, pad], axis=0)
        row = iota((8, width), 0)
        xs = x * math.sqrt(LOG2E)
        q = 0.5 * jnp.sum(xs * xs, axis=0, keepdims=True)
        full = jnp.where(row < 3, xs, jnp.where(row < 5, q, 0.0))
        h = [p.astype(F32) for p in split3(full)]

        def mix(a, b, is_target):
            base = h[a]
            if b is None:
                return jnp.where(row < 3, base, 0.0)
            if is_target:
                return jnp.where(row < 3, base, jnp.where(row == 3, h[b], jnp.where(row == 4, 1.0, 0.0)))
            return jnp.where(row < 3, base, jnp.where(row == 3, -1.0, jnp.where(row == 4, -h[b], 0.0)))

        extra = [0, 1, 2, None, None, None]
        ta = [0, 0, 1, 1, 0, 2]
        sa = [0, 1, 0, 1, 2, 0]
        for p in range(0, 6, 2):
            lt = jnp.concatenate([mix(ta[p], extra[p], True), mix(ta[p + 1], extra[p + 1], True)], axis=0)
            rt = jnp.concatenate([mix(sa[p], extra[p], False), mix(sa[p + 1], extra[p + 1], False)], axis=0)
            left[pl.ds(8 * p, 16), pl.ds(at, width)] = lt.astype(BF16)
            right[pl.ds(8 * p, 16), pl.ds(at, width)] = rt.astype(BF16)
        w = (2.0 * x - v) * (1.0 / 256.0)
        wh = w.astype(BF16).astype(F32)
        wl = w - wh
        w2 = jnp.concatenate([jnp.where(row == 3, 1.0, wh), wl], axis=0)
        stat[:, pl.ds(at, width)] = w2.astype(BF16)

    prepare(halo_lo[0:3, :], halo_lo[3:6, :], 0, HB * 128)
    prepare(halo_hi[0:3, :], halo_hi[3:6, :], (NB + HB) * 128, HB * 128)

    def prep(i, carry):
        at = pl.multiple_of(i * wide, wide)
        prepare(loc[:, pl.ds(at, wide)], vel[:, pl.ds(at, wide)], pl.multiple_of(at + HB * 128, 128), wide)
        return carry

    lax.fori_loop(0, NPART // wide, prep, 0)
    acc[...] = jnp.zeros_like(acc)
    live = cnt[0]

    def tiles(g, carry):
        outs = []
        for u in range(TILE_UNROLL):
            t = g * TILE_UNROLL + u
            a = tgt[t] & (NB - 1)
            b = a + (src[t] - tgt[t]) + HB
            lm = left[:, pl.ds(pl.multiple_of((a + HB) * 128, 128), 128)]
            rm = right[:, pl.ds(pl.multiple_of(b * 128, 128), 128)]
            arg = lax.dot_general(rm, lm, (((0,), (0,)), ((), ())), preferred_element_type=F32)
            g_mn = jnp.exp2(arg)
            gh = g_mn.astype(BF16)
            gl = (g_mn - gh.astype(F32)).astype(BF16)
            s = stat[:, pl.ds(pl.multiple_of(b * 128, 128), 128)]
            out = jnp.dot(
                jnp.concatenate([s, s], axis=1),
                jnp.concatenate([gh, gl], axis=0),
                preferred_element_type=F32,
            )
            home = jnp.where(t < live, a, NB)
            outs.append((home, out[0:8] + out[8:16]))
        for home, out in outs:
            at = pl.multiple_of(home * 8, 8)
            acc[pl.ds(at, 8), :] = acc[pl.ds(at, 8), :] + out
        return carry

    lax.fori_loop(0, (live + TILE_UNROLL - 1) // TILE_UNROLL, tiles, 0)

    def advance(i, carry):
        for u in range(8):
            b = i * 8 + u
            at = pl.multiple_of(b * 128, 128)
            x = loc[:, pl.ds(at, 128)]
            v = vel[:, pl.ds(at, 128)]
            f = acc[pl.ds(pl.multiple_of(b * 8, 8), 8), :]
            w = (2.0 * x - v) * (1.0 / 256.0)
            force = w * f[3:4] - f[0:3]
            nv = v + 0.5 * force
            nx = x + 0.5 * nv
            nvel[:, pl.ds(at, 128)] = nv
            nloc[:, pl.ds(at, 128)] = nx
            zrow[pl.ds(b, 1), :] = nx[2:3]
            p = site[:, pl.ds(at, 128)]
            cell = (p[1:2] - origin[0]) * CY + (p[2:3] - origin[1])
            key[pl.ds(b, 1), :] = cell * DEPTH + p[0:1]
        return carry

    lax.fori_loop(0, NB // 8, advance, 0)

    charge = bulk[...] * octants[...].astype(F32) * 0.125 * (1.0 + 0.5 * jnp.tanh(zrow[...]))
    keys = key[...]
    ks = [keys[8 * r : 8 * r + 8] for r in range(16)]
    cs = [charge[8 * r : 8 * r + 8] for r in range(16)]
    ks, cs = bitonic(ks, cs)
    last[...] = ks[15][7:8]
    last_v[...] = ks[15]
    lasts = pltpu.make_async_copy(last_v, last_s, sem.at[0])
    lasts.start()
    kt = jnp.concatenate(ks, axis=0)
    ct = jnp.concatenate(cs, axis=0)
    kt = jnp.transpose(kt)
    ct = jnp.transpose(ct)
    skey[...] = kt
    schg[...] = ct
    for ref, at in ((send_lo, 0), (send_hi, 96)):
        kk = kt[at : at + 32]
        ref[0:32] = (kk >> 15).astype(F32)
        ref[32:64] = ((kk >> 6) & 511).astype(F32)
        ref[64:96] = (kk & 63).astype(F32)
        ref[96:128] = ct[at : at + 32]
    for r in range(4):
        ref = send_lo if r < 2 else send_hi
        for c in range(4):
            at = 128 + ((r % 2) * 4 + c) * DEPTH
            ref[at : at + DEPTH] = urow[r, :, 128 * c : 128 * c + 128]
    rows[...] = jnp.zeros_like(rows)
    lasts.wait()

    def cells(i):
        return skey[pl.ds(i, 1), :] >> 6

    def prof(i):
        return profile((skey[pl.ds(i, 1), :] & 63).astype(F32), schg[pl.ds(i, 1), :])

    for n, x in enumerate((G, G + CX - 2)):
        walk(
            rows, cells, prof, OWN, (ks[15][7:8] >> 14).astype(F32), lambda i: last_s[7, i] >> 14,
            2 * x, 2 * x + 3, 2 * x - 4 * n, ROW_UNROLL,
        )
    for r in range(4):
        ref = send_lo if r < 2 else send_hi
        for c in range(4):
            at = PART + ((r % 2) * 4 + c) * DEPTH
            ref[at : at + DEPTH] = rows[r, :, 128 * c : 128 * c + 128]
    for ref in (send_lo, send_hi):
        ref[SEND - 8 : SEND] = jnp.broadcast_to(last[...].astype(F32), (8, 128))


def particles(tgt, src, cnt, origin, loc, vel, halo_lo, halo_hi, site, bulk, octants, urow):
    sd = jax.ShapeDtypeStruct
    return pl.pallas_call(
        particle_kernel,
        out_shape=(
            sd((3, NPART), F32), sd((3, NPART), F32),
            sd((128, 128), I32), sd((128, 128), F32), sd((1, 128), I32),
            sd((SEND, 128), F32), sd((SEND, 128), F32),
        ),
        in_specs=[SSPEC] * 4 + [VSPEC] * 8,
        out_specs=(VSPEC,) * 7,
        scratch_shapes=[
            pltpu.VMEM((48, NEXT * 128), BF16),
            pltpu.VMEM((48, NEXT * 128), BF16),
            pltpu.VMEM((16, NEXT * 128), BF16),
            pltpu.VMEM(((NB + 1) * 8, 128), F32),
            pltpu.VMEM((NB, 128), F32),
            pltpu.VMEM((NB, 128), I32),
            pltpu.VMEM((8, 128), I32),
            pltpu.SMEM((8, 128), I32),
            pltpu.VMEM((4, DEPTH, CY), F32),
            pltpu.SemaphoreType.DMA((1,)),
        ],
        compiler_params=pltpu.CompilerParams(vmem_limit_bytes=VMEM_LIMIT),
        name="particle_step",
    )(tgt, src, cnt, origin, loc, vel, halo_lo, halo_hi, site, bulk, octants, urow)


def own_deposit_kernel(last, last_v, skey, schg, pile, cells, prof):
    own = skey[...]
    cells[0:OWN] = (own >> 6) - (G - HB) * CY

    def profiles(i, carry):
        for u in range(8):
            b = i * 8 + u
            z = (skey[pl.ds(b, 1), :] & 63).astype(F32)
            prof[b] = profile(z, schg[pl.ds(b, 1), :])
        return carry

    lax.fori_loop(0, OWN // 8, profiles, 0)

    def clear(i, carry):
        pile[i] = jnp.zeros((DEPTH, CY), F32)
        return carry

    lax.fori_loop(0, XW, clear, 0)
    walk(
        pile, lambda i: cells[pl.ds(i, 1), :], lambda i: prof[i], OWN,
        ((last_v[...] >> 14) - 2 * (G - HB)).astype(F32),
        lambda i: (last[i] >> 14) - 2 * (G - HB), 0, BINS - 1, 0, WALK_UNROLL,
    )


def own_deposit(last, last_v, skey, schg):
    sd = jax.ShapeDtypeStruct
    return pl.pallas_call(
        own_deposit_kernel,
        out_shape=sd((XW, DEPTH, CY), F32),
        in_specs=[SSPEC, VSPEC, VSPEC, VSPEC],
        out_specs=VSPEC,
        scratch_shapes=[
            pltpu.VMEM((OWN, 128), I32),
            pltpu.VMEM((OWN, 128, 128), BF16),
        ],
        compiler_params=pltpu.CompilerParams(vmem_limit_bytes=VMEM_LIMIT),
        name="own_deposit",
    )(last, last_v, skey, schg)


def edge_deposit_kernel(
    meta, pile_in, recv_lo, recv_hi, ucol,
    share, vrow, pay_lo, pay_hi,
    pile, cells, prof, packs, last_v, last_s, sems,
):
    load = pltpu.make_async_copy(pile_in, pile, sems.at[0])
    load.start()
    last_v[0:1] = recv_lo[SEND - 8 : SEND - 7].astype(I32)
    last_v[1:2] = recv_hi[SEND - 8 : SEND - 7].astype(I32)
    lasts = pltpu.make_async_copy(last_v, last_s, sems.at[1])
    lasts.start()
    for ref, at, shift in ((recv_lo, 0, HB - G - CX), (recv_hi, RECV, HB + CX - G)):
        x = ref[0:32].astype(I32) + shift
        cells[at : at + RECV] = x * CY + ref[32:64].astype(I32)

    def profiles(i, carry):
        for ref, at in ((recv_lo, 0), (recv_hi, RECV)):
            for u in range(4):
                b = i * 4 + u
                prof[at + b] = profile(ref[pl.ds(64 + b, 1), :], ref[pl.ds(96 + b, 1), :])
        return carry

    lax.fori_loop(0, RECV // 4, profiles, 0)
    lasts.wait()
    load.wait()
    half = 2 * (2 + G)
    slot = iota((1, 128), 1)
    for n, (at, by, first, end) in enumerate((
        (OWN - RECV, HB - G - CX, 4, half - 1), (0, HB + CX - G, half, 2 * (2 + CX) - 1),
    )):
        sent = jnp.logical_and(slot >= at, slot < at + RECV)
        bins = jnp.where(sent, (last_v[n : n + 1] >> 14) + 2 * by, 4 * BINS).astype(F32)
        walk(
            pile, lambda i: cells[pl.ds(n * RECV + i, 1), :], lambda i: prof[n * RECV + i], RECV, bins,
            lambda i: (last_s[n, at + i] >> 14) + 2 * by, first, end, 0, WALK_UNROLL,
        )

    def turn(x):
        return pltpu.make_async_copy(pile.at[x + HB], share.at[:, x, :], sems.at[2 + x])

    def turn_start(x, carry):
        turn(x).start()
        return carry

    lax.fori_loop(0, CX, turn_start, 0)
    for ref, x0, flag in ((recv_lo, 0, meta[2]), (recv_hi, CX + 2, meta[3])):
        for r in range(2):
            for c in range(4):
                at = PART + (r * 4 + c) * DEPTH
                cols = slice(128 * c, 128 * c + 128)
                pile[x0 + r, :, cols] = flag * (pile[x0 + r, :, cols] + ref[at : at + DEPTH])
    for n, x in enumerate((0, 1, 2, CX + 1, CX + 2, CX + 3)):
        vrow[n] = pile[x]
    lane = iota((DEPTH, 128), 1)
    packs[...] = jnp.zeros_like(packs)

    def pick(row, at):
        a = pile[row, :, 0:128]
        b = pile[row, :, 384:512]
        for n, (t, by) in enumerate(((a, at), (a, at + 127), (b, at + 2), (b, at + 1))):
            packs[n] = jnp.where(lane == at, pltpu.roll(t, by & 127, 1), packs[n])

    def picks(x, carry):
        pick(x + 2, x)
        return carry

    lax.fori_loop(0, CX, picks, 0, unroll=4)
    pick(1, CX)
    pick(CX + 2, CX + 1)
    base = 128 + 4 * DEPTH
    for pay, recv_col, near, far in ((pay_lo, 0, 0, 1), (pay_hi, 3, 3, 2)):
        lo = recv_lo[base + recv_col * DEPTH : base + recv_col * DEPTH + DEPTH]
        hi = recv_hi[128 + recv_col * DEPTH : 128 + recv_col * DEPTH + DEPTH]
        by = 0 if recv_col == 0 else 1
        corner = jnp.where(lane == CX, pltpu.roll(lo, CX + by, 1), 0.0)
        corner = jnp.where(lane == CX + 1, pltpu.roll(hi, CX + 1 + by, 1), corner)
        t = jnp.transpose(jnp.concatenate([corner, packs[near]], axis=0))
        pay[0:CX] = t[0:CX] + ucol[near]
        pay[CX : CX + 8] = t[CX : CX + 8]
        t = jnp.transpose(jnp.concatenate([jnp.zeros((DEPTH, 128), F32), packs[far]], axis=0))
        pay[40 : 40 + CX] = t[0:CX] + ucol[far]
        pay[40 + CX : 80] = jnp.zeros((8, 128), F32)

    def turn_wait(x, carry):
        turn(x).wait()
        return carry

    lax.fori_loop(0, CX, turn_wait, 0)


def edge_deposit(meta, pile, recv_lo, recv_hi, ucol):
    sd = jax.ShapeDtypeStruct
    return pl.pallas_call(
        edge_deposit_kernel,
        out_shape=(
            sd((DEPTH, CX, CY), F32), sd((6, DEPTH, CY), F32),
            sd((80, 128), F32), sd((80, 128), F32),
        ),
        in_specs=[SSPEC, ASPEC] + [VSPEC] * 3,
        out_specs=(HSPEC, VSPEC, VSPEC, VSPEC),
        scratch_shapes=[
            pltpu.VMEM((XW, DEPTH, CY), F32),
            pltpu.VMEM((2 * RECV, 128), I32),
            pltpu.VMEM((2 * RECV, 128, 128), BF16),
            pltpu.VMEM((4, DEPTH, 128), F32),
            pltpu.VMEM((2, 128), I32),
            pltpu.SMEM((2, 128), I32),
            pltpu.SemaphoreType.DMA((2 + CX,)),
        ],
        compiler_params=pltpu.CompilerParams(vmem_limit_bytes=VMEM_LIMIT),
        name="edge_deposit",
    )(meta, pile, recv_lo, recv_hi, ucol)


def edges_kernel(cells, urow, ucol, left, right, sems):
    rows = [
        pltpu.make_async_copy(cells.at[:, x, :], urow.at[r], sems.at[r])
        for r, x in enumerate((0, 1, CX - 2, CX - 1))
    ]
    cols = [
        pltpu.make_async_copy(
            cells.at[pl.ds(z, 16), :, pl.ds(at, 128)], ref.at[pl.ds(z, 16)], sems.at[4 + n + z // 8]
        )
        for z in range(0, DEPTH, 16)
        for n, (ref, at) in enumerate(((left, 0), (right, CY - 128)))
    ]
    for copy in cols + rows:
        copy.start()
    lane = iota((CX, 128), 1)
    acc = [jnp.zeros((CX, 128), F32)] * 4
    for z in range(DEPTH):
        if z % 16 == 0:
            for copy in cols[z // 8 : z // 8 + 2]:
                copy.wait()
        for n, (ref, by) in enumerate(((left, z), (left, z + 127), (right, z + 2), (right, z + 1))):
            by = by & 127
            a = ref[z] if by == 0 else pltpu.roll(ref[z], by, 1)
            acc[n] = jnp.where(lane == z, a, acc[n])
    for n in range(4):
        ucol[n] = acc[n]
    for copy in rows:
        copy.wait()


def edges(cells):
    sd = jax.ShapeDtypeStruct
    return pl.pallas_call(
        edges_kernel,
        out_shape=(sd((4, DEPTH, CY), F32), sd((4, CX, 128), F32)),
        in_specs=[ASPEC],
        out_specs=(VSPEC, VSPEC),
        scratch_shapes=[
            pltpu.VMEM((DEPTH, CX, 128), F32),
            pltpu.VMEM((DEPTH, CX, 128), F32),
            pltpu.SemaphoreType.DMA((12,)),
        ],
        compiler_params=pltpu.CompilerParams(vmem_limit_bytes=VMEM_LIMIT),
        name="temperature_edges",
    )(cells)


def half_kappa(u, v):
    return 0.05 * (1.0 + 0.5 * jnp.tanh(u)) / (1.0 + v)


def flux(k, kn, u, un):
    return (k + kn) * (un - u)


def glow_of(rows):
    d = rows * (1.0 / BAND)
    return 0.5 * jnp.exp(-(d * d))


TILES = range(CY // 128)


def tile(c):
    return slice(128 * c, 128 * c + 128)


def load(ref, z):
    return [ref[z, :, tile(c)] for c in TILES]


def heat_planes(src, dst, vs, kz, fz, row_f, col_f, fix, glow, before, after):
    lane = iota((CX, 128), 1)
    sub = iota((CX, 128), 0)

    def both(ref, z):
        return pltpu.roll(ref[...], (128 - 2 * z) & 127, 1)

    def fetch(z):
        u = load(src, z)
        if fix is not None:
            ends = both(fix, z)
            u[0] = jnp.where(lane == 0, ends, u[0])
            u[3] = jnp.where(lane == 127, ends, u[3])
        return u

    u0 = fetch(0)
    v0 = load(vs, 0)
    for c in TILES:
        k = half_kappa(u0[c], v0[c])
        kz[:, tile(c)] = k
        fz[:, tile(c)] = (k + 0.05) * u0[c]

    def planes(z0, is_last):
        k = [kz[:, tile(c)] for c in TILES]
        down = [fz[:, tile(c)] for c in TILES]
        u = fetch(z0)
        for p in range(PLANES):
            z = z0 + p
            v = load(vs, z)
            if is_last and p == PLANES - 1:
                un, kn = u, k
                up = [(k[c] + 0.05) * (0.0 - u[c]) for c in TILES]
            else:
                un = fetch(z + 1)
                vn = load(vs, z + 1)
                kn = [half_kappa(un[c], vn[c]) for c in TILES]
                up = [flux(k[c], kn[c], u[c], un[c]) for c in TILES]
            row_first = row_f[pl.ds(z, 1), :]
            row_end = row_f[pl.ds(z + DEPTH, 1), :]
            ru = [pltpu.roll(u[c], 1, 1) for c in TILES]
            rk = [pltpu.roll(k[c], 1, 1) for c in TILES]
            ends = None if col_f is None else both(col_f, z)
            g = []
            for c in TILES:
                if c == 0:
                    f = flux(k[0], rk[0], ru[0], u[0])
                    if col_f is not None:
                        f = jnp.where(lane == 0, ends, f)
                else:
                    pu = jnp.where(lane == 0, ru[c - 1], ru[c])
                    pk = jnp.where(lane == 0, rk[c - 1], rk[c])
                    f = flux(k[c], pk, pu, u[c])
                g.append(f)
            rg = [pltpu.roll(g[c], 127, 1) for c in TILES]
            for c in TILES:
                if c < 3:
                    gn = jnp.where(lane == 127, rg[c + 1], rg[c])
                elif col_f is not None:
                    gn = jnp.where(lane == 127, ends, rg[c])
                else:
                    gn = rg[c]
                f = flux(k[c], pltpu.roll(k[c], 1, 0), pltpu.roll(u[c], 1, 0), u[c])
                f = jnp.where(sub == 0, row_first[:, tile(c)], f)
                fn = jnp.where(sub == CX - 1, row_end[:, tile(c)], pltpu.roll(f, CX - 1, 0))
                total = (up[c] - down[c]) + (fn - f) + (gn - g[c])
                dst[z, :, tile(c)] = u[c] + total + glow * v[c]
            k, down, u = kn, up, un
        for c in TILES:
            kz[:, tile(c)] = k[c]
            fz[:, tile(c)] = down[c]

    groups = DEPTH // PLANES

    def group(g, carry):
        before(g)
        planes(g * PLANES, False)
        after(g)
        return carry

    lax.fori_loop(0, groups - 1, group, 0)
    planes(DEPTH - PLANES, True)


def heat_one_kernel(meta, us, share, urow, recv_lo, recv_hi, vrow, mid, mrow, vs, kz, fz, row1, sems):
    def bring(c):
        at = pl.ds(pl.multiple_of(c * CHUNK, CHUNK), CHUNK)
        return pltpu.make_async_copy(share.at[at], vs.at[at], sems.at[c])

    for c in range(AHEAD):
        bring(c).start()
    lane_w = iota((DEPTH, CY), 1)
    sub_w = iota((DEPTH, CY), 0)
    for n in range(2):
        recv = recv_lo if n == 0 else recv_hi

        def got_row(r):
            base = 128 + r * 4 * DEPTH
            return jnp.concatenate([recv[base + c * DEPTH : base + (c + 1) * DEPTH] for c in range(4)], axis=1)

        uo, uh = (got_row(0), got_row(1)) if n == 0 else (got_row(1), got_row(0))
        ui = urow[0] if n == 0 else urow[3]
        vo, vh, vi = (vrow[0], vrow[1], vrow[2]) if n == 0 else (vrow[5], vrow[4], vrow[3])
        kh = half_kappa(uh, vh)
        ki = half_kappa(ui, vi)
        total = flux(kh, half_kappa(uo, vo), uh, uo) + flux(kh, ki, uh, ui)

        def near(a, pad):
            left = jnp.where(lane_w == 0, a, pltpu.roll(a, 1, 1))
            right = jnp.where(lane_w == CY - 1, a, pltpu.roll(a, CY - 1, 1))
            up = jnp.where(sub_w == DEPTH - 1, pad, pltpu.roll(a, DEPTH - 1, 0))
            down = jnp.where(sub_w == 0, pad, pltpu.roll(a, 1, 0))
            return left, right, up, down

        for kn, un in zip(near(kh, 0.05), near(uh, 0.0)):
            total = total + flux(kh, kn, uh, un)
        row_at = meta[0] + (-1.0 if n == 0 else float(CX))
        gl = glow_of(jnp.full((1, CY), 1.0, F32) * row_at)
        mrow[n] = uh + total + gl * vh
        row1[DEPTH * n : DEPTH * n + DEPTH] = flux(kh, ki, uh, ui) if n == 0 else flux(ki, kh, ui, uh)
    glow = glow_of(iota((CX, 128), 0).astype(F32) + meta[0])

    def before(g):
        per = CHUNK // PLANES

        @pl.when(lax.rem(g, per) == per - 1)
        def _():
            c = (g + 1) // per
            bring(c).wait()

            @pl.when(c + AHEAD - 1 < DEPTH // CHUNK)
            def _():
                bring(c + AHEAD - 1).start()

    bring(0).wait()
    heat_planes(us, mid, vs, kz, fz, row1, None, None, glow, before, lambda g: None)


def heat_one(meta, u, v, urow, recv_lo, recv_hi, vrow):
    sd = jax.ShapeDtypeStruct
    return pl.pallas_call(
        heat_one_kernel,
        out_shape=(sd((DEPTH, CX, CY), F32), sd((2, DEPTH, CY), F32), sd((DEPTH, CX, CY), F32)),
        in_specs=[SSPEC, VSPEC, HSPEC] + [VSPEC] * 4,
        out_specs=(VSPEC,) * 3,
        scratch_shapes=[
            pltpu.VMEM((CX, CY), F32), pltpu.VMEM((CX, CY), F32),
            pltpu.VMEM((2 * DEPTH, CY), F32),
            pltpu.SemaphoreType.DMA((DEPTH // CHUNK,)),
        ],
        compiler_params=pltpu.CompilerParams(vmem_limit_bytes=VMEM_LIMIT),
        cost_estimate=pl.CostEstimate(flops=1 << 25, bytes_accessed=1 << 24, transcendentals=1 << 21),
        name="heat_step_one",
    )(meta, u, v, urow, recv_lo, recv_hi, vrow)


def heat_two_kernel(
    meta, mid, vs, mpart, recv_lo, recv_hi, vrow, pay_lo, pay_hi, got_lo, got_hi, out_hbm,
    os, kz, fz, row2, fix, col2, sems,
):
    lane = iota((CX, 128), 1)
    sub = iota((CX, 128), 0)
    lo_half = lane < DEPTH
    side = jnp.where(lo_half, meta[4], meta[5])
    glow1 = glow_of(sub.astype(F32) + meta[0])

    def stacks(a, b, at, size):
        p, q = a[at : at + size], b[at : at + size]
        low = iota((size, 128), 1) < DEPTH
        return jnp.where(low, p, pltpu.roll(q, DEPTH, 1)), jnp.where(low, pltpu.roll(p, DEPTH, 1), q)

    def column_step(outer, here, inner, ends):
        (uo, vo), (uh, vh), (ui, vi), (ue, ve) = outer, here, inner, ends
        kh = half_kappa(uh, vh)
        ke = half_kappa(ue, ve)
        total = flux(kh, half_kappa(uo, vo), uh, uo) + flux(kh, half_kappa(ui, vi), uh, ui)

        def near(a, e, pad):
            below = jnp.where(sub == 0, e[0:1], pltpu.roll(a, 1, 0))
            above = jnp.where(sub == CX - 1, e[1:2], pltpu.roll(a, CX - 1, 0))
            up = jnp.where((lane & (DEPTH - 1)) == DEPTH - 1, pad, pltpu.roll(a, 127, 1))
            down = jnp.where((lane & (DEPTH - 1)) == 0, pad, pltpu.roll(a, 1, 1))
            return below, above, up, down

        for kn, un in zip(near(kh, ke, 0.05), near(uh, ue, 0.0)):
            total = total + flux(kh, kn, uh, un)
        return uh + total + glow1 * vh

    outer = stacks(got_lo, got_hi, 40, CX)
    here = stacks(got_lo, got_hi, 0, CX)
    inner = stacks(pay_lo, pay_hi, 0, CX)
    next_in = stacks(pay_lo, pay_hi, 40, CX)
    mid_out = column_step(outer, here, inner, stacks(got_lo, got_hi, CX, 8)) * side
    mid_in = column_step(here, inner, next_in, stacks(pay_lo, pay_hi, CX, 8))
    sign = jnp.where(lo_half, 1.0, -1.0)
    lane8 = iota((8, 128), 1)
    source = ((lane8 + 1) >> 1) & (DEPTH - 1)
    source = jnp.where((lane8 & 1) == 0, source, source + DEPTH)

    def weave(ref, a):
        for i in range(0, CX, 8):
            ref[i : i + 8] = jnp.take_along_axis(a[i : i + 8], source, axis=1)

    weave(fix, mid_in)
    weave(col2, sign * flux(half_kappa(mid_out, here[1]), half_kappa(mid_in, inner[1]), mid_out, mid_in))

    tail = [jnp.transpose(jnp.concatenate([g[CX : CX + 8]] * 16, axis=0)) for g in (got_lo, got_hi)]
    ends = jnp.transpose(jnp.concatenate([mid_in] * 4, axis=0))
    lane_t = iota((DEPTH, 128), 1)

    def turned(a, by):
        return pltpu.roll(a, by & 127, 1) if by & 127 else a

    for n in range(2):
        x = 0 if n == 0 else CX - 1
        recv, r, vh = (recv_lo, 1, vrow[1]) if n == 0 else (recv_hi, 0, vrow[4])
        mh = [mpart[n, :, tile(c)] for c in TILES]
        mi = [mid[:, x, tile(c)] for c in TILES]
        for c, at, half, g, e in ((0, 0, 0, 0, 0), (3, 127, DEPTH, 1, 127)):
            base = 128 + (r * 4 + c) * DEPTH
            uc = recv[base : base + DEPTH]
            kc = half_kappa(uc, vh[:, tile(c)])
            ue = turned(tail[g][:DEPTH], e - n)
            ke = half_kappa(ue, turned(tail[g][DEPTH:], e - n))
            mh[c] = mh[c] + jnp.where(lane_t == at, flux(kc, ke, uc, ue), 0.0)
            mi[c] = jnp.where(lane_t == at, turned(ends[half : half + DEPTH], e - x), mi[c])
        vi = vrow[2] if n == 0 else vrow[3]
        for c in TILES:
            m = mh[c] * meta[2 + n]
            kh = half_kappa(m, vh[:, tile(c)])
            ki = half_kappa(mi[c], vi[:, tile(c)])
            row2[DEPTH * n : DEPTH * n + DEPTH, tile(c)] = flux(kh, ki, m, mi[c]) if n == 0 else flux(ki, kh, mi[c], m)

    per = 8 // PLANES

    def store(c):
        at = pl.ds(pl.multiple_of(c * 8, 8), 8)
        return pltpu.make_async_copy(os.at[at], out_hbm.at[at], sems.at[c])

    def after(g):
        @pl.when(lax.rem(g, per) == per - 1)
        def _():
            store(g // per).start()

    glow = glow_of(sub.astype(F32) + meta[1])
    heat_planes(mid, os, vs, kz, fz, row2, col2, fix, glow, lambda g: None, after)
    store(DEPTH // 8 - 1).start()
    for c in range(DEPTH // 8):
        store(c).wait()


def heat_two(meta, mid, v, mpart, recv_lo, recv_hi, vrow, pay_lo, pay_hi, got_lo, got_hi):
    return pl.pallas_call(
        heat_two_kernel,
        out_shape=jax.ShapeDtypeStruct((DEPTH, CX, CY), F32),
        in_specs=[SSPEC] + [VSPEC] * 10,
        out_specs=ASPEC,
        scratch_shapes=[
            pltpu.VMEM((DEPTH, CX, CY), F32),
            pltpu.VMEM((CX, CY), F32), pltpu.VMEM((CX, CY), F32),
            pltpu.VMEM((2 * DEPTH, CY), F32),
            pltpu.VMEM((CX, 128), F32), pltpu.VMEM((CX, 128), F32),
            pltpu.SemaphoreType.DMA((DEPTH // 8,)),
        ],
        compiler_params=pltpu.CompilerParams(vmem_limit_bytes=VMEM_LIMIT),
        name="heat_step_two",
    )(meta, mid, v, mpart, recv_lo, recv_hi, vrow, pay_lo, pay_hi, got_lo, got_hi)


def shift(value, axis, steps):
    count = lax.axis_size(axis)
    first, stop = max(0, -steps), min(count, count - steps)
    return lax.ppermute(value, axis, [(i, i + steps) for i in range(first, stop)])


def body(
    particle_locations,
    particle_speeds,
    particle_bulk,
    receiving_group_per_pair,
    emitting_group_per_pair,
    active_pair_slots,
    landing_site_triple,
    landing_weight_octants,
    thermal_excess,
    molten_strip_midlines,
):
    states = jnp.concatenate([particle_locations, particle_speeds], axis=0)
    width = HB * 128
    halo_lo = shift(states[:, NPART - width :], ("gx", "gy"), 1)
    halo_hi = shift(states[:, :width], ("gx", "gy"), -1)
    urow, ucol = edges(pltpu.with_memory_space_constraint(thermal_excess, pltpu.HBM))

    gx, gy = lax.axis_index("gx"), lax.axis_index("gy")
    row_start, col_start = gx * CX, gy * CY
    beam = row_start - molten_strip_midlines
    inside = jnp.stack([gx > 0, gx < lax.axis_size("gx") - 1, gy > 0, gy < lax.axis_size("gy") - 1])
    meta = jnp.concatenate([beam.astype(F32), inside.astype(F32)])
    origin = jnp.stack([row_start - G, col_start])

    nloc, nvel, skey, schg, last, send_lo, send_hi = particles(
        receiving_group_per_pair, emitting_group_per_pair, active_pair_slots, origin,
        particle_locations, particle_speeds, halo_lo, halo_hi, landing_site_triple,
        particle_bulk.reshape(128, 128), landing_weight_octants.reshape(128, 128), urow,
    )
    recv_lo = shift(send_hi, "gx", 1)
    recv_hi = shift(send_lo, "gx", -1)
    pile = own_deposit(last.reshape(128), last, skey, schg)
    share, vrow, pay_lo, pay_hi = edge_deposit(meta, pile, recv_lo, recv_hi, ucol)
    got_lo = shift(pay_hi, "gy", 1)
    got_hi = shift(pay_lo, "gy", -1)
    mid, mpart, here = heat_one(meta, thermal_excess, pltpu.with_memory_space_constraint(share, pltpu.HBM), urow, recv_lo, recv_hi, vrow)
    final = heat_two(meta, mid, here, mpart, recv_lo, recv_hi, vrow, pay_lo, pay_hi, got_lo, got_hi)
    return nloc, nvel, share, final


def solution(mesh):
    placed = (
        P(None, ("gx", "gy")),
        P(None, ("gx", "gy")),
        P(("gx", "gy")),
        P(("gx", "gy")),
        P(("gx", "gy")),
        P(("gx", "gy")),
        P(None, ("gx", "gy")),
        P(("gx", "gy")),
        P(None, "gx", "gy"),
        P(),
    )
    return jax.shard_map(
        body,
        mesh=mesh,
        in_specs=placed,
        out_specs=(
            P(None, ("gx", "gy")),
            P(None, ("gx", "gy")),
            P(None, "gx", "gy"),
            P(None, "gx", "gy"),
        ),
        check_vma=False,
    )
```

```python
import math

import jax
import jax.numpy as jnp
from jax import lax
from jax.experimental import pallas as pl
from jax.experimental.pallas import tpu as pltpu
from jax.sharding import PartitionSpec as P

F32 = jnp.float32
BF16 = jnp.bfloat16
I32 = jnp.int32

DEPTH = 64
CX = 32
CY = 512
NPART = 16384
G = 16
HB = 2
NB = 128
NEXT = NB + 2 * HB
SLOTS = 256
BAND = 64.0
BIN = 256
LOG2E = 1.4426950408889634
VMEM_LIMIT = 30 * 1024 * 1024
TILE_UNROLL = 64
WALK_UNROLL = 32
ROW_UNROLL = 16
PLANES = 8
CHUNK = 8
AHEAD = 8
XW = CX + 4
BINS = 2 * XW
PART = 128 + 8 * DEPTH
SEND = PART + 8 * DEPTH + 8

VSPEC = pl.BlockSpec(memory_space=pltpu.VMEM)
SSPEC = pl.BlockSpec(memory_space=pltpu.SMEM)
ASPEC = pl.BlockSpec(memory_space=pl.ANY)
HSPEC = pl.BlockSpec(memory_space=pltpu.HBM)


def iota(shape, dim):
    return lax.broadcasted_iota(I32, shape, dim)


def cross_stage(ks, cs, step, axis):
    at = iota((8, 128), axis)
    other = at ^ step
    low = (at & step) == 0
    nk, nc = [], []
    for k, c in zip(ks, cs):
        pk = jnp.take_along_axis(k, other, axis=axis)
        pc = jnp.take_along_axis(c, other, axis=axis)
        m = jnp.where(low, jnp.minimum(k, pk), jnp.maximum(k, pk))
        nk.append(m)
        nc.append(jnp.where(m != k, pc, c))
    return nk, nc


def vreg_stage(ks, cs, j, descending):
    ks, cs = list(ks), list(cs)
    for r in range(16):
        if r & (1 << j):
            continue
        a, b = r, r | (1 << j)
        if descending(r):
            a, b = b, a
        less = ks[b] < ks[a]
        ks[a], ks[b] = jnp.minimum(ks[a], ks[b]), jnp.maximum(ks[a], ks[b])
        cs[a], cs[b] = jnp.where(less, cs[b], cs[a]), jnp.where(less, cs[a], cs[b])
    return ks, cs


def bitonic(ks, cs):
    sub = iota((8, 128), 0)
    lane = iota((8, 128), 1)
    up = lambda r: False

    def low_stages(ks, cs, top):
        for j in range(top, 3, -1):
            step = 1 << (j - 4)
            ks, cs = cross_stage(ks, cs, step, 0)
        for j in range(min(top, 3), -1, -1):
            ks, cs = vreg_stage(ks, cs, j, up)
        return ks, cs

    for k in range(1, 4):
        for j in range(k - 1, -1, -1):
            ks, cs = vreg_stage(ks, cs, j, lambda r: bool(r & (1 << k)))
    for k in range(4, 7):
        flip = -((sub >> (k - 4)) & 1)
        ks = [a ^ flip for a in ks]
        ks, cs = low_stages(ks, cs, k - 1)
        ks = [a ^ flip for a in ks]

    def phase(k, carry):
        ks, cs = list(carry[:16]), list(carry[16:])
        flip = -((lane >> (k - 7)) & 1)
        ks = [a ^ flip for a in ks]

        def lane_step(t, inner):
            step = jnp.left_shift(jnp.int32(1), k - 8 - t)
            nk, nc = cross_stage(list(inner[:16]), list(inner[16:]), step, 1)
            return tuple(nk) + tuple(nc)

        out = lax.fori_loop(0, k - 7, lane_step, tuple(ks) + tuple(cs))
        ks, cs = low_stages(list(out[:16]), list(out[16:]), 6)
        ks = [a ^ flip for a in ks]
        return tuple(ks) + tuple(cs)

    out = lax.fori_loop(7, 15, phase, tuple(ks) + tuple(cs))
    return list(out[:16]), list(out[16:])


OWN, RECV = 128, 32


def profile(z, charge):
    level = iota((DEPTH, 128), 0).astype(F32)
    d = (level - z) * (math.sqrt(LOG2E) / 12.0)
    p = jnp.exp2(-(d * d)) * charge
    hi = p.astype(BF16)
    lo = (p - hi.astype(F32)).astype(BF16)
    return jnp.concatenate([hi, lo], axis=0)


def count_below(bins, limit):
    return jnp.sum(jnp.where(bins < limit, 1.0, 0.0)).astype(I32)


def walk(pile, cells, prof, count, bins, last_bin, first_bin, end_bin, origin, unroll):
    spot = iota((BIN, 128), 0).astype(F32).astype(BF16)
    one, zero = jnp.ones((), BF16), jnp.zeros((), BF16)
    start = count_below(bins, float(first_bin))
    stop = jnp.minimum(count_below(bins, float(end_bin + 1)), count - 1)
    steps = stop - start + 1 + (end_bin - first_bin)

    def step(g, state):
        i, j = state
        work = []
        for u in range(unroll):
            inside = i <= stop
            ii = jnp.minimum(i, count - 1)
            work.append((ii, jnp.where(inside, j * BIN, -(1 << 20)), j - origin))
            more = jnp.logical_and(last_bin(ii) > j, j < end_bin)
            j = jnp.where(more, j + 1, j)
            i = jnp.where(more, i, jnp.minimum(i + 1, count))
        outs = []
        for ii, first, home in work:
            col = cells(ii) - first
            col = jnp.where(jnp.logical_and(col >= 0, col < BIN), col, 300).astype(F32).astype(BF16)
            hot = jnp.where(spot == col, one, zero)
            out = lax.dot_general(prof(ii), hot, (((1,), (1,)), ((), ())), preferred_element_type=F32)
            outs.append(out[:DEPTH] + out[DEPTH:])
        for (ii, first, home), out in zip(work, outs):
            x, at = home >> 1, pl.ds(pl.multiple_of((home & 1) * BIN, BIN), BIN)
            pile[x, :, at] = pile[x, :, at] + out
        return i, j

    @pl.when(start <= stop)
    def _():
        lax.fori_loop(0, (steps + unroll - 1) // unroll, step, (start, jnp.int32(first_bin)))


def split3(a):
    h1 = a.astype(BF16)
    r = a - h1.astype(F32)
    h2 = r.astype(BF16)
    h3 = (r - h2.astype(F32)).astype(BF16)
    return h1, h2, h3


def particle_kernel(
    tgt, src, cnt, origin, loc, vel, halo_lo, halo_hi, site, bulk, octants, urow,
    nloc, nvel, skey, schg, last, send_lo, send_hi,
    left, right, stat, acc, zrow, key, last_v, last_s, rows, sem,
):
    wide = 4 * 128

    def prepare(x3, v3, at, width):
        pad = jnp.zeros((5, width), F32)
        x = jnp.concatenate([x3, pad], axis=0)
        v = jnp.concatenate([v3, pad], axis=0)
        row = iota((8, width), 0)
        xs = x * math.sqrt(LOG2E)
        q = 0.5 * jnp.sum(xs * xs, axis=0, keepdims=True)
        full = jnp.where(row < 3, xs, jnp.where(row < 5, q, 0.0))
        h = [p.astype(F32) for p in split3(full)]

        def mix(a, b, is_target):
            base = h[a]
            if b is None:
                return jnp.where(row < 3, base, 0.0)
            if is_target:
                return jnp.where(row < 3, base, jnp.where(row == 3, h[b], jnp.where(row == 4, 1.0, 0.0)))
            return jnp.where(row < 3, base, jnp.where(row == 3, -1.0, jnp.where(row == 4, -h[b], 0.0)))

        extra = [0, 1, 2, None, None, None]
        ta = [0, 0, 1, 1, 0, 2]
        sa = [0, 1, 0, 1, 2, 0]
        for p in range(0, 6, 2):
            lt = jnp.concatenate([mix(ta[p], extra[p], True), mix(ta[p + 1], extra[p + 1], True)], axis=0)
            rt = jnp.concatenate([mix(sa[p], extra[p], False), mix(sa[p + 1], extra[p + 1], False)], axis=0)
            left[pl.ds(8 * p, 16), pl.ds(at, width)] = lt.astype(BF16)
            right[pl.ds(8 * p, 16), pl.ds(at, width)] = rt.astype(BF16)
        w = (2.0 * x - v) * (1.0 / 256.0)
        wh = w.astype(BF16).astype(F32)
        wl = w - wh
        w2 = jnp.concatenate([jnp.where(row == 3, 1.0, wh), wl], axis=0)
        stat[:, pl.ds(at, width)] = w2.astype(BF16)

    prepare(halo_lo[0:3, :], halo_lo[3:6, :], 0, HB * 128)
    prepare(halo_hi[0:3, :], halo_hi[3:6, :], (NB + HB) * 128, HB * 128)

    def prep(i, carry):
        at = pl.multiple_of(i * wide, wide)
        prepare(loc[:, pl.ds(at, wide)], vel[:, pl.ds(at, wide)], pl.multiple_of(at + HB * 128, 128), wide)
        return carry

    lax.fori_loop(0, NPART // wide, prep, 0)
    acc[...] = jnp.zeros_like(acc)
    live = cnt[0]

    def tiles(g, carry):
        outs = []
        for u in range(TILE_UNROLL):
            t = g * TILE_UNROLL + u
            a = tgt[t] & (NB - 1)
            b = a + (src[t] - tgt[t]) + HB
            lm = left[:, pl.ds(pl.multiple_of((a + HB) * 128, 128), 128)]
            rm = right[:, pl.ds(pl.multiple_of(b * 128, 128), 128)]
            arg = lax.dot_general(rm, lm, (((0,), (0,)), ((), ())), preferred_element_type=F32)
            g_mn = jnp.exp2(arg)
            gh = g_mn.astype(BF16)
            gl = (g_mn - gh.astype(F32)).astype(BF16)
            s = stat[:, pl.ds(pl.multiple_of(b * 128, 128), 128)]
            out = jnp.dot(
                jnp.concatenate([s, s], axis=1),
                jnp.concatenate([gh, gl], axis=0),
                preferred_element_type=F32,
            )
            home = jnp.where(t < live, a, NB)
            outs.append((home, out[0:8] + out[8:16]))
        for home, out in outs:
            at = pl.multiple_of(home * 8, 8)
            acc[pl.ds(at, 8), :] = acc[pl.ds(at, 8), :] + out
        return carry

    lax.fori_loop(0, (live + TILE_UNROLL - 1) // TILE_UNROLL, tiles, 0)

    def advance(i, carry):
        for u in range(8):
            b = i * 8 + u
            at = pl.multiple_of(b * 128, 128)
            x = loc[:, pl.ds(at, 128)]
            v = vel[:, pl.ds(at, 128)]
            f = acc[pl.ds(pl.multiple_of(b * 8, 8), 8), :]
            w = (2.0 * x - v) * (1.0 / 256.0)
            force = w * f[3:4] - f[0:3]
            nv = v + 0.5 * force
            nx = x + 0.5 * nv
            nvel[:, pl.ds(at, 128)] = nv
            nloc[:, pl.ds(at, 128)] = nx
            zrow[pl.ds(b, 1), :] = nx[2:3]
            p = site[:, pl.ds(at, 128)]
            cell = (p[1:2] - origin[0]) * CY + (p[2:3] - origin[1])
            key[pl.ds(b, 1), :] = cell * DEPTH + p[0:1]
        return carry

    lax.fori_loop(0, NB // 8, advance, 0)

    charge = bulk[...] * octants[...].astype(F32) * 0.125 * (1.0 + 0.5 * jnp.tanh(zrow[...]))
    keys = key[...]
    ks = [keys[8 * r : 8 * r + 8] for r in range(16)]
    cs = [charge[8 * r : 8 * r + 8] for r in range(16)]
    ks, cs = bitonic(ks, cs)
    last[...] = ks[15][7:8]
    last_v[...] = ks[15]
    lasts = pltpu.make_async_copy(last_v, last_s, sem.at[0])
    lasts.start()
    kt = jnp.concatenate(ks, axis=0)
    ct = jnp.concatenate(cs, axis=0)
    kt = jnp.transpose(kt)
    ct = jnp.transpose(ct)
    skey[...] = kt
    schg[...] = ct
    for ref, at in ((send_lo, 0), (send_hi, 96)):
        kk = kt[at : at + 32]
        ref[0:32] = (kk >> 15).astype(F32)
        ref[32:64] = ((kk >> 6) & 511).astype(F32)
        ref[64:96] = (kk & 63).astype(F32)
        ref[96:128] = ct[at : at + 32]
    for r in range(4):
        ref = send_lo if r < 2 else send_hi
        for c in range(4):
            at = 128 + ((r % 2) * 4 + c) * DEPTH
            ref[at : at + DEPTH] = urow[r, :, 128 * c : 128 * c + 128]
    rows[...] = jnp.zeros_like(rows)
    lasts.wait()

    def cells(i):
        return skey[pl.ds(i, 1), :] >> 6

    def prof(i):
        return profile((skey[pl.ds(i, 1), :] & 63).astype(F32), schg[pl.ds(i, 1), :])

    for n, x in enumerate((G, G + CX - 2)):
        walk(
            rows, cells, prof, OWN, (ks[15][7:8] >> 14).astype(F32), lambda i: last_s[7, i] >> 14,
            2 * x, 2 * x + 3, 2 * x - 4 * n, ROW_UNROLL,
        )
    for r in range(4):
        ref = send_lo if r < 2 else send_hi
        for c in range(4):
            at = PART + ((r % 2) * 4 + c) * DEPTH
            ref[at : at + DEPTH] = rows[r, :, 128 * c : 128 * c + 128]
    for ref in (send_lo, send_hi):
        ref[SEND - 8 : SEND] = jnp.broadcast_to(last[...].astype(F32), (8, 128))


def particles(tgt, src, cnt, origin, loc, vel, halo_lo, halo_hi, site, bulk, octants, urow):
    sd = jax.ShapeDtypeStruct
    return pl.pallas_call(
        particle_kernel,
        out_shape=(
            sd((3, NPART), F32), sd((3, NPART), F32),
            sd((128, 128), I32), sd((128, 128), F32), sd((1, 128), I32),
            sd((SEND, 128), F32), sd((SEND, 128), F32),
        ),
        in_specs=[SSPEC] * 4 + [VSPEC] * 8,
        out_specs=(VSPEC,) * 7,
        scratch_shapes=[
            pltpu.VMEM((48, NEXT * 128), BF16),
            pltpu.VMEM((48, NEXT * 128), BF16),
            pltpu.VMEM((16, NEXT * 128), BF16),
            pltpu.VMEM(((NB + 1) * 8, 128), F32),
            pltpu.VMEM((NB, 128), F32),
            pltpu.VMEM((NB, 128), I32),
            pltpu.VMEM((8, 128), I32),
            pltpu.SMEM((8, 128), I32),
            pltpu.VMEM((4, DEPTH, CY), F32),
            pltpu.SemaphoreType.DMA((1,)),
        ],
        compiler_params=pltpu.CompilerParams(vmem_limit_bytes=VMEM_LIMIT),
        name="particle_step",
    )(tgt, src, cnt, origin, loc, vel, halo_lo, halo_hi, site, bulk, octants, urow)


def own_deposit_kernel(last, last_v, skey, schg, pile, cells, prof):
    own = skey[...]
    cells[0:OWN] = (own >> 6) - (G - HB) * CY

    def profiles(i, carry):
        for u in range(8):
            b = i * 8 + u
            z = (skey[pl.ds(b, 1), :] & 63).astype(F32)
            prof[b] = profile(z, schg[pl.ds(b, 1), :])
        return carry

    lax.fori_loop(0, OWN // 8, profiles, 0)

    def clear(i, carry):
        pile[i] = jnp.zeros((DEPTH, CY), F32)
        return carry

    lax.fori_loop(0, XW, clear, 0)
    walk(
        pile, lambda i: cells[pl.ds(i, 1), :], lambda i: prof[i], OWN,
        ((last_v[...] >> 14) - 2 * (G - HB)).astype(F32),
        lambda i: (last[i] >> 14) - 2 * (G - HB), 0, BINS - 1, 0, WALK_UNROLL,
    )


def own_deposit(last, last_v, skey, schg):
    sd = jax.ShapeDtypeStruct
    return pl.pallas_call(
        own_deposit_kernel,
        out_shape=sd((XW, DEPTH, CY), F32),
        in_specs=[SSPEC, VSPEC, VSPEC, VSPEC],
        out_specs=VSPEC,
        scratch_shapes=[
            pltpu.VMEM((OWN, 128), I32),
            pltpu.VMEM((OWN, 128, 128), BF16),
        ],
        compiler_params=pltpu.CompilerParams(vmem_limit_bytes=VMEM_LIMIT),
        name="own_deposit",
    )(last, last_v, skey, schg)


def edge_deposit_kernel(
    meta, pile_in, recv_lo, recv_hi, ucol,
    share, vrow, pay_lo, pay_hi,
    pile, cells, prof, packs, last_v, last_s, sems,
):
    load = pltpu.make_async_copy(pile_in, pile, sems.at[0])
    load.start()
    last_v[0:1] = recv_lo[SEND - 8 : SEND - 7].astype(I32)
    last_v[1:2] = recv_hi[SEND - 8 : SEND - 7].astype(I32)
    lasts = pltpu.make_async_copy(last_v, last_s, sems.at[1])
    lasts.start()
    for ref, at, shift in ((recv_lo, 0, HB - G - CX), (recv_hi, RECV, HB + CX - G)):
        x = ref[0:32].astype(I32) + shift
        cells[at : at + RECV] = x * CY + ref[32:64].astype(I32)

    def profiles(i, carry):
        for ref, at in ((recv_lo, 0), (recv_hi, RECV)):
            for u in range(4):
                b = i * 4 + u
                prof[at + b] = profile(ref[pl.ds(64 + b, 1), :], ref[pl.ds(96 + b, 1), :])
        return carry

    lax.fori_loop(0, RECV // 4, profiles, 0)
    lasts.wait()
    load.wait()
    half = 2 * (2 + G)
    slot = iota((1, 128), 1)
    for n, (at, by, first, end) in enumerate((
        (OWN - RECV, HB - G - CX, 4, half - 1), (0, HB + CX - G, half, 2 * (2 + CX) - 1),
    )):
        sent = jnp.logical_and(slot >= at, slot < at + RECV)
        bins = jnp.where(sent, (last_v[n : n + 1] >> 14) + 2 * by, 4 * BINS).astype(F32)
        walk(
            pile, lambda i: cells[pl.ds(n * RECV + i, 1), :], lambda i: prof[n * RECV + i], RECV, bins,
            lambda i: (last_s[n, at + i] >> 14) + 2 * by, first, end, 0, WALK_UNROLL,
        )

    def turn(x):
        return pltpu.make_async_copy(pile.at[x + HB], share.at[:, x, :], sems.at[2 + x])

    def turn_start(x, carry):
        turn(x).start()
        return carry

    lax.fori_loop(0, CX, turn_start, 0)
    for ref, x0, flag in ((recv_lo, 0, meta[2]), (recv_hi, CX + 2, meta[3])):
        for r in range(2):
            for c in range(4):
                at = PART + (r * 4 + c) * DEPTH
                cols = slice(128 * c, 128 * c + 128)
                pile[x0 + r, :, cols] = flag * (pile[x0 + r, :, cols] + ref[at : at + DEPTH])
    for n, x in enumerate((0, 1, 2, CX + 1, CX + 2, CX + 3)):
        vrow[n] = pile[x]
    lane = iota((DEPTH, 128), 1)
    packs[...] = jnp.zeros_like(packs)

    def pick(row, at):
        a = pile[row, :, 0:128]
        b = pile[row, :, 384:512]
        for n, (t, by) in enumerate(((a, at), (a, at + 127), (b, at + 2), (b, at + 1))):
            packs[n] = jnp.where(lane == at, pltpu.roll(t, by & 127, 1), packs[n])

    def picks(x, carry):
        pick(x + 2, x)
        return carry

    lax.fori_loop(0, CX, picks, 0, unroll=4)
    pick(1, CX)
    pick(CX + 2, CX + 1)
    base = 128 + 4 * DEPTH
    for pay, recv_col, near, far in ((pay_lo, 0, 0, 1), (pay_hi, 3, 3, 2)):
        lo = recv_lo[base + recv_col * DEPTH : base + recv_col * DEPTH + DEPTH]
        hi = recv_hi[128 + recv_col * DEPTH : 128 + recv_col * DEPTH + DEPTH]
        by = 0 if recv_col == 0 else 1
        corner = jnp.where(lane == CX, pltpu.roll(lo, CX + by, 1), 0.0)
        corner = jnp.where(lane == CX + 1, pltpu.roll(hi, CX + 1 + by, 1), corner)
        t = jnp.transpose(jnp.concatenate([corner, packs[near]], axis=0))
        pay[0:CX] = t[0:CX] + ucol[near]
        pay[CX : CX + 8] = t[CX : CX + 8]
        t = jnp.transpose(jnp.concatenate([jnp.zeros((DEPTH, 128), F32), packs[far]], axis=0))
        pay[40 : 40 + CX] = t[0:CX] + ucol[far]
        pay[40 + CX : 80] = jnp.zeros((8, 128), F32)

    def turn_wait(x, carry):
        turn(x).wait()
        return carry

    lax.fori_loop(0, CX, turn_wait, 0)


def edge_deposit(meta, pile, recv_lo, recv_hi, ucol):
    sd = jax.ShapeDtypeStruct
    return pl.pallas_call(
        edge_deposit_kernel,
        out_shape=(
            sd((DEPTH, CX, CY), F32), sd((6, DEPTH, CY), F32),
            sd((80, 128), F32), sd((80, 128), F32),
        ),
        in_specs=[SSPEC, ASPEC] + [VSPEC] * 3,
        out_specs=(HSPEC, VSPEC, VSPEC, VSPEC),
        scratch_shapes=[
            pltpu.VMEM((XW, DEPTH, CY), F32),
            pltpu.VMEM((2 * RECV, 128), I32),
            pltpu.VMEM((2 * RECV, 128, 128), BF16),
            pltpu.VMEM((4, DEPTH, 128), F32),
            pltpu.VMEM((2, 128), I32),
            pltpu.SMEM((2, 128), I32),
            pltpu.SemaphoreType.DMA((2 + CX,)),
        ],
        compiler_params=pltpu.CompilerParams(vmem_limit_bytes=VMEM_LIMIT),
        name="edge_deposit",
    )(meta, pile, recv_lo, recv_hi, ucol)


def edges_kernel(cells, urow, ucol, left, right, sems):
    rows = [
        pltpu.make_async_copy(cells.at[:, x, :], urow.at[r], sems.at[r])
        for r, x in enumerate((0, 1, CX - 2, CX - 1))
    ]
    cols = [
        pltpu.make_async_copy(
            cells.at[pl.ds(z, 16), :, pl.ds(at, 128)], ref.at[pl.ds(z, 16)], sems.at[4 + n + z // 8]
        )
        for z in range(0, DEPTH, 16)
        for n, (ref, at) in enumerate(((left, 0), (right, CY - 128)))
    ]
    for copy in cols + rows:
        copy.start()
    lane = iota((CX, 128), 1)
    acc = [jnp.zeros((CX, 128), F32)] * 4
    for z in range(DEPTH):
        if z % 16 == 0:
            for copy in cols[z // 8 : z // 8 + 2]:
                copy.wait()
        for n, (ref, by) in enumerate(((left, z), (left, z + 127), (right, z + 2), (right, z + 1))):
            by = by & 127
            a = ref[z] if by == 0 else pltpu.roll(ref[z], by, 1)
            acc[n] = jnp.where(lane == z, a, acc[n])
    for n in range(4):
        ucol[n] = acc[n]
    for copy in rows:
        copy.wait()


def edges(cells):
    sd = jax.ShapeDtypeStruct
    return pl.pallas_call(
        edges_kernel,
        out_shape=(sd((4, DEPTH, CY), F32), sd((4, CX, 128), F32)),
        in_specs=[ASPEC],
        out_specs=(VSPEC, VSPEC),
        scratch_shapes=[
            pltpu.VMEM((DEPTH, CX, 128), F32),
            pltpu.VMEM((DEPTH, CX, 128), F32),
            pltpu.SemaphoreType.DMA((12,)),
        ],
        compiler_params=pltpu.CompilerParams(vmem_limit_bytes=VMEM_LIMIT),
        name="temperature_edges",
    )(cells)


def half_kappa(u, v):
    return 0.05 * (1.0 + 0.5 * jnp.tanh(u)) / (1.0 + v)


def flux(k, kn, u, un):
    return (k + kn) * (un - u)


def glow_of(rows):
    d = rows * (1.0 / BAND)
    return 0.5 * jnp.exp(-(d * d))


TILES = range(CY // 128)


def tile(c):
    return slice(128 * c, 128 * c + 128)


def load(ref, z):
    return [ref[z, :, tile(c)] for c in TILES]


def heat_planes(src, dst, vs, kz, fz, row_f, col_f, fix, glow, before, after):
    lane = iota((CX, 128), 1)
    sub = iota((CX, 128), 0)

    def both(ref, z):
        return pltpu.roll(ref[...], (128 - 2 * z) & 127, 1)

    def fetch(z):
        u = load(src, z)
        if fix is not None:
            ends = both(fix, z)
            u[0] = jnp.where(lane == 0, ends, u[0])
            u[3] = jnp.where(lane == 127, ends, u[3])
        return u

    u0 = fetch(0)
    v0 = load(vs, 0)
    for c in TILES:
        k = half_kappa(u0[c], v0[c])
        kz[:, tile(c)] = k
        fz[:, tile(c)] = (k + 0.05) * u0[c]

    def planes(z0, is_last):
        k = [kz[:, tile(c)] for c in TILES]
        down = [fz[:, tile(c)] for c in TILES]
        u = fetch(z0)
        for p in range(PLANES):
            z = z0 + p
            v = load(vs, z)
            if is_last and p == PLANES - 1:
                un, kn = u, k
                up = [(k[c] + 0.05) * (0.0 - u[c]) for c in TILES]
            else:
                un = fetch(z + 1)
                vn = load(vs, z + 1)
                kn = [half_kappa(un[c], vn[c]) for c in TILES]
                up = [flux(k[c], kn[c], u[c], un[c]) for c in TILES]
            row_first = row_f[pl.ds(z, 1), :]
            row_end = row_f[pl.ds(z + DEPTH, 1), :]
            ru = [pltpu.roll(u[c], 1, 1) for c in TILES]
            rk = [pltpu.roll(k[c], 1, 1) for c in TILES]
            ends = None if col_f is None else both(col_f, z)
            g = []
            for c in TILES:
                if c == 0:
                    f = flux(k[0], rk[0], ru[0], u[0])
                    if col_f is not None:
                        f = jnp.where(lane == 0, ends, f)
                else:
                    pu = jnp.where(lane == 0, ru[c - 1], ru[c])
                    pk = jnp.where(lane == 0, rk[c - 1], rk[c])
                    f = flux(k[c], pk, pu, u[c])
                g.append(f)
            rg = [pltpu.roll(g[c], 127, 1) for c in TILES]
            for c in TILES:
                if c < 3:
                    gn = jnp.where(lane == 127, rg[c + 1], rg[c])
                elif col_f is not None:
                    gn = jnp.where(lane == 127, ends, rg[c])
                else:
                    gn = rg[c]
                f = flux(k[c], pltpu.roll(k[c], 1, 0), pltpu.roll(u[c], 1, 0), u[c])
                f = jnp.where(sub == 0, row_first[:, tile(c)], f)
                fn = jnp.where(sub == CX - 1, row_end[:, tile(c)], pltpu.roll(f, CX - 1, 0))
                total = (up[c] - down[c]) + (fn - f) + (gn - g[c])
                dst[z, :, tile(c)] = u[c] + total + glow * v[c]
            k, down, u = kn, up, un
        for c in TILES:
            kz[:, tile(c)] = k[c]
            fz[:, tile(c)] = down[c]

    groups = DEPTH // PLANES

    def group(g, carry):
        before(g)
        planes(g * PLANES, False)
        after(g)
        return carry

    lax.fori_loop(0, groups - 1, group, 0)
    planes(DEPTH - PLANES, True)


def heat_one_kernel(meta, us, share, urow, recv_lo, recv_hi, vrow, mid, mrow, vs, kz, fz, row1, sems):
    def bring(c):
        at = pl.ds(pl.multiple_of(c * CHUNK, CHUNK), CHUNK)
        return pltpu.make_async_copy(share.at[at], vs.at[at], sems.at[c])

    for c in range(AHEAD):
        bring(c).start()
    lane_w = iota((DEPTH, CY), 1)
    sub_w = iota((DEPTH, CY), 0)
    for n in range(2):
        recv = recv_lo if n == 0 else recv_hi

        def got_row(r):
            base = 128 + r * 4 * DEPTH
            return jnp.concatenate([recv[base + c * DEPTH : base + (c + 1) * DEPTH] for c in range(4)], axis=1)

        uo, uh = (got_row(0), got_row(1)) if n == 0 else (got_row(1), got_row(0))
        ui = urow[0] if n == 0 else urow[3]
        vo, vh, vi = (vrow[0], vrow[1], vrow[2]) if n == 0 else (vrow[5], vrow[4], vrow[3])
        kh = half_kappa(uh, vh)
        ki = half_kappa(ui, vi)
        total = flux(kh, half_kappa(uo, vo), uh, uo) + flux(kh, ki, uh, ui)

        def near(a, pad):
            left = jnp.where(lane_w == 0, a, pltpu.roll(a, 1, 1))
            right = jnp.where(lane_w == CY - 1, a, pltpu.roll(a, CY - 1, 1))
            up = jnp.where(sub_w == DEPTH - 1, pad, pltpu.roll(a, DEPTH - 1, 0))
            down = jnp.where(sub_w == 0, pad, pltpu.roll(a, 1, 0))
            return left, right, up, down

        for kn, un in zip(near(kh, 0.05), near(uh, 0.0)):
            total = total + flux(kh, kn, uh, un)
        row_at = meta[0] + (-1.0 if n == 0 else float(CX))
        gl = glow_of(jnp.full((1, CY), 1.0, F32) * row_at)
        mrow[n] = uh + total + gl * vh
        row1[DEPTH * n : DEPTH * n + DEPTH] = flux(kh, ki, uh, ui) if n == 0 else flux(ki, kh, ui, uh)
    glow = glow_of(iota((CX, 128), 0).astype(F32) + meta[0])

    def before(g):
        per = CHUNK // PLANES

        @pl.when(lax.rem(g, per) == per - 1)
        def _():
            c = (g + 1) // per
            bring(c).wait()

            @pl.when(c + AHEAD - 1 < DEPTH // CHUNK)
            def _():
                bring(c + AHEAD - 1).start()

    bring(0).wait()
    heat_planes(us, mid, vs, kz, fz, row1, None, None, glow, before, lambda g: None)


def heat_one(meta, u, v, urow, recv_lo, recv_hi, vrow):
    sd = jax.ShapeDtypeStruct
    return pl.pallas_call(
        heat_one_kernel,
        out_shape=(sd((DEPTH, CX, CY), F32), sd((2, DEPTH, CY), F32), sd((DEPTH, CX, CY), F32)),
        in_specs=[SSPEC, VSPEC, HSPEC] + [VSPEC] * 4,
        out_specs=(VSPEC,) * 3,
        scratch_shapes=[
            pltpu.VMEM((CX, CY), F32), pltpu.VMEM((CX, CY), F32),
            pltpu.VMEM((2 * DEPTH, CY), F32),
            pltpu.SemaphoreType.DMA((DEPTH // CHUNK,)),
        ],
        compiler_params=pltpu.CompilerParams(vmem_limit_bytes=VMEM_LIMIT),
        cost_estimate=pl.CostEstimate(flops=1 << 25, bytes_accessed=1 << 24, transcendentals=1 << 21),
        name="heat_step_one",
    )(meta, u, v, urow, recv_lo, recv_hi, vrow)


def heat_two_kernel(
    meta, mid, vs, mpart, recv_lo, recv_hi, vrow, pay_lo, pay_hi, got_lo, got_hi, out_hbm,
    os, kz, fz, row2, fix, col2, sems,
):
    lane = iota((CX, 128), 1)
    sub = iota((CX, 128), 0)
    lo_half = lane < DEPTH
    side = jnp.where(lo_half, meta[4], meta[5])
    glow1 = glow_of(sub.astype(F32) + meta[0])

    def stacks(a, b, at, size, fa=1.0, fb=1.0):
        p, q = a[at : at + size] * fa, b[at : at + size] * fb
        low = iota((size, 128), 1) < DEPTH
        return jnp.where(low, p, pltpu.roll(q, DEPTH, 1)), jnp.where(low, pltpu.roll(p, DEPTH, 1), q)

    def column_step(outer, here, inner, ends):
        (uo, vo), (uh, vh), (ui, vi), (ue, ve) = outer, here, inner, ends
        kh = half_kappa(uh, vh)
        ke = half_kappa(ue, ve)
        total = flux(kh, half_kappa(uo, vo), uh, uo) + flux(kh, half_kappa(ui, vi), uh, ui)

        def near(a, e, pad):
            below = jnp.where(sub == 0, e[0:1], pltpu.roll(a, 1, 0))
            above = jnp.where(sub == CX - 1, e[1:2], pltpu.roll(a, CX - 1, 0))
            up = jnp.where((lane & (DEPTH - 1)) == DEPTH - 1, pad, pltpu.roll(a, 127, 1))
            down = jnp.where((lane & (DEPTH - 1)) == 0, pad, pltpu.roll(a, 1, 1))
            return below, above, up, down

        for kn, un in zip(near(kh, ke, 0.05), near(uh, ue, 0.0)):
            total = total + flux(kh, kn, uh, un)
        return uh + total + glow1 * vh

    outer = stacks(got_lo, got_hi, 40, CX, meta[4], meta[5])
    here = stacks(got_lo, got_hi, 0, CX, meta[4], meta[5])
    inner = stacks(pay_lo, pay_hi, 0, CX)
    next_in = stacks(pay_lo, pay_hi, 40, CX)
    mid_out = column_step(outer, here, inner, stacks(got_lo, got_hi, CX, 8, meta[4], meta[5])) * side
    mid_in = column_step(here, inner, next_in, stacks(pay_lo, pay_hi, CX, 8))
    sign = jnp.where(lo_half, 1.0, -1.0)
    lane8 = iota((8, 128), 1)
    source = ((lane8 + 1) >> 1) & (DEPTH - 1)
    source = jnp.where((lane8 & 1) == 0, source, source + DEPTH)

    def weave(ref, a):
        for i in range(0, CX, 8):
            ref[i : i + 8] = jnp.take_along_axis(a[i : i + 8], source, axis=1)

    weave(fix, mid_in)
    weave(col2, sign * flux(half_kappa(mid_out, here[1]), half_kappa(mid_in, inner[1]), mid_out, mid_in))

    tail = [
        jnp.transpose(jnp.concatenate([g[CX : CX + 8] * meta[4 + i]] * 16, axis=0))
        for i, g in enumerate((got_lo, got_hi))
    ]
    ends = jnp.transpose(jnp.concatenate([mid_in] * 4, axis=0))
    lane_t = iota((DEPTH, 128), 1)

    def turned(a, by):
        return pltpu.roll(a, by & 127, 1) if by & 127 else a

    for n in range(2):
        x = 0 if n == 0 else CX - 1
        recv, r, vh = (recv_lo, 1, vrow[1]) if n == 0 else (recv_hi, 0, vrow[4])
        mh = [mpart[n, :, tile(c)] for c in TILES]
        mi = [mid[:, x, tile(c)] for c in TILES]
        for c, at, half, g, e in ((0, 0, 0, 0, 0), (3, 127, DEPTH, 1, 127)):
            base = 128 + (r * 4 + c) * DEPTH
            uc = recv[base : base + DEPTH]
            kc = half_kappa(uc, vh[:, tile(c)])
            ue = turned(tail[g][:DEPTH], e - n)
            ke = half_kappa(ue, turned(tail[g][DEPTH:], e - n))
            mh[c] = mh[c] + jnp.where(lane_t == at, flux(kc, ke, uc, ue), 0.0)
            mi[c] = jnp.where(lane_t == at, turned(ends[half : half + DEPTH], e - x), mi[c])
        vi = vrow[2] if n == 0 else vrow[3]
        for c in TILES:
            m = mh[c] * meta[2 + n]
            kh = half_kappa(m, vh[:, tile(c)])
            ki = half_kappa(mi[c], vi[:, tile(c)])
            row2[DEPTH * n : DEPTH * n + DEPTH, tile(c)] = flux(kh, ki, m, mi[c]) if n == 0 else flux(ki, kh, mi[c], m)

    per = 8 // PLANES

    def store(c):
        at = pl.ds(pl.multiple_of(c * 8, 8), 8)
        return pltpu.make_async_copy(os.at[at], out_hbm.at[at], sems.at[c])

    def after(g):
        @pl.when(lax.rem(g, per) == per - 1)
        def _():
            store(g // per).start()

    glow = glow_of(sub.astype(F32) + meta[1])
    heat_planes(mid, os, vs, kz, fz, row2, col2, fix, glow, lambda g: None, after)
    store(DEPTH // 8 - 1).start()
    for c in range(DEPTH // 8):
        store(c).wait()


def heat_two(meta, mid, v, mpart, recv_lo, recv_hi, vrow, pay_lo, pay_hi, got_lo, got_hi):
    return pl.pallas_call(
        heat_two_kernel,
        out_shape=jax.ShapeDtypeStruct((DEPTH, CX, CY), F32),
        in_specs=[SSPEC] + [VSPEC] * 10,
        out_specs=ASPEC,
        scratch_shapes=[
            pltpu.VMEM((DEPTH, CX, CY), F32),
            pltpu.VMEM((CX, CY), F32), pltpu.VMEM((CX, CY), F32),
            pltpu.VMEM((2 * DEPTH, CY), F32),
            pltpu.VMEM((CX, 128), F32), pltpu.VMEM((CX, 128), F32),
            pltpu.SemaphoreType.DMA((DEPTH // 8,)),
        ],
        compiler_params=pltpu.CompilerParams(vmem_limit_bytes=VMEM_LIMIT),
        name="heat_step_two",
    )(meta, mid, v, mpart, recv_lo, recv_hi, vrow, pay_lo, pay_hi, got_lo, got_hi)


def shift(value, axis, steps):
    count = lax.axis_size(axis)
    first, stop = max(0, -steps), min(count, count - steps)
    return lax.ppermute(value, axis, [(i, i + steps) for i in range(first, stop)])


def ring(value, axis, steps):
    count = lax.axis_size(axis)
    return lax.ppermute(value, axis, [(i, (i + steps) % count) for i in range(count)])


def body(
    particle_locations,
    particle_speeds,
    particle_bulk,
    receiving_group_per_pair,
    emitting_group_per_pair,
    active_pair_slots,
    landing_site_triple,
    landing_weight_octants,
    thermal_excess,
    molten_strip_midlines,
):
    states = jnp.concatenate([particle_locations, particle_speeds], axis=0)
    width = HB * 128
    halo_lo = ring(states[:, NPART - width :], ("gx", "gy"), 1)
    halo_hi = ring(states[:, :width], ("gx", "gy"), -1)
    urow, ucol = edges(pltpu.with_memory_space_constraint(thermal_excess, pltpu.HBM))

    gx, gy = lax.axis_index("gx"), lax.axis_index("gy")
    row_start, col_start = gx * CX, gy * CY
    beam = row_start - molten_strip_midlines
    inside = jnp.stack([gx > 0, gx < lax.axis_size("gx") - 1, gy > 0, gy < lax.axis_size("gy") - 1])
    meta = jnp.concatenate([beam.astype(F32), inside.astype(F32)])
    origin = jnp.stack([row_start - G, col_start])

    nloc, nvel, skey, schg, last, send_lo, send_hi = particles(
        receiving_group_per_pair, emitting_group_per_pair, active_pair_slots, origin,
        particle_locations, particle_speeds, halo_lo, halo_hi, landing_site_triple,
        particle_bulk.reshape(128, 128), landing_weight_octants.reshape(128, 128), urow,
    )
    recv_lo = shift(send_hi, "gx", 1)
    recv_hi = shift(send_lo, "gx", -1)
    pile = own_deposit(last.reshape(128), last, skey, schg)
    share, vrow, pay_lo, pay_hi = edge_deposit(meta, pile, recv_lo, recv_hi, ucol)
    got_lo = ring(pay_hi, "gy", 1)
    got_hi = ring(pay_lo, "gy", -1)
    mid, mpart, here = heat_one(meta, thermal_excess, pltpu.with_memory_space_constraint(share, pltpu.HBM), urow, recv_lo, recv_hi, vrow)
    final = heat_two(meta, mid, here, mpart, recv_lo, recv_hi, vrow, pay_lo, pay_hi, got_lo, got_hi)
    return nloc, nvel, share, final


def solution(mesh):
    placed = (
        P(None, ("gx", "gy")),
        P(None, ("gx", "gy")),
        P(("gx", "gy")),
        P(("gx", "gy")),
        P(("gx", "gy")),
        P(("gx", "gy")),
        P(None, ("gx", "gy")),
        P(("gx", "gy")),
        P(None, "gx", "gy"),
        P(),
    )
    return jax.shard_map(
        body,
        mesh=mesh,
        in_specs=placed,
        out_specs=(
            P(None, ("gx", "gy")),
            P(None, ("gx", "gy")),
            P(None, "gx", "gy"),
            P(None, "gx", "gy"),
        ),
        check_vma=False,
    )
```

```python
import math

import jax
import jax.numpy as jnp
from jax import lax
from jax.experimental import pallas as pl
from jax.experimental.pallas import tpu as pltpu
from jax.sharding import PartitionSpec as P

F32 = jnp.float32
BF16 = jnp.bfloat16
I32 = jnp.int32

DEPTH = 64
CX = 32
CY = 512
NPART = 16384
G = 16
HB = 2
NB = 128
NEXT = NB + 2 * HB
SLOTS = 256
BAND = 64.0
BIN = 256
LOG2E = 1.4426950408889634
VMEM_LIMIT = 30 * 1024 * 1024
TILE_UNROLL = 64
WALK_UNROLL = 32
ROW_UNROLL = 16
PLANES = 8
CHUNK = 8
AHEAD = 8
XW = CX + 4
BINS = 2 * XW
PART = 128 + 8 * DEPTH
SEND = PART + 8 * DEPTH + 8

VSPEC = pl.BlockSpec(memory_space=pltpu.VMEM)
SSPEC = pl.BlockSpec(memory_space=pltpu.SMEM)
ASPEC = pl.BlockSpec(memory_space=pl.ANY)
HSPEC = pl.BlockSpec(memory_space=pltpu.HBM)


def iota(shape, dim):
    return lax.broadcasted_iota(I32, shape, dim)


def cross_stage(ks, cs, step, axis):
    at = iota((8, 128), axis)
    other = at ^ step
    low = (at & step) == 0
    nk, nc = [], []
    for k, c in zip(ks, cs):
        pk = jnp.take_along_axis(k, other, axis=axis)
        pc = jnp.take_along_axis(c, other, axis=axis)
        m = jnp.where(low, jnp.minimum(k, pk), jnp.maximum(k, pk))
        nk.append(m)
        nc.append(jnp.where(m != k, pc, c))
    return nk, nc


def vreg_stage(ks, cs, j, descending):
    ks, cs = list(ks), list(cs)
    for r in range(16):
        if r & (1 << j):
            continue
        a, b = r, r | (1 << j)
        if descending(r):
            a, b = b, a
        less = ks[b] < ks[a]
        ks[a], ks[b] = jnp.minimum(ks[a], ks[b]), jnp.maximum(ks[a], ks[b])
        cs[a], cs[b] = jnp.where(less, cs[b], cs[a]), jnp.where(less, cs[a], cs[b])
    return ks, cs


def bitonic(ks, cs):
    sub = iota((8, 128), 0)
    lane = iota((8, 128), 1)
    up = lambda r: False

    def low_stages(ks, cs, top):
        for j in range(top, 3, -1):
            step = 1 << (j - 4)
            ks, cs = cross_stage(ks, cs, step, 0)
        for j in range(min(top, 3), -1, -1):
            ks, cs = vreg_stage(ks, cs, j, up)
        return ks, cs

    for k in range(1, 4):
        for j in range(k - 1, -1, -1):
            ks, cs = vreg_stage(ks, cs, j, lambda r: bool(r & (1 << k)))
    for k in range(4, 7):
        flip = -((sub >> (k - 4)) & 1)
        ks = [a ^ flip for a in ks]
        ks, cs = low_stages(ks, cs, k - 1)
        ks = [a ^ flip for a in ks]

    def phase(k, carry):
        ks, cs = list(carry[:16]), list(carry[16:])
        flip = -((lane >> (k - 7)) & 1)
        ks = [a ^ flip for a in ks]

        def lane_step(t, inner):
            step = jnp.left_shift(jnp.int32(1), k - 8 - t)
            nk, nc = cross_stage(list(inner[:16]), list(inner[16:]), step, 1)
            return tuple(nk) + tuple(nc)

        out = lax.fori_loop(0, k - 7, lane_step, tuple(ks) + tuple(cs))
        ks, cs = low_stages(list(out[:16]), list(out[16:]), 6)
        ks = [a ^ flip for a in ks]
        return tuple(ks) + tuple(cs)

    out = lax.fori_loop(7, 15, phase, tuple(ks) + tuple(cs))
    return list(out[:16]), list(out[16:])


OWN, RECV = 128, 32


def profile(z, charge):
    level = iota((DEPTH, 128), 0).astype(F32)
    d = (level - z) * (math.sqrt(LOG2E) / 12.0)
    p = jnp.exp2(-(d * d)) * charge
    hi = p.astype(BF16)
    lo = (p - hi.astype(F32)).astype(BF16)
    return jnp.concatenate([hi, lo], axis=0)


def count_below(bins, limit):
    return jnp.sum(jnp.where(bins < limit, 1.0, 0.0)).astype(I32)


def walk(pile, cells, prof, count, bins, last_bin, first_bin, end_bin, origin, unroll):
    spot = iota((BIN, 128), 0).astype(F32).astype(BF16)
    one, zero = jnp.ones((), BF16), jnp.zeros((), BF16)
    start = count_below(bins, float(first_bin))
    stop = jnp.minimum(count_below(bins, float(end_bin + 1)), count - 1)
    steps = stop - start + 1 + (end_bin - first_bin)

    def step(g, state):
        i, j = state
        work = []
        for u in range(unroll):
            inside = i <= stop
            ii = jnp.minimum(i, count - 1)
            work.append((ii, jnp.where(inside, j * BIN, -(1 << 20)), j - origin))
            more = jnp.logical_and(last_bin(ii) > j, j < end_bin)
            j = jnp.where(more, j + 1, j)
            i = jnp.where(more, i, jnp.minimum(i + 1, count))
        outs = []
        for ii, first, home in work:
            col = cells(ii) - first
            col = jnp.where(jnp.logical_and(col >= 0, col < BIN), col, 300).astype(F32).astype(BF16)
            hot = jnp.where(spot == col, one, zero)
            out = lax.dot_general(prof(ii), hot, (((1,), (1,)), ((), ())), preferred_element_type=F32)
            outs.append(out[:DEPTH] + out[DEPTH:])
        for (ii, first, home), out in zip(work, outs):
            x, at = home >> 1, pl.ds(pl.multiple_of((home & 1) * BIN, BIN), BIN)
            pile[x, :, at] = pile[x, :, at] + out
        return i, j

    @pl.when(start <= stop)
    def _():
        lax.fori_loop(0, (steps + unroll - 1) // unroll, step, (start, jnp.int32(first_bin)))


def split3(a):
    h1 = a.astype(BF16)
    r = a - h1.astype(F32)
    h2 = r.astype(BF16)
    h3 = (r - h2.astype(F32)).astype(BF16)
    return h1, h2, h3


def particle_kernel(
    tgt, src, cnt, origin, loc, vel, halo_lo, halo_hi, site, bulk, octants, urow,
    nloc, nvel, skey, schg, last, send_lo, send_hi,
    left, right, stat, acc, zrow, key, last_v, last_s, rows, sem,
):
    wide = 4 * 128

    def prepare(x3, v3, at, width):
        pad = jnp.zeros((5, width), F32)
        x = jnp.concatenate([x3, pad], axis=0)
        v = jnp.concatenate([v3, pad], axis=0)
        row = iota((8, width), 0)
        xs = x * math.sqrt(LOG2E)
        q = 0.5 * jnp.sum(xs * xs, axis=0, keepdims=True)
        full = jnp.where(row < 3, xs, jnp.where(row < 5, q, 0.0))
        h = [p.astype(F32) for p in split3(full)]

        def mix(a, b, is_target):
            base = h[a]
            if b is None:
                return jnp.where(row < 3, base, 0.0)
            if is_target:
                return jnp.where(row < 3, base, jnp.where(row == 3, h[b], jnp.where(row == 4, 1.0, 0.0)))
            return jnp.where(row < 3, base, jnp.where(row == 3, -1.0, jnp.where(row == 4, -h[b], 0.0)))

        extra = [0, 1, 2, None, None, None]
        ta = [0, 0, 1, 1, 0, 2]
        sa = [0, 1, 0, 1, 2, 0]
        for p in range(0, 6, 2):
            lt = jnp.concatenate([mix(ta[p], extra[p], True), mix(ta[p + 1], extra[p + 1], True)], axis=0)
            rt = jnp.concatenate([mix(sa[p], extra[p], False), mix(sa[p + 1], extra[p + 1], False)], axis=0)
            left[pl.ds(8 * p, 16), pl.ds(at, width)] = lt.astype(BF16)
            right[pl.ds(8 * p, 16), pl.ds(at, width)] = rt.astype(BF16)
        w = (2.0 * x - v) * (1.0 / 256.0)
        wh = w.astype(BF16).astype(F32)
        wl = w - wh
        w2 = jnp.concatenate([jnp.where(row == 3, 1.0, wh), wl], axis=0)
        stat[:, pl.ds(at, width)] = w2.astype(BF16)

    prepare(halo_lo[0:3, :], halo_lo[3:6, :], 0, HB * 128)
    prepare(halo_hi[0:3, :], halo_hi[3:6, :], (NB + HB) * 128, HB * 128)

    def prep(i, carry):
        at = pl.multiple_of(i * wide, wide)
        prepare(loc[:, pl.ds(at, wide)], vel[:, pl.ds(at, wide)], pl.multiple_of(at + HB * 128, 128), wide)
        return carry

    lax.fori_loop(0, NPART // wide, prep, 0)
    acc[...] = jnp.zeros_like(acc)
    live = cnt[0]

    def tiles(g, carry):
        outs = []
        for u in range(TILE_UNROLL):
            t = g * TILE_UNROLL + u
            a = tgt[t] & (NB - 1)
            b = a + (src[t] - tgt[t]) + HB
            lm = left[:, pl.ds(pl.multiple_of((a + HB) * 128, 128), 128)]
            rm = right[:, pl.ds(pl.multiple_of(b * 128, 128), 128)]
            arg = lax.dot_general(rm, lm, (((0,), (0,)), ((), ())), preferred_element_type=F32)
            g_mn = jnp.exp2(arg)
            gh = g_mn.astype(BF16)
            gl = (g_mn - gh.astype(F32)).astype(BF16)
            s = stat[:, pl.ds(pl.multiple_of(b * 128, 128), 128)]
            out = jnp.dot(
                jnp.concatenate([s, s], axis=1),
                jnp.concatenate([gh, gl], axis=0),
                preferred_element_type=F32,
            )
            home = jnp.where(t < live, a, NB)
            outs.append((home, out[0:8] + out[8:16]))
        for home, out in outs:
            at = pl.multiple_of(home * 8, 8)
            acc[pl.ds(at, 8), :] = acc[pl.ds(at, 8), :] + out
        return carry

    lax.fori_loop(0, (live + TILE_UNROLL - 1) // TILE_UNROLL, tiles, 0)

    def advance(i, carry):
        for u in range(8):
            b = i * 8 + u
            at = pl.multiple_of(b * 128, 128)
            x = loc[:, pl.ds(at, 128)]
            v = vel[:, pl.ds(at, 128)]
            f = acc[pl.ds(pl.multiple_of(b * 8, 8), 8), :]
            w = (2.0 * x - v) * (1.0 / 256.0)
            force = w * f[3:4] - f[0:3]
            nv = v + 0.5 * force
            nx = x + 0.5 * nv
            nvel[:, pl.ds(at, 128)] = nv
            nloc[:, pl.ds(at, 128)] = nx
            zrow[pl.ds(b, 1), :] = nx[2:3]
            p = site[:, pl.ds(at, 128)]
            cell = (p[1:2] - origin[0]) * CY + (p[2:3] - origin[1])
            key[pl.ds(b, 1), :] = cell * DEPTH + p[0:1]
        return carry

    lax.fori_loop(0, NB // 8, advance, 0)

    charge = bulk[...] * octants[...].astype(F32) * 0.125 * (1.0 + 0.5 * jnp.tanh(zrow[...]))
    keys = key[...]
    ks = [keys[8 * r : 8 * r + 8] for r in range(16)]
    cs = [charge[8 * r : 8 * r + 8] for r in range(16)]
    ks, cs = bitonic(ks, cs)
    last[...] = ks[15][7:8]
    last_v[...] = ks[15]
    lasts = pltpu.make_async_copy(last_v, last_s, sem.at[0])
    lasts.start()
    kt = jnp.concatenate(ks, axis=0)
    ct = jnp.concatenate(cs, axis=0)
    kt = jnp.transpose(kt)
    ct = jnp.transpose(ct)
    skey[...] = kt
    schg[...] = ct
    for ref, at in ((send_lo, 0), (send_hi, 96)):
        kk = kt[at : at + 32]
        ref[0:32] = (kk >> 15).astype(F32)
        ref[32:64] = ((kk >> 6) & 511).astype(F32)
        ref[64:96] = (kk & 63).astype(F32)
        ref[96:128] = ct[at : at + 32]
    for r in range(4):
        ref = send_lo if r < 2 else send_hi
        for c in range(4):
            at = 128 + ((r % 2) * 4 + c) * DEPTH
            ref[at : at + DEPTH] = urow[r, :, 128 * c : 128 * c + 128]
    rows[...] = jnp.zeros_like(rows)
    lasts.wait()

    def cells(i):
        return skey[pl.ds(i, 1), :] >> 6

    def prof(i):
        return profile((skey[pl.ds(i, 1), :] & 63).astype(F32), schg[pl.ds(i, 1), :])

    for n, x in enumerate((G, G + CX - 2)):
        walk(
            rows, cells, prof, OWN, (ks[15][7:8] >> 14).astype(F32), lambda i: last_s[7, i] >> 14,
            2 * x, 2 * x + 3, 2 * x - 4 * n, ROW_UNROLL,
        )
    for r in range(4):
        ref = send_lo if r < 2 else send_hi
        for c in range(4):
            at = PART + ((r % 2) * 4 + c) * DEPTH
            ref[at : at + DEPTH] = rows[r, :, 128 * c : 128 * c + 128]
    for ref in (send_lo, send_hi):
        ref[SEND - 8 : SEND] = jnp.broadcast_to(last[...].astype(F32), (8, 128))


def particles(tgt, src, cnt, origin, loc, vel, halo_lo, halo_hi, site, bulk, octants, urow):
    sd = jax.ShapeDtypeStruct
    return pl.pallas_call(
        particle_kernel,
        out_shape=(
            sd((3, NPART), F32), sd((3, NPART), F32),
            sd((128, 128), I32), sd((128, 128), F32), sd((1, 128), I32),
            sd((SEND, 128), F32), sd((SEND, 128), F32),
        ),
        in_specs=[SSPEC] * 4 + [VSPEC] * 8,
        out_specs=(VSPEC,) * 7,
        scratch_shapes=[
            pltpu.VMEM((48, NEXT * 128), BF16),
            pltpu.VMEM((48, NEXT * 128), BF16),
            pltpu.VMEM((16, NEXT * 128), BF16),
            pltpu.VMEM(((NB + 1) * 8, 128), F32),
            pltpu.VMEM((NB, 128), F32),
            pltpu.VMEM((NB, 128), I32),
            pltpu.VMEM((8, 128), I32),
            pltpu.SMEM((8, 128), I32),
            pltpu.VMEM((4, DEPTH, CY), F32),
            pltpu.SemaphoreType.DMA((1,)),
        ],
        compiler_params=pltpu.CompilerParams(vmem_limit_bytes=VMEM_LIMIT),
        name="particle_step",
    )(tgt, src, cnt, origin, loc, vel, halo_lo, halo_hi, site, bulk, octants, urow)


def own_deposit_kernel(last, last_v, skey, schg, pile, cells, prof):
    own = skey[...]
    cells[0:OWN] = (own >> 6) - (G - HB) * CY

    def profiles(i, carry):
        for u in range(8):
            b = i * 8 + u
            z = (skey[pl.ds(b, 1), :] & 63).astype(F32)
            prof[b] = profile(z, schg[pl.ds(b, 1), :])
        return carry

    lax.fori_loop(0, OWN // 8, profiles, 0)

    def clear(i, carry):
        pile[i] = jnp.zeros((DEPTH, CY), F32)
        return carry

    lax.fori_loop(0, XW, clear, 0)
    walk(
        pile, lambda i: cells[pl.ds(i, 1), :], lambda i: prof[i], OWN,
        ((last_v[...] >> 14) - 2 * (G - HB)).astype(F32),
        lambda i: (last[i] >> 14) - 2 * (G - HB), 0, BINS - 1, 0, WALK_UNROLL,
    )


def own_deposit(last, last_v, skey, schg):
    sd = jax.ShapeDtypeStruct
    return pl.pallas_call(
        own_deposit_kernel,
        out_shape=sd((XW, DEPTH, CY), F32),
        in_specs=[SSPEC, VSPEC, VSPEC, VSPEC],
        out_specs=VSPEC,
        scratch_shapes=[
            pltpu.VMEM((OWN, 128), I32),
            pltpu.VMEM((OWN, 128, 128), BF16),
        ],
        compiler_params=pltpu.CompilerParams(vmem_limit_bytes=VMEM_LIMIT),
        name="own_deposit",
    )(last, last_v, skey, schg)


def edge_deposit_kernel(
    meta, pile_in, recv_lo, recv_hi, ucol,
    share, vrow, pay_lo, pay_hi,
    pile, cells, prof, packs, last_v, last_s, sems,
):
    load = pltpu.make_async_copy(pile_in, pile, sems.at[0])
    load.start()
    last_v[0:1] = recv_lo[SEND - 8 : SEND - 7].astype(I32)
    last_v[1:2] = recv_hi[SEND - 8 : SEND - 7].astype(I32)
    lasts = pltpu.make_async_copy(last_v, last_s, sems.at[1])
    lasts.start()
    for ref, at, shift in ((recv_lo, 0, HB - G - CX), (recv_hi, RECV, HB + CX - G)):
        x = ref[0:32].astype(I32) + shift
        cells[at : at + RECV] = x * CY + ref[32:64].astype(I32)

    def profiles(i, carry):
        for ref, at, flag in ((recv_lo, 0, meta[2]), (recv_hi, RECV, meta[3])):
            for u in range(4):
                b = i * 4 + u
                prof[at + b] = profile(ref[pl.ds(64 + b, 1), :], flag * ref[pl.ds(96 + b, 1), :])
        return carry

    lax.fori_loop(0, RECV // 4, profiles, 0)
    lasts.wait()
    load.wait()
    half = 2 * (2 + G)
    slot = iota((1, 128), 1)
    for n, (at, by, first, end) in enumerate((
        (OWN - RECV, HB - G - CX, 4, half - 1), (0, HB + CX - G, half, 2 * (2 + CX) - 1),
    )):
        sent = jnp.logical_and(slot >= at, slot < at + RECV)
        bins = jnp.where(sent, (last_v[n : n + 1] >> 14) + 2 * by, 4 * BINS).astype(F32)
        walk(
            pile, lambda i: cells[pl.ds(n * RECV + i, 1), :], lambda i: prof[n * RECV + i], RECV, bins,
            lambda i: (last_s[n, at + i] >> 14) + 2 * by, first, end, 0, WALK_UNROLL,
        )

    def turn(x):
        return pltpu.make_async_copy(pile.at[x + HB], share.at[:, x, :], sems.at[2 + x])

    def turn_start(x, carry):
        turn(x).start()
        return carry

    lax.fori_loop(0, CX, turn_start, 0)
    for ref, x0, flag in ((recv_lo, 0, meta[2]), (recv_hi, CX + 2, meta[3])):
        for r in range(2):
            for c in range(4):
                at = PART + (r * 4 + c) * DEPTH
                cols = slice(128 * c, 128 * c + 128)
                pile[x0 + r, :, cols] = flag * (pile[x0 + r, :, cols] + ref[at : at + DEPTH])
    for n, x in enumerate((0, 1, 2, CX + 1, CX + 2, CX + 3)):
        vrow[n] = pile[x]
    lane = iota((DEPTH, 128), 1)
    packs[...] = jnp.zeros_like(packs)

    def pick(row, at):
        a = pile[row, :, 0:128]
        b = pile[row, :, 384:512]
        for n, (t, by) in enumerate(((a, at), (a, at + 127), (b, at + 2), (b, at + 1))):
            packs[n] = jnp.where(lane == at, pltpu.roll(t, by & 127, 1), packs[n])

    def picks(x, carry):
        pick(x + 2, x)
        return carry

    lax.fori_loop(0, CX, picks, 0, unroll=4)
    pick(1, CX)
    pick(CX + 2, CX + 1)
    base = 128 + 4 * DEPTH
    for pay, recv_col, near, far in ((pay_lo, 0, 0, 1), (pay_hi, 3, 3, 2)):
        lo = meta[2] * recv_lo[base + recv_col * DEPTH : base + recv_col * DEPTH + DEPTH]
        hi = meta[3] * recv_hi[128 + recv_col * DEPTH : 128 + recv_col * DEPTH + DEPTH]
        by = 0 if recv_col == 0 else 1
        corner = jnp.where(lane == CX, pltpu.roll(lo, CX + by, 1), 0.0)
        corner = jnp.where(lane == CX + 1, pltpu.roll(hi, CX + 1 + by, 1), corner)
        t = jnp.transpose(jnp.concatenate([corner, packs[near]], axis=0))
        pay[0:CX] = t[0:CX] + ucol[near]
        pay[CX : CX + 8] = t[CX : CX + 8]
        t = jnp.transpose(jnp.concatenate([jnp.zeros((DEPTH, 128), F32), packs[far]], axis=0))
        pay[40 : 40 + CX] = t[0:CX] + ucol[far]
        pay[40 + CX : 80] = jnp.zeros((8, 128), F32)

    def turn_wait(x, carry):
        turn(x).wait()
        return carry

    lax.fori_loop(0, CX, turn_wait, 0)


def edge_deposit(meta, pile, recv_lo, recv_hi, ucol):
    sd = jax.ShapeDtypeStruct
    return pl.pallas_call(
        edge_deposit_kernel,
        out_shape=(
            sd((DEPTH, CX, CY), F32), sd((6, DEPTH, CY), F32),
            sd((80, 128), F32), sd((80, 128), F32),
        ),
        in_specs=[SSPEC, ASPEC] + [VSPEC] * 3,
        out_specs=(HSPEC, VSPEC, VSPEC, VSPEC),
        scratch_shapes=[
            pltpu.VMEM((XW, DEPTH, CY), F32),
            pltpu.VMEM((2 * RECV, 128), I32),
            pltpu.VMEM((2 * RECV, 128, 128), BF16),
            pltpu.VMEM((4, DEPTH, 128), F32),
            pltpu.VMEM((2, 128), I32),
            pltpu.SMEM((2, 128), I32),
            pltpu.SemaphoreType.DMA((2 + CX,)),
        ],
        compiler_params=pltpu.CompilerParams(vmem_limit_bytes=VMEM_LIMIT),
        name="edge_deposit",
    )(meta, pile, recv_lo, recv_hi, ucol)


def edges_kernel(cells, urow, ucol, left, right, sems):
    rows = [
        pltpu.make_async_copy(cells.at[:, x, :], urow.at[r], sems.at[r])
        for r, x in enumerate((0, 1, CX - 2, CX - 1))
    ]
    cols = [
        pltpu.make_async_copy(
            cells.at[pl.ds(z, 16), :, pl.ds(at, 128)], ref.at[pl.ds(z, 16)], sems.at[4 + n + z // 8]
        )
        for z in range(0, DEPTH, 16)
        for n, (ref, at) in enumerate(((left, 0), (right, CY - 128)))
    ]
    for copy in cols + rows:
        copy.start()
    lane = iota((CX, 128), 1)
    acc = [jnp.zeros((CX, 128), F32)] * 4
    for z in range(DEPTH):
        if z % 16 == 0:
            for copy in cols[z // 8 : z // 8 + 2]:
                copy.wait()
        for n, (ref, by) in enumerate(((left, z), (left, z + 127), (right, z + 2), (right, z + 1))):
            by = by & 127
            a = ref[z] if by == 0 else pltpu.roll(ref[z], by, 1)
            acc[n] = jnp.where(lane == z, a, acc[n])
    for n in range(4):
        ucol[n] = acc[n]
    for copy in rows:
        copy.wait()


def edges(cells):
    sd = jax.ShapeDtypeStruct
    return pl.pallas_call(
        edges_kernel,
        out_shape=(sd((4, DEPTH, CY), F32), sd((4, CX, 128), F32)),
        in_specs=[ASPEC],
        out_specs=(VSPEC, VSPEC),
        scratch_shapes=[
            pltpu.VMEM((DEPTH, CX, 128), F32),
            pltpu.VMEM((DEPTH, CX, 128), F32),
            pltpu.SemaphoreType.DMA((12,)),
        ],
        compiler_params=pltpu.CompilerParams(vmem_limit_bytes=VMEM_LIMIT),
        name="temperature_edges",
    )(cells)


def half_kappa(u, v):
    return 0.05 * (1.0 + 0.5 * jnp.tanh(u)) / (1.0 + v)


def flux(k, kn, u, un):
    return (k + kn) * (un - u)


def glow_of(rows):
    d = rows * (1.0 / BAND)
    return 0.5 * jnp.exp(-(d * d))


TILES = range(CY // 128)


def tile(c):
    return slice(128 * c, 128 * c + 128)


def load(ref, z):
    return [ref[z, :, tile(c)] for c in TILES]


def heat_planes(src, dst, vs, kz, fz, row_f, col_f, fix, glow, before, after):
    lane = iota((CX, 128), 1)
    sub = iota((CX, 128), 0)

    def both(ref, z):
        return pltpu.roll(ref[...], (128 - 2 * z) & 127, 1)

    def fetch(z):
        u = load(src, z)
        if fix is not None:
            ends = both(fix, z)
            u[0] = jnp.where(lane == 0, ends, u[0])
            u[3] = jnp.where(lane == 127, ends, u[3])
        return u

    u0 = fetch(0)
    v0 = load(vs, 0)
    for c in TILES:
        k = half_kappa(u0[c], v0[c])
        kz[:, tile(c)] = k
        fz[:, tile(c)] = (k + 0.05) * u0[c]

    def planes(z0, is_last):
        k = [kz[:, tile(c)] for c in TILES]
        down = [fz[:, tile(c)] for c in TILES]
        u = fetch(z0)
        for p in range(PLANES):
            z = z0 + p
            v = load(vs, z)
            if is_last and p == PLANES - 1:
                un, kn = u, k
                up = [(k[c] + 0.05) * (0.0 - u[c]) for c in TILES]
            else:
                un = fetch(z + 1)
                vn = load(vs, z + 1)
                kn = [half_kappa(un[c], vn[c]) for c in TILES]
                up = [flux(k[c], kn[c], u[c], un[c]) for c in TILES]
            row_first = row_f[pl.ds(z, 1), :]
            row_end = row_f[pl.ds(z + DEPTH, 1), :]
            ru = [pltpu.roll(u[c], 1, 1) for c in TILES]
            rk = [pltpu.roll(k[c], 1, 1) for c in TILES]
            ends = None if col_f is None else both(col_f, z)
            g = []
            for c in TILES:
                if c == 0:
                    f = flux(k[0], rk[0], ru[0], u[0])
                    if col_f is not None:
                        f = jnp.where(lane == 0, ends, f)
                else:
                    pu = jnp.where(lane == 0, ru[c - 1], ru[c])
                    pk = jnp.where(lane == 0, rk[c - 1], rk[c])
                    f = flux(k[c], pk, pu, u[c])
                g.append(f)
            rg = [pltpu.roll(g[c], 127, 1) for c in TILES]
            for c in TILES:
                if c < 3:
                    gn = jnp.where(lane == 127, rg[c + 1], rg[c])
                elif col_f is not None:
                    gn = jnp.where(lane == 127, ends, rg[c])
                else:
                    gn = rg[c]
                f = flux(k[c], pltpu.roll(k[c], 1, 0), pltpu.roll(u[c], 1, 0), u[c])
                f = jnp.where(sub == 0, row_first[:, tile(c)], f)
                fn = jnp.where(sub == CX - 1, row_end[:, tile(c)], pltpu.roll(f, CX - 1, 0))
                total = (up[c] - down[c]) + (fn - f) + (gn - g[c])
                dst[z, :, tile(c)] = u[c] + total + glow * v[c]
            k, down, u = kn, up, un
        for c in TILES:
            kz[:, tile(c)] = k[c]
            fz[:, tile(c)] = down[c]

    groups = DEPTH // PLANES

    def group(g, carry):
        before(g)
        planes(g * PLANES, False)
        after(g)
        return carry

    lax.fori_loop(0, groups - 1, group, 0)
    planes(DEPTH - PLANES, True)


def heat_one_kernel(meta, us, share, urow, recv_lo, recv_hi, vrow, mid, mrow, vs, kz, fz, row1, sems):
    def bring(c):
        at = pl.ds(pl.multiple_of(c * CHUNK, CHUNK), CHUNK)
        return pltpu.make_async_copy(share.at[at], vs.at[at], sems.at[c])

    for c in range(AHEAD):
        bring(c).start()
    lane_w = iota((DEPTH, CY), 1)
    sub_w = iota((DEPTH, CY), 0)
    for n in range(2):
        recv = recv_lo if n == 0 else recv_hi

        def got_row(r):
            base = 128 + r * 4 * DEPTH
            got = [recv[base + c * DEPTH : base + (c + 1) * DEPTH] for c in range(4)]
            return meta[2 + n] * jnp.concatenate(got, axis=1)

        uo, uh = (got_row(0), got_row(1)) if n == 0 else (got_row(1), got_row(0))
        ui = urow[0] if n == 0 else urow[3]
        vo, vh, vi = (vrow[0], vrow[1], vrow[2]) if n == 0 else (vrow[5], vrow[4], vrow[3])
        kh = half_kappa(uh, vh)
        ki = half_kappa(ui, vi)
        total = flux(kh, half_kappa(uo, vo), uh, uo) + flux(kh, ki, uh, ui)

        def near(a, pad):
            left = jnp.where(lane_w == 0, a, pltpu.roll(a, 1, 1))
            right = jnp.where(lane_w == CY - 1, a, pltpu.roll(a, CY - 1, 1))
            up = jnp.where(sub_w == DEPTH - 1, pad, pltpu.roll(a, DEPTH - 1, 0))
            down = jnp.where(sub_w == 0, pad, pltpu.roll(a, 1, 0))
            return left, right, up, down

        for kn, un in zip(near(kh, 0.05), near(uh, 0.0)):
            total = total + flux(kh, kn, uh, un)
        row_at = meta[0] + (-1.0 if n == 0 else float(CX))
        gl = glow_of(jnp.full((1, CY), 1.0, F32) * row_at)
        mrow[n] = uh + total + gl * vh
        row1[DEPTH * n : DEPTH * n + DEPTH] = flux(kh, ki, uh, ui) if n == 0 else flux(ki, kh, ui, uh)
    glow = glow_of(iota((CX, 128), 0).astype(F32) + meta[0])

    def before(g):
        per = CHUNK // PLANES

        @pl.when(lax.rem(g, per) == per - 1)
        def _():
            c = (g + 1) // per
            bring(c).wait()

            @pl.when(c + AHEAD - 1 < DEPTH // CHUNK)
            def _():
                bring(c + AHEAD - 1).start()

    bring(0).wait()
    heat_planes(us, mid, vs, kz, fz, row1, None, None, glow, before, lambda g: None)


def heat_one(meta, u, v, urow, recv_lo, recv_hi, vrow):
    sd = jax.ShapeDtypeStruct
    return pl.pallas_call(
        heat_one_kernel,
        out_shape=(sd((DEPTH, CX, CY), F32), sd((2, DEPTH, CY), F32), sd((DEPTH, CX, CY), F32)),
        in_specs=[SSPEC, VSPEC, HSPEC] + [VSPEC] * 4,
        out_specs=(VSPEC,) * 3,
        scratch_shapes=[
            pltpu.VMEM((CX, CY), F32), pltpu.VMEM((CX, CY), F32),
            pltpu.VMEM((2 * DEPTH, CY), F32),
            pltpu.SemaphoreType.DMA((DEPTH // CHUNK,)),
        ],
        compiler_params=pltpu.CompilerParams(vmem_limit_bytes=VMEM_LIMIT),
        cost_estimate=pl.CostEstimate(flops=1 << 25, bytes_accessed=1 << 24, transcendentals=1 << 21),
        name="heat_step_one",
    )(meta, u, v, urow, recv_lo, recv_hi, vrow)


def heat_two_kernel(
    meta, mid, vs, mpart, recv_lo, recv_hi, vrow, pay_lo, pay_hi, got_lo, got_hi, out_hbm,
    os, kz, fz, row2, fix, col2, sems,
):
    lane = iota((CX, 128), 1)
    sub = iota((CX, 128), 0)
    lo_half = lane < DEPTH
    side = jnp.where(lo_half, meta[4], meta[5])
    glow1 = glow_of(sub.astype(F32) + meta[0])

    def stacks(a, b, at, size, fa=1.0, fb=1.0):
        p, q = a[at : at + size] * fa, b[at : at + size] * fb
        low = iota((size, 128), 1) < DEPTH
        return jnp.where(low, p, pltpu.roll(q, DEPTH, 1)), jnp.where(low, pltpu.roll(p, DEPTH, 1), q)

    def column_step(outer, here, inner, ends):
        (uo, vo), (uh, vh), (ui, vi), (ue, ve) = outer, here, inner, ends
        kh = half_kappa(uh, vh)
        ke = half_kappa(ue, ve)
        total = flux(kh, half_kappa(uo, vo), uh, uo) + flux(kh, half_kappa(ui, vi), uh, ui)

        def near(a, e, pad):
            below = jnp.where(sub == 0, e[0:1], pltpu.roll(a, 1, 0))
            above = jnp.where(sub == CX - 1, e[1:2], pltpu.roll(a, CX - 1, 0))
            up = jnp.where((lane & (DEPTH - 1)) == DEPTH - 1, pad, pltpu.roll(a, 127, 1))
            down = jnp.where((lane & (DEPTH - 1)) == 0, pad, pltpu.roll(a, 1, 1))
            return below, above, up, down

        for kn, un in zip(near(kh, ke, 0.05), near(uh, ue, 0.0)):
            total = total + flux(kh, kn, uh, un)
        return uh + total + glow1 * vh

    outer = stacks(got_lo, got_hi, 40, CX, meta[4], meta[5])
    here = stacks(got_lo, got_hi, 0, CX, meta[4], meta[5])
    inner = stacks(pay_lo, pay_hi, 0, CX)
    next_in = stacks(pay_lo, pay_hi, 40, CX)
    mid_out = column_step(outer, here, inner, stacks(got_lo, got_hi, CX, 8, meta[4], meta[5])) * side
    mid_in = column_step(here, inner, next_in, stacks(pay_lo, pay_hi, CX, 8))
    sign = jnp.where(lo_half, 1.0, -1.0)
    lane8 = iota((8, 128), 1)
    source = ((lane8 + 1) >> 1) & (DEPTH - 1)
    source = jnp.where((lane8 & 1) == 0, source, source + DEPTH)

    def weave(ref, a):
        for i in range(0, CX, 8):
            ref[i : i + 8] = jnp.take_along_axis(a[i : i + 8], source, axis=1)

    weave(fix, mid_in)
    weave(col2, sign * flux(half_kappa(mid_out, here[1]), half_kappa(mid_in, inner[1]), mid_out, mid_in))

    tail = [
        jnp.transpose(jnp.concatenate([g[CX : CX + 8] * meta[4 + i]] * 16, axis=0))
        for i, g in enumerate((got_lo, got_hi))
    ]
    ends = jnp.transpose(jnp.concatenate([mid_in] * 4, axis=0))
    lane_t = iota((DEPTH, 128), 1)

    def turned(a, by):
        return pltpu.roll(a, by & 127, 1) if by & 127 else a

    for n in range(2):
        x = 0 if n == 0 else CX - 1
        recv, r, vh = (recv_lo, 1, vrow[1]) if n == 0 else (recv_hi, 0, vrow[4])
        mh = [mpart[n, :, tile(c)] for c in TILES]
        mi = [mid[:, x, tile(c)] for c in TILES]
        for c, at, half, g, e in ((0, 0, 0, 0, 0), (3, 127, DEPTH, 1, 127)):
            base = 128 + (r * 4 + c) * DEPTH
            uc = meta[2 + n] * recv[base : base + DEPTH]
            kc = half_kappa(uc, vh[:, tile(c)])
            ue = turned(tail[g][:DEPTH], e - n)
            ke = half_kappa(ue, turned(tail[g][DEPTH:], e - n))
            mh[c] = mh[c] + jnp.where(lane_t == at, flux(kc, ke, uc, ue), 0.0)
            mi[c] = jnp.where(lane_t == at, turned(ends[half : half + DEPTH], e - x), mi[c])
        vi = vrow[2] if n == 0 else vrow[3]
        for c in TILES:
            m = mh[c] * meta[2 + n]
            kh = half_kappa(m, vh[:, tile(c)])
            ki = half_kappa(mi[c], vi[:, tile(c)])
            row2[DEPTH * n : DEPTH * n + DEPTH, tile(c)] = flux(kh, ki, m, mi[c]) if n == 0 else flux(ki, kh, mi[c], m)

    per = 8 // PLANES

    def store(c):
        at = pl.ds(pl.multiple_of(c * 8, 8), 8)
        return pltpu.make_async_copy(os.at[at], out_hbm.at[at], sems.at[c])

    def after(g):
        @pl.when(lax.rem(g, per) == per - 1)
        def _():
            store(g // per).start()

    glow = glow_of(sub.astype(F32) + meta[1])
    heat_planes(mid, os, vs, kz, fz, row2, col2, fix, glow, lambda g: None, after)
    store(DEPTH // 8 - 1).start()
    for c in range(DEPTH // 8):
        store(c).wait()


def heat_two(meta, mid, v, mpart, recv_lo, recv_hi, vrow, pay_lo, pay_hi, got_lo, got_hi):
    return pl.pallas_call(
        heat_two_kernel,
        out_shape=jax.ShapeDtypeStruct((DEPTH, CX, CY), F32),
        in_specs=[SSPEC] + [VSPEC] * 10,
        out_specs=ASPEC,
        scratch_shapes=[
            pltpu.VMEM((DEPTH, CX, CY), F32),
            pltpu.VMEM((CX, CY), F32), pltpu.VMEM((CX, CY), F32),
            pltpu.VMEM((2 * DEPTH, CY), F32),
            pltpu.VMEM((CX, 128), F32), pltpu.VMEM((CX, 128), F32),
            pltpu.SemaphoreType.DMA((DEPTH // 8,)),
        ],
        compiler_params=pltpu.CompilerParams(vmem_limit_bytes=VMEM_LIMIT),
        name="heat_step_two",
    )(meta, mid, v, mpart, recv_lo, recv_hi, vrow, pay_lo, pay_hi, got_lo, got_hi)


def ring(value, axis, steps):
    count = lax.axis_size(axis)
    return lax.ppermute(value, axis, [(i, (i + steps) % count) for i in range(count)])


def body(
    particle_locations,
    particle_speeds,
    particle_bulk,
    receiving_group_per_pair,
    emitting_group_per_pair,
    active_pair_slots,
    landing_site_triple,
    landing_weight_octants,
    thermal_excess,
    molten_strip_midlines,
):
    states = jnp.concatenate([particle_locations, particle_speeds], axis=0)
    width = HB * 128
    halo_lo = ring(states[:, NPART - width :], ("gx", "gy"), 1)
    halo_hi = ring(states[:, :width], ("gx", "gy"), -1)
    urow, ucol = edges(pltpu.with_memory_space_constraint(thermal_excess, pltpu.HBM))

    gx, gy = lax.axis_index("gx"), lax.axis_index("gy")
    row_start, col_start = gx * CX, gy * CY
    beam = row_start - molten_strip_midlines
    inside = jnp.stack([gx > 0, gx < lax.axis_size("gx") - 1, gy > 0, gy < lax.axis_size("gy") - 1])
    meta = jnp.concatenate([beam.astype(F32), inside.astype(F32)])
    origin = jnp.stack([row_start - G, col_start])

    nloc, nvel, skey, schg, last, send_lo, send_hi = particles(
        receiving_group_per_pair, emitting_group_per_pair, active_pair_slots, origin,
        particle_locations, particle_speeds, halo_lo, halo_hi, landing_site_triple,
        particle_bulk.reshape(128, 128), landing_weight_octants.reshape(128, 128), urow,
    )
    recv_lo = ring(send_hi, "gx", 1)
    recv_hi = ring(send_lo, "gx", -1)
    pile = own_deposit(last.reshape(128), last, skey, schg)
    share, vrow, pay_lo, pay_hi = edge_deposit(meta, pile, recv_lo, recv_hi, ucol)
    got_lo = ring(pay_hi, "gy", 1)
    got_hi = ring(pay_lo, "gy", -1)
    mid, mpart, here = heat_one(meta, thermal_excess, pltpu.with_memory_space_constraint(share, pltpu.HBM), urow, recv_lo, recv_hi, vrow)
    final = heat_two(meta, mid, here, mpart, recv_lo, recv_hi, vrow, pay_lo, pay_hi, got_lo, got_hi)
    return nloc, nvel, share, final


def solution(mesh):
    placed = (
        P(None, ("gx", "gy")),
        P(None, ("gx", "gy")),
        P(("gx", "gy")),
        P(("gx", "gy")),
        P(("gx", "gy")),
        P(("gx", "gy")),
        P(None, ("gx", "gy")),
        P(("gx", "gy")),
        P(None, "gx", "gy"),
        P(),
    )
    return jax.shard_map(
        body,
        mesh=mesh,
        in_specs=placed,
        out_specs=(
            P(None, ("gx", "gy")),
            P(None, ("gx", "gy")),
            P(None, "gx", "gy"),
            P(None, "gx", "gy"),
        ),
        check_vma=False,
    )
```
